32 devices in a mesh: sec: 4 (over y, x), gx: 8 (over z, core).
Axes of the slice: x: 2, y: 2, z: 4, core: 2. Of those that a mesh axis runs over, the one named last changes fastest.
Arguments:
- pressure_start: float32 [16, 128, 1024], P('sec', 'gx'), may hold values from -8 to 8
- soil_type: int32 [16, 128, 1024], P('sec', 'gx'), may hold values from 0 to 11
- saturated_conductivity: float32 [12], replicated, may hold values from 0.2 to 5
- storage_coefficient: float32 [12], replicated, may hold values from 0.1 to 1
- rainfall: float32 [3, 128, 1024], P(None, 'gx'), may hold values from 0 to 2
Outputs:
- pressure: float32 [16, 128, 1024], P('sec', 'gx')
- inflow: float32 [4, 3, 128, 1024], P('sec', None, 'gx')
The draws below stay inside these ranges and needn't reach their ends.
All inputs are finite; a program needn't handle non-finite values.
Results may differ from the reference program's by a relative error of at most 0.0001.
Values sent between devices are 32-bit elements; how exact they have to be, the bound alone decides.
A program may use at most 64 MiB of HBM per device.

```python
import math
import jax
import jax.numpy as jnp

LZ = 4
STEPS = 3
ITERS = 4
SOILS = 12
NZ = 16
NX = 128
NY = 1024
N_SEC = 4


def touch_ends(array, stream_key, low, high):
    longest = array.shape.index(max(array.shape))
    spots = []
    for shift in (0, 1):
        where = [jax.random.randint(jax.random.fold_in(stream_key, axis), (), 0, length) for axis, length in enumerate(array.shape)]
        where[longest] = (where[longest] + shift) % array.shape[longest]
        spots.append(tuple(where))
    return array.at[spots[0]].set(low).at[spots[1]].set(high)


def levels(rng, extent, split, smallest, largest):
    factor_of = 1.0
    for axis_at, parts in split:
        steps = jax.random.uniform(jax.random.fold_in(jax.random.fold_in(rng, 6), axis_at), (parts,), jnp.float32, smallest / len(split), largest / len(split))
        factor_of = factor_of * jnp.repeat(jnp.exp(steps), extent[axis_at] // parts).reshape((-1,) + (1,) * (len(extent) - 1 - axis_at))
    return factor_of


def bell_draw(stream_key, dims, deviation, bound, split=(), held_as=jnp.bfloat16):
    values = jax.random.normal(stream_key, dims, jnp.float32) * deviation
    if len(split) > 0:
        values = levels(stream_key, dims, split, -0.22, 0.18) * values
    return jnp.clip(values, min=-bound, max=bound).astype(held_as)


def setup_inputs(seed: int = 0) -> dict:
    key_list = jax.random.split(jax.random.key(seed), 6)
    return {
        "pressure_start": bell_draw(key_list[0], (NZ, NX, NY), 1.5, 8.0, ((0, 4), (1, 8)), jnp.float32),
        "soil_type": touch_ends(jax.random.randint(key_list[1], (NZ, NX, NY), 0, SOILS), jax.random.fold_in(key_list[1], 1), 0, SOILS - 1).astype(jnp.int32),
        "saturated_conductivity": jnp.clip(jnp.exp(jax.random.uniform(key_list[2], (SOILS,), jnp.float32, math.log(0.2), math.log(5.0))), 0.2, 5.0),
        "storage_coefficient": jnp.clip(jnp.exp(jax.random.uniform(key_list[3], (SOILS,), jnp.float32, math.log(0.1), math.log(1.0))), 0.1, 1.0),
        "rainfall": jnp.clip(2.0 * jax.random.uniform(key_list[4], (STEPS, NX, NY), jnp.float32) ** levels(key_list[4], (STEPS, NX, NY), ((1, 8),), -0.2, 0.2), 0.0, 2.0),
    }


def harmonic(cond, other):
    return 2.0 * cond * other / (cond + other)


def neighbours(padded):
    return [padded[:-2, 1:-1, 1:-1], padded[2:, 1:-1, 1:-1], padded[1:-1, :-2, 1:-1],
            padded[1:-1, 2:, 1:-1], padded[1:-1, 1:-1, :-2], padded[1:-1, 1:-1, 2:]]


def operate(field, faces, capacity):
    result = capacity * field
    for face, other in zip(faces, neighbours(jnp.pad(field, 1))):
        result = result + face * (field - other)
    return result


def reference(pressure_start, soil_type, saturated_conductivity, storage_coefficient, rainfall):
    cond_table = saturated_conductivity[soil_type]
    store_table = storage_coefficient[soil_type]
    head = pressure_start
    flows = []
    for step in range(STEPS):
        saturation = jax.nn.sigmoid(head)
        conductivity = cond_table * (0.05 + saturation * saturation)
        capacity = store_table * (0.1 + saturation * (1.0 - saturation))
        faces = [harmonic(conductivity, other) for other in neighbours(jnp.pad(conductivity, 1))]
        water = jnp.sum(saturation.reshape(N_SEC, LZ, NX, NY), axis=1)
        bottom = conductivity.reshape(N_SEC, LZ, NX, NY)[:, LZ - 1]
        depth = jnp.float32(LZ)
        below = jnp.zeros((NX, NY), jnp.float32)
        slopes = [None] * N_SEC
        for section in reversed(range(N_SEC)):
            slopes[section] = (water[section] / depth) * (0.5 + 0.5 * below / (below + depth))
            below = below + water[section]
        prefix_a = jnp.ones((NX, NY), jnp.float32)
        prefix_b = jnp.zeros((NX, NY), jnp.float32)
        inflows = []
        sources = []
        for section in range(N_SEC):
            entering = prefix_a * rainfall[step] + prefix_b
            offset = 0.5 * bottom[section]
            leaving = slopes[section] * entering + offset
            inflows.append(entering)
            local = jnp.zeros((LZ, NX, NY), jnp.float32).at[0].add(entering).at[LZ - 1].add(-leaving)
            sources.append(local)
            prefix_b = slopes[section] * prefix_b + offset
            prefix_a = slopes[section] * prefix_a
        flows.append(jnp.stack(inflows))
        source = jnp.concatenate(sources, axis=0)
        gravity = faces[0] - faces[1]
        rhs = capacity * head + gravity + source
        diagonal = capacity
        for face in faces:
            diagonal = diagonal + face
        iterate = head
        residual = rhs - operate(iterate, faces, capacity)
        precond = residual / diagonal
        direction = precond
        product = jnp.sum(residual * precond)
        for turn in range(ITERS):
            image = operate(direction, faces, capacity)
            alpha = product / jnp.sum(direction * image)
            iterate = iterate + alpha * direction
            residual = residual - alpha * image
            if turn + 1 < ITERS:
                precond = residual / diagonal
                renewed = jnp.sum(residual * precond)
                direction = precond + (renewed / product) * direction
                product = renewed
        head = iterate
    return head, jnp.stack(flows, axis=1)
```

```python
import functools

import jax
import jax.numpy as jnp
from jax import lax
from jax.experimental import pallas as pl
from jax.experimental.pallas import tpu as pltpu
from jax.sharding import PartitionSpec as P


MESH = pl.DeviceIdType.MESH
RIM = 8
LANES = 128
ITERS = 4


def by_group(low, high, each, body, carry):
    def trip(i, carry):
        for j in range(each):
            carry = body(low + i * each + j, carry)
        return carry

    return lax.fori_loop(0, (high - low) // each, trip, carry)


def place_of(s):
    return s + s // 2 - 2 * (s // 3)


def coefficients(g, h):
    nu = [g[0], h[0]]
    for k in range(1, ITERS):
        nu.append(2.0 * g[k] - nu[0])
        nu.append(4.0 * h[k] - 2.0 * nu[1] - nu[2 * k - 1])

    def gram(i, j):
        return 0.5 * (nu[i + j] + nu[abs(i - j)])

    def gram_a(i, j):
        shifted = gram(i, 1) if j == 0 else 0.5 * (gram(i, j + 1) + gram(i, j - 1))
        return gram(i, j) - shifted

    G = [[gram(i, j) for j in range(ITERS)] for i in range(ITERS)]
    H = [[gram_a(max(i, j), min(i, j)) for j in range(ITERS)] for i in range(ITERS)]
    zero = jnp.zeros_like(g[0])

    def form(matrix, v, top):
        total = zero
        for i in range(top + 1):
            row = matrix[i][i] * v[i]
            for j in range(i):
                row = row + 2.0 * matrix[i][j] * v[j]
            total = total + row * v[i]
        return total

    z = [zero + 1.0] + [zero] * (ITERS - 1)
    p = list(z)
    x = [zero] * ITERS
    rz = nu[0]
    for k in range(ITERS):
        curve = form(H, p, k)
        alpha = jnp.where(curve > 0.0, rz / jnp.where(curve > 0.0, curve, 1.0), 0.0)
        x = [a + alpha * b for a, b in zip(x, p)]
        if k + 1 < ITERS:
            image = list(p)
            for i in range(k + 1):
                if i == 0:
                    image[1] = image[1] - p[0]
                else:
                    image[i + 1] = image[i + 1] - 0.5 * p[i]
                    image[i - 1] = image[i - 1] - 0.5 * p[i]
            z = [a - alpha * b for a, b in zip(z, image)]
            new = jnp.maximum(form(G, z, k + 1), 0.0)
            beta = jnp.where(rz > 0.0, new / jnp.where(rz > 0.0, rz, 1.0), 0.0)
            p = [a + beta * b for a, b in zip(z, p)]
            rz = new
    return x


def kernel(
    n_sec, n_gx, steps, kinds,
    start_ref, soil_ref, cond_ref, store_ref, rain_ref,
    out_ref, flow_ref,
    head, soils, kind, store, cond, cap, face_l, face_r, face_c, diag, dinv, t0, t1, t2, t3,
    water, enter, leave, rainx, flows, pack_out, pack_in, soil_out, soil_in, landed, stats,
    met_sem, own_sem, swap_send, swap_recv, col_send, col_recv, row_send, row_recv, land_send, land_recv,
    sum_send, sum_recv, flow_send, flow_recv, back_send, back_recv,
):
    f32 = jnp.float32
    layers, rows, wide = start_ref.shape
    cols = wide // n_sec
    total = layers * n_sec
    sec, gx = lax.axis_index("sec"), lax.axis_index("gx")
    here = place_of(sec)
    ext_r, ext_c = rows + 2 * RIM, cols + LANES
    own = (slice(0, rows), slice(0, cols))

    def at(place):
        return pl.ds(pl.multiple_of(place * cols, LANES), cols)

    def layers_of(s):
        return pl.ds(1 + s * layers, layers)

    sec_peers = [lax.rem(sec + k, n_sec) for k in range(1, n_sec)]
    gx_peers = [lax.rem(gx + k, n_gx) for k in range(1, n_gx)]
    everyone = [
        {"sec": lax.rem(sec + i, n_sec), "gx": lax.rem(gx + j, n_gx)}
        for j in range(n_gx) for i in range(n_sec) if i + j
    ]
    barrier = pltpu.get_barrier_semaphore()
    for peer in sec_peers:
        pl.semaphore_signal(barrier, inc=1, device_id={"sec": peer}, device_id_type=MESH)
    for peer in gx_peers:
        pl.semaphore_signal(barrier, inc=1, device_id={"gx": peer}, device_id_type=MESH)

    plane = jnp.zeros((ext_r, ext_c), f32)
    for ref in (head, cond, t0, t1, t2, t3, face_l):
        ref[0] = plane
        ref[total + 1] = plane
    for d in (0, 1):
        rim = slice(rows + d * RIM, rows + d * RIM + RIM)

        @pl.when(gx == n_gx - 1 if d == 0 else gx == 0)
        def _(d=d, rim=rim):
            def wipe(l, carry):
                head[l + 1, rim, :] = jnp.zeros((RIM, ext_c), f32)
                soils[l + 1, rim, :] = jnp.zeros((RIM, ext_c), jnp.int32)
                for c in range(steps - 1):
                    for k in range(ITERS):
                        landed[c, k, d, l] = jnp.zeros((RIM, cols), f32)
                return carry

            lax.fori_loop(0, total, wipe, 0)
            for c in range(steps):
                rainx[c, rim, :] = jnp.zeros((RIM, ext_c), f32)

        @pl.when(here == n_sec - 1 if d == 0 else here == 0)
        def _(d=d):
            for c in range(steps):
                pack_in[c, d] = jnp.zeros((ext_r, LANES), f32)
            soil_in[d] = jnp.zeros((ext_r, LANES), jnp.int32)

    at_row = lax.broadcasted_iota(jnp.int32, (ext_r, ext_c), 0)
    at_col = lax.broadcasted_iota(jnp.int32, (ext_r, ext_c), 1)
    outside = (at_col >= cols + RIM) & (at_col < ext_c - RIM)
    outside = outside | ((at_row >= rows) & (at_row < rows + RIM) & (gx == n_gx - 1))
    outside = outside | ((at_row >= rows + RIM) & (gx == 0))
    outside = outside | ((at_col >= cols) & (at_col < cols + RIM) & (here == n_sec - 1))
    outside = outside | ((at_col >= ext_c - RIM) & (here == 0))

    lane = lax.broadcasted_iota(jnp.int32, (ext_r, LANES), 1)
    after = pl.multiple_of(lax.rem(here + 1, n_sec) * cols, LANES)
    before = pl.multiple_of(lax.rem(here + n_sec - 1, n_sec) * cols + cols - LANES, LANES)
    for c in range(steps):
        rainx[c, 0:rows, 0:cols] = rain_ref[c, :, at(here)]
        rainx[c, 0:rows, cols:] = jnp.where(
            lane[0:rows] < LANES // 2, rain_ref[c, :, pl.ds(after, LANES)], rain_ref[c, :, pl.ds(before, LANES)]
        )
    pl.semaphore_wait(barrier, n_sec + n_gx - 2)
    for peer in sec_peers:
        pl.semaphore_signal(met_sem, inc=1, device_id={"sec": peer}, device_id_type=MESH)

    swaps = []
    for f, (src, dst) in enumerate(((start_ref, head), (soil_ref, soils))):
        moves = []
        swaps.append(moves)
        copy = pltpu.make_async_copy(
            src.at[:, :, at(here)], dst.at[layers_of(sec), 0:rows, 0:cols], own_sem.at[f]
        )
        copy.start()
        moves.append(copy)
        for k, peer in enumerate(sec_peers):
            copy = pltpu.make_async_remote_copy(
                src_ref=src.at[:, :, at(place_of(peer))],
                dst_ref=dst.at[layers_of(sec), 0:rows, 0:cols],
                send_sem=swap_send.at[f, k],
                recv_sem=swap_recv.at[f, k],
                device_id={"sec": peer},
                device_id_type=MESH,
            )
            copy.start()
            moves.append(copy)

    def packed(field, low):
        outs = jnp.zeros((ext_r, LANES), field.dtype)
        for l in range(total):
            if low:
                tile = field[1 + l, :, 0:LANES]
                shift = RIM * l
            else:
                tile = field[1 + l, :, cols - LANES:cols]
                shift = (RIM * l + RIM) % LANES
            moved = pltpu.roll(tile, shift, 1) if shift else tile
            outs = jnp.where(lane // RIM == l, moved, outs)
        return outs

    def send_cols(slot, field):
        out, _ = packs(slot)
        out[0] = packed(field, True)
        out[1] = packed(field, False)
        for d in (0, 1):
            @pl.when(here > 0 if d == 0 else here < n_sec - 1)
            def _(d=d):
                col_copy(slot, d).start()

    def packs(slot):
        return (pack_out.at[slot], pack_in.at[slot]) if slot < steps else (soil_out, soil_in)

    def col_copy(slot, d):
        return pltpu.make_async_remote_copy(
            src_ref=packs(slot)[0].at[d],
            dst_ref=packs(slot)[1].at[d],
            send_sem=col_send.at[slot, d],
            recv_sem=col_recv.at[slot, d],
            device_id={"sec": place_of(lax.rem(here + n_sec - 1, n_sec) if d == 0 else lax.rem(here + 1, n_sec))},
            device_id_type=MESH,
        )

    def take_cols(slot, field):
        @pl.when(here > 0)
        def _():
            col_copy(slot, 0).wait_send()
            col_copy(slot, 1).wait_recv()

        @pl.when(here < n_sec - 1)
        def _():
            col_copy(slot, 1).wait_send()
            col_copy(slot, 0).wait_recv()

        taken = packs(slot)[1]
        right, left, nil = taken[0], taken[1], jnp.zeros((ext_r, LANES), field.dtype)
        for l in range(total):
            a, b = (-RIM * l) % LANES, (LANES - RIM - RIM * l) % LANES
            ra = pltpu.roll(right, a, 1) if a else right
            rb = pltpu.roll(left, b, 1) if b else left
            field[1 + l, :, cols:] = jnp.where(lane < RIM, ra, jnp.where(lane >= LANES - RIM, rb, nil))

    def row_copy(slot, field, first, count, width, d):
        src = pl.ds(0, RIM) if d == 0 else pl.ds(rows - RIM, RIM)
        dst = pl.ds(rows, RIM) if d == 0 else pl.ds(rows + RIM, RIM)
        return pltpu.make_async_remote_copy(
            src_ref=field.at[pl.ds(first, count), src, 0:width],
            dst_ref=field.at[pl.ds(first, count), dst, 0:width],
            send_sem=row_send.at[slot, d],
            recv_sem=row_recv.at[slot, d],
            device_id={"gx": lax.rem(gx + n_gx - 1, n_gx) if d == 0 else lax.rem(gx + 1, n_gx)},
            device_id_type=MESH,
        )

    def send_rows(*what):
        for d in (0, 1):
            @pl.when(gx > 0 if d == 0 else gx < n_gx - 1)
            def _(d=d):
                row_copy(*what, d).start()

    def take_rows(*what):
        @pl.when(gx > 0)
        def _():
            row_copy(*what, 0).wait_send()
            row_copy(*what, 1).wait_recv()

        @pl.when(gx < n_gx - 1)
        def _():
            row_copy(*what, 1).wait_send()
            row_copy(*what, 0).wait_recv()

    def shift(v, by, axis):
        return pltpu.roll(v, by % v.shape[axis], axis)

    def harmonic(a, b):
        return 2.0 * a * b / jnp.maximum(a + b, 1e-30)

    def folded(v):
        out = None
        for i in range(0, rows, RIM):
            for j in range(0, cols, LANES):
                part = v[i:i + RIM, j:j + LANES]
                out = part if out is None else out + part
        return out

    none = jnp.zeros((RIM, LANES), f32)
    basis = (t0, t1, t2, t3)

    def back_copy(k, peer):
        return pltpu.make_async_remote_copy(
            src_ref=head.at[layers_of(peer), 0:rows, 0:cols],
            dst_ref=out_ref.at[:, :, at(here)],
            send_sem=back_send.at[k],
            recv_sem=back_recv.at[k],
            device_id={"sec": peer},
            device_id_type=MESH,
        )

    outgoing = []
    for c in range(steps):
        if c == 0:
            fields = ((0, head, 1, total, cols), (1, soils, 1, total, cols), (2, rainx, 0, steps, ext_c))
            for f in range(2):
                for copy in swaps[f]:
                    copy.wait()
                send_rows(*fields[f])
            send_rows(*fields[2])
            take_rows(*fields[0])
            send_cols(c, head)
            take_rows(*fields[1])
            send_cols(steps, soils)
            take_rows(*fields[2])

            spot = lax.broadcasted_iota(jnp.int32, (ext_r, LANES), 1)
            of_cond = jnp.zeros((ext_r, LANES), f32)
            of_store = jnp.zeros((ext_r, LANES), f32)
            for k in range(kinds):
                of_cond = jnp.where(spot == k, cond_ref[k], of_cond)
                of_store = jnp.where(spot == k, store_ref[k], of_store)

            def look(lanes, l, carry):
                for j in range(lanes.start, lanes.stop, LANES):
                    which = soils[l, :, j:j + LANES]
                    hide = outside[:, j:j + LANES]
                    a = jnp.take_along_axis(of_cond, which, axis=1, mode="promise_in_bounds")
                    b = jnp.take_along_axis(of_store, which, axis=1, mode="promise_in_bounds")
                    kind[l, :, j:j + LANES] = jnp.where(hide, 0.0, a)
                    store[l, :, j:j + LANES] = jnp.where(hide, 0.0, b)
                return carry

        else:
            send_cols(c, head)

        def soil(lanes, s, carry):
            amount = jnp.zeros((ext_r, lanes.stop - lanes.start), f32)
            for j in range(layers):
                l = 1 + s * layers + j
                sat = jax.nn.sigmoid(head[l, :, lanes])
                cond[l, :, lanes] = kind[l, :, lanes] * (0.05 + sat * sat)
                cap[l, :, lanes] = store[l, :, lanes] * (0.1 + sat * (1.0 - sat))
                amount = amount + sat
            water[s, :, lanes] = amount
            return carry

        def couple(lanes):
            depth = jnp.float32(layers)
            below = jnp.zeros((ext_r, lanes.stop - lanes.start), f32)
            slopes = [None] * n_sec
            for s in reversed(range(n_sec)):
                amount = water[s, :, lanes]
                slopes[s] = amount / depth * (0.5 + 0.5 * below / (below + depth))
                below = below + amount
            entering = rainx[c, :, lanes]
            for s in range(n_sec):
                enter[s, :, lanes] = entering
                if lanes.start == 0:
                    flows[s, c] = entering[own]
                entering = slopes[s] * entering + 0.5 * cond[(s + 1) * layers, :, lanes]
                leave[s, :, lanes] = entering

        def faces(lanes, l, carry):
            k = cond[l, :, lanes]
            face_l[l, :, lanes] = harmonic(k, cond[l + 1, :, lanes])
            face_r[l, :, lanes] = harmonic(k, shift(k, -1, 0))
            return carry

        def faces_across(l, carry):
            k = cond[l]
            face_c[l] = harmonic(k, shift(k, -1, 1))
            return carry

        def prepare(lanes):
            if c == 0:
                by_group(1, total + 1, layers, functools.partial(look, lanes), 0)
            lax.fori_loop(0, n_sec, functools.partial(soil, lanes), 0)
            couple(lanes)
            by_group(1, total + 1, layers, functools.partial(faces, lanes), 0)

        prepare(slice(0, cols))
        own_flow = pltpu.make_async_copy(flows.at[sec, c], flow_ref.at[0, c, :, at(here)], own_sem.at[3 + c])
        own_flow.start()
        late = [own_flow]
        for k, peer in enumerate(sec_peers):
            copy = pltpu.make_async_remote_copy(
                src_ref=flows.at[peer, c],
                dst_ref=flow_ref.at[0, c, :, at(here)],
                send_sem=flow_send.at[c, k],
                recv_sem=flow_recv.at[c, k],
                device_id={"sec": peer},
                device_id_type=MESH,
            )
            copy.start()
            late.append(copy)
        outgoing += late

        if c == 0:
            take_cols(steps, soils)
        take_cols(c, head)
        prepare(slice(cols, ext_c))
        by_group(1, total + 1, layers, faces_across, 0)

        def first(s, acc):
            for j in range(layers):
                l = 1 + s * layers + j
                up, down = face_l[l - 1], face_l[l]
                fr, fc = face_r[l], face_c[l]
                v = head[l]
                whole = cap[l] + up + down + fr + shift(fr, 1, 0) + fc + shift(fc, 1, 1)
                flux_r = fr * (shift(v, -1, 0) - v)
                flux_c = fc * (shift(v, -1, 1) - v)
                res = up - down + up * (head[l - 1] - v) + down * (head[l + 1] - v)
                res = res + flux_r - shift(flux_r, 1, 0) + flux_c - shift(flux_c, 1, 1)
                if j == 0:
                    res = res + enter[s]
                if j == layers - 1:
                    res = res - leave[s]
                inverse = jnp.where(whole > 0.0, 1.0 / jnp.maximum(whole, 1e-30), 0.0)
                z = res * inverse
                diag[l] = whole
                dinv[l] = inverse
                t0[l] = z
                acc = acc + folded(res * z)
            return acc

        def land_copy(k, d, c=c):
            src = pl.ds(0, RIM) if d == 0 else pl.ds(rows - RIM, RIM)
            return pltpu.make_async_remote_copy(
                src_ref=basis[k].at[pl.ds(1, total), src, 0:cols],
                dst_ref=landed.at[c, k, d],
                send_sem=land_send.at[c, k, d],
                recv_sem=land_recv.at[c, k, d],
                device_id={"gx": lax.rem(gx + n_gx - 1, n_gx) if d == 0 else lax.rem(gx + 1, n_gx)},
                device_id_type=MESH,
            )

        def send_land(k):
            if c + 1 < steps:
                for d in (0, 1):
                    @pl.when(gx > 0 if d == 0 else gx < n_gx - 1)
                    def _(d=d):
                        land_copy(k, d).start()

        g = [lax.fori_loop(0, n_sec, first, none)]
        send_land(0)
        h = []
        for k in range(ITERS):
            def apply(l, acc, k=k):
                t = basis[k]
                fr, fc = face_r[l], face_c[l]
                v = t[l]
                near = face_l[l - 1] * t[l - 1] + face_l[l] * t[l + 1]
                near = near + fr * shift(v, -1, 0) + shift(fr * v, 1, 0)
                near = near + fc * shift(v, -1, 1) + shift(fc * v, 1, 1)
                ah = acc[0] + folded(v * near)
                ag = acc[1]
                if k + 1 < ITERS:
                    new = dinv[l] * near
                    if k > 0:
                        new = 2.0 * new - basis[k - 1][l]
                    basis[k + 1][l] = new
                    ag = ag + folded(diag[l] * new * new)
                return (ah, ag)

            ah, ag = by_group(1, total + 1, layers, apply, (none, none))
            h.append(ah)
            if k + 1 < ITERS:
                g.append(ag)
                send_land(k + 1)

        flat = jnp.concatenate([jnp.sum(v, axis=0, keepdims=True) for v in g + h], axis=0)
        part = LANES // (2 * ITERS)
        by = LANES // 2
        while by >= part:
            flat = flat + pltpu.roll(flat, by, 1)
            by //= 2
        which = lax.broadcasted_iota(jnp.int32, flat.shape, 0)
        group = lax.broadcasted_iota(jnp.int32, flat.shape, 1) // part
        mine = sec * n_gx + gx
        stats[c, mine] = jnp.sum(jnp.where(which == group, flat, 0.0), axis=0, keepdims=True)
        if c == 0:
            pl.semaphore_wait(met_sem, n_sec - 1)
        sends = []
        for k, peer in enumerate(everyone):
            copy = pltpu.make_async_remote_copy(
                src_ref=stats.at[c, mine],
                dst_ref=stats.at[c, mine],
                send_sem=sum_send.at[c, k],
                recv_sem=sum_recv.at[c, k],
                device_id=peer,
                device_id_type=MESH,
            )
            copy.start()
            sends.append(copy)
        for copy in sends:
            copy.wait()
        summed = stats[c, 0]
        for k in range(1, n_sec * n_gx):
            summed = summed + stats[c, k]
        parts = [
            jnp.sum(jnp.where(group[0:1] == k, summed, 0.0), axis=1, keepdims=True)
            for k in range(2 * ITERS)
        ]
        x = coefficients(parts[:ITERS], parts[ITERS:])
        x = [jnp.broadcast_to(v, (rows, cols)) for v in x]

        def update(l, carry):
            v = head[l, 0:rows, 0:cols]
            for k in range(ITERS):
                v = v + x[k] * basis[k][l, 0:rows, 0:cols]
            head[l, 0:rows, 0:cols] = v
            return carry

        if c + 1 == steps:
            for i in range(1, n_sec):
                peer = sec_peers[i - 1]
                lax.fori_loop(1 + peer * layers, 1 + (peer + 1) * layers, update, 0)
                back_copy(i - 1, peer).start()
                outgoing.append(back_copy(i - 1, peer))
            lax.fori_loop(1 + sec * layers, 1 + (sec + 1) * layers, update, 0)
        else:
            by_group(1, total + 1, layers, update, 0)
        if c + 1 < steps:
            for d in (0, 1):
                @pl.when(gx > 0 if d == 0 else gx < n_gx - 1)
                def _(d=d):
                    for k in range(ITERS):
                        land_copy(k, d).wait_send()

                @pl.when(gx < n_gx - 1 if d == 0 else gx > 0)
                def _(d=d):
                    for k in range(ITERS):
                        land_copy(k, d).wait_recv()

            def update_rim(l, carry):
                for d in (0, 1):
                    at_rows = slice(rows + d * RIM, rows + d * RIM + RIM)
                    v = head[l, at_rows, 0:cols]
                    for k in range(ITERS):
                        v = v + x[k][0:RIM] * landed[c, k, d, l - 1]
                    head[l, at_rows, 0:cols] = v
                return carry

            by_group(1, total + 1, layers, update_rim, 0)

    copy = pltpu.make_async_copy(head.at[layers_of(sec), 0:rows, 0:cols], out_ref.at[:, :, at(here)], own_sem.at[2])
    copy.start()
    outgoing.append(copy)
    for copy in outgoing:
        copy.wait()


def body(n_sec, n_gx, start, soil, conductivity, storage, rain):
    layers, rows, wide = start.shape
    steps = rain.shape[0]
    cols = wide // n_sec
    total = layers * n_sec
    assert total * RIM <= LANES and cols % LANES == 0 and rows % RIM == 0 and n_sec == 4
    ext = (rows + 2 * RIM, cols + LANES)
    f32 = jnp.float32
    field = pltpu.VMEM((total + 2,) + ext, f32)
    per_sec = pltpu.VMEM((n_sec,) + ext, f32)
    dma = pltpu.SemaphoreType.DMA
    vmem = pl.BlockSpec(memory_space=pltpu.VMEM)
    hbm = pl.BlockSpec(memory_space=pl.ANY)
    smem = pl.BlockSpec(memory_space=pltpu.SMEM)
    return tuple(pl.pallas_call(
        functools.partial(kernel, n_sec, n_gx, steps, conductivity.shape[0]),
        out_shape=(
            jax.ShapeDtypeStruct(start.shape, f32),
            jax.ShapeDtypeStruct((1, steps, rows, wide), f32),
        ),
        in_specs=[hbm, hbm, smem, smem, vmem],
        out_specs=(hbm, hbm),
        scratch_shapes=[field, pltpu.VMEM((total + 2,) + ext, jnp.int32)]
        + [field] * 13
        + [per_sec] * 3
        + [
            pltpu.VMEM((steps,) + ext, f32),
            pltpu.VMEM((n_sec, steps, rows, cols), f32),
            pltpu.VMEM((steps, 2, ext[0], LANES), f32),
            pltpu.VMEM((steps, 2, ext[0], LANES), f32),
            pltpu.VMEM((2, ext[0], LANES), jnp.int32),
            pltpu.VMEM((2, ext[0], LANES), jnp.int32),
            pltpu.VMEM((steps, ITERS, 2, total, RIM, cols), f32),
            pltpu.VMEM((steps, n_sec * n_gx, 1, LANES), f32),
            pltpu.SemaphoreType.REGULAR,
            dma((3 + steps,)),
            dma((2, n_sec - 1)),
            dma((2, n_sec - 1)),
            dma((steps + 1, 2)),
            dma((steps + 1, 2)),
            dma((3, 2)),
            dma((3, 2)),
            dma((steps, ITERS, 2)),
            dma((steps, ITERS, 2)),
            dma((steps, n_sec * n_gx)),
            dma((steps, n_sec * n_gx)),
            dma((steps, n_sec - 1)),
            dma((steps, n_sec - 1)),
            dma((n_sec - 1,)),
            dma((n_sec - 1,)),
        ],
        compiler_params=pltpu.CompilerParams(collective_id=0, has_side_effects=True),
    )(start, soil, conductivity, storage, rain))


def solution(mesh):
    placed = (P("sec", "gx", None), P("sec", "gx", None), P(), P(), P(None, "gx", None))
    return jax.shard_map(
        functools.partial(body, mesh.shape["sec"], mesh.shape["gx"]),
        mesh=mesh,
        in_specs=placed,
        out_specs=(P("sec", "gx", None), P("sec", None, "gx", None)),
        check_vma=False,
    )
```

```python
import functools

import jax
import jax.numpy as jnp
from jax import lax
from jax.experimental import pallas as pl
from jax.experimental.pallas import tpu as pltpu
from jax.sharding import PartitionSpec as P


MESH = pl.DeviceIdType.MESH
RIM = 8
LANES = 128
ITERS = 4
LOW = RIM // 2


def by_group(low, high, each, body, carry):
    def trip(i, carry):
        for j in range(each):
            carry = body(low + i * each + j, carry)
        return carry

    return lax.fori_loop(0, (high - low) // each, trip, carry)


def place_of(s):
    return s + s // 2 - 2 * (s // 3)


def mirrored(a, mask, count):
    out, bit = 0, 1
    while bit < count:
        out = out + lax.rem(a // bit + (mask // bit) % 2, 2) * bit
        bit *= 2
    return out


def coefficients(g, h):
    nu = [g[0], h[0]]
    for k in range(1, ITERS):
        nu.append(2.0 * g[k] - nu[0])
        nu.append(4.0 * h[k] - 2.0 * nu[1] - nu[2 * k - 1])

    def gram(i, j):
        return 0.5 * (nu[i + j] + nu[abs(i - j)])

    def gram_a(i, j):
        shifted = gram(i, 1) if j == 0 else 0.5 * (gram(i, j + 1) + gram(i, j - 1))
        return gram(i, j) - shifted

    G = [[gram(i, j) for j in range(ITERS)] for i in range(ITERS)]
    H = [[gram_a(max(i, j), min(i, j)) for j in range(ITERS)] for i in range(ITERS)]
    zero = jnp.zeros_like(g[0])

    def form(matrix, v, top):
        total = zero
        for i in range(top + 1):
            row = matrix[i][i] * v[i]
            for j in range(i):
                row = row + 2.0 * matrix[i][j] * v[j]
            total = total + row * v[i]
        return total

    z = [zero + 1.0] + [zero] * (ITERS - 1)
    p = list(z)
    x = [zero] * ITERS
    rz = nu[0]
    for k in range(ITERS):
        curve = form(H, p, k)
        alpha = jnp.where(curve > 0.0, rz / jnp.where(curve > 0.0, curve, 1.0), 0.0)
        x = [a + alpha * b for a, b in zip(x, p)]
        if k + 1 < ITERS:
            image = list(p)
            for i in range(k + 1):
                if i == 0:
                    image[1] = image[1] - p[0]
                else:
                    image[i + 1] = image[i + 1] - 0.5 * p[i]
                    image[i - 1] = image[i - 1] - 0.5 * p[i]
            z = [a - alpha * b for a, b in zip(z, image)]
            new = jnp.maximum(form(G, z, k + 1), 0.0)
            beta = jnp.where(rz > 0.0, new / jnp.where(rz > 0.0, rz, 1.0), 0.0)
            p = [a + beta * b for a, b in zip(z, p)]
            rz = new
    return x


def kernel(
    n_sec, n_gx, steps, kinds,
    start_ref, soil_ref, cond_ref, store_ref, rain_ref,
    out_ref, flow_ref,
    head, soils, kind, store, cond, cap, face_l, face_r, face_c, diag, dinv, t0, t1, t2, t3,
    water, enter, leave, rainx, flows, pack_out, pack_in, edge_f, edge_i, edges_f, edges_i,
    stage_f, stage_i, stage_r, rows_out, landed, stats,
    met_sem, own_sem, load_sem, swap_send, swap_recv, row_send, row_recv, rain_send, rain_recv,
    col_send, col_recv, land_send, land_recv, sum_send, sum_recv, flow_send, flow_recv, back_send, back_recv,
):
    f32 = jnp.float32
    layers, rows, wide = start_ref.shape
    cols = wide // n_sec
    tiles = cols // LANES
    total = layers * n_sec
    ext = rows + 2 * RIM
    sec, gx = lax.axis_index("sec"), lax.axis_index("gx")
    here = place_of(sec)
    own = slice(RIM, RIM + rows)
    work = slice(LOW, ext - LOW)
    above = slice(LOW - 1, ext - LOW - 1)
    under = slice(LOW + 1, ext - LOW + 1)
    everywhere = list(range(tiles + 1))
    inner = list(range(tiles))

    def lanes_at(place, tile):
        return pl.ds(pl.multiple_of(place * cols + tile * LANES, LANES), LANES)

    def layers_of(s):
        return pl.ds(1 + s * layers, layers)

    sec_peers = [lax.rem(sec + k, n_sec) for k in range(1, n_sec)]
    sec_froms = [lax.rem(sec + n_sec - k, n_sec) for k in range(n_sec)]
    gx_peers = [lax.rem(gx + k, n_gx) for k in range(1, n_gx)]
    everyone = [
        {"sec": mirrored(sec, i, n_sec), "gx": mirrored(gx, j, n_gx)}
        for j in reversed(range(n_gx)) for i in reversed(range(n_sec)) if i + j
    ]

    loads = [
        pltpu.make_async_copy(src, dst, load_sem.at[f])
        for f, (src, dst) in enumerate(((start_ref, stage_f), (soil_ref, stage_i), (rain_ref, stage_r)))
    ]
    for copy in loads:
        copy.start()
    barrier = pltpu.get_barrier_semaphore()
    for peer in sec_peers:
        pl.semaphore_signal(barrier, inc=1, device_id={"sec": peer}, device_id_type=MESH)
    for peer in gx_peers:
        pl.semaphore_signal(barrier, inc=1, device_id={"gx": peer}, device_id_type=MESH)

    def nil(*shape, dtype=f32):
        return jnp.zeros(shape, dtype)

    for ref in (head, cond, t0, t1, t2, t3, face_l):
        ref[0] = nil(tiles + 1, ext, LANES)
        ref[total + 1] = nil(tiles + 1, ext, LANES)

    def hem(l, carry):
        for ref in (t0, t1, t2, t3, face_r):
            ref[l, :, 0:RIM] = nil(tiles + 1, RIM, LANES)
            ref[l, :, ext - RIM:ext] = nil(tiles + 1, RIM, LANES)
        return carry

    lax.fori_loop(1, total + 1, hem, 0)
    for d in (0, 1):
        rim = slice(ext - RIM, ext) if d == 0 else slice(0, RIM)

        @pl.when(gx == n_gx - 1 if d == 0 else gx == 0)
        def _(d=d, rim=rim):
            def wipe(l, carry):
                head[l + 1, :, rim] = nil(tiles + 1, RIM, LANES)
                soils[l + 1, :, rim] = nil(tiles + 1, RIM, LANES, dtype=jnp.int32)
                return carry

            lax.fori_loop(0, total, wipe, 0)
            for c in range(steps):
                rainx[c, :, rim] = nil(tiles + 1, RIM, LANES)
            edge_f[:, rim] = nil(n_sec, RIM, LANES)
            edge_i[:, rim] = nil(n_sec, RIM, LANES, dtype=jnp.int32)
            for c in range(steps - 1):
                for k in range(ITERS):
                    landed[c, k, d] = nil(total // 2, tiles, RIM, LANES)

        @pl.when(here == n_sec - 1 if d == 0 else here == 0)
        def _(d=d):
            for c in range(steps - 1):
                pack_in[c, d] = nil(ext, LANES)

    lane = lax.broadcasted_iota(jnp.int32, (ext, LANES), 1)
    lane_w = lax.broadcasted_iota(jnp.int32, (rows + RIM, LANES), 1)
    lane_o = lax.broadcasted_iota(jnp.int32, (rows, LANES), 1)
    at_row = lax.broadcasted_iota(jnp.int32, (ext, LANES), 0)
    beyond = ((at_row >= rows + RIM) & (gx == n_gx - 1)) | ((at_row < RIM) & (gx == 0))
    beside = (lane >= RIM) & (lane < LANES - RIM)
    beside = beside | ((lane < RIM) & (here == n_sec - 1)) | ((lane >= LANES - RIM) & (here == 0))
    outside = [beyond] * tiles + [beyond | beside]

    for copy in loads:
        copy.wait()

    after = lanes_at(lax.rem(here + 1, n_sec), 0)
    before = lanes_at(lax.rem(here + n_sec - 1, n_sec), tiles - 1)
    for c in range(steps):
        for ct in inner:
            rainx[c, ct, own] = stage_r[c, :, lanes_at(here, ct)]
        rainx[c, tiles, own] = jnp.where(lane_o < LANES // 2, stage_r[c, :, after], stage_r[c, :, before])
    for stage, edges in ((stage_f, edges_f), (stage_i, edges_i)):
        for place in range(n_sec):
            out = nil(rows, LANES, dtype=stage.dtype)
            for j in range(layers):
                right = nil(rows, LANES, dtype=stage.dtype)
                left = right
                if place + 1 < n_sec:
                    right = stage[j, :, (place + 1) * cols:(place + 1) * cols + LANES]
                if place > 0:
                    left = stage[j, :, place * cols - LANES:place * cols]
                both = jnp.where(lane_o < RIM, right, left)
                moved = pltpu.roll(both, (2 * RIM * j + RIM) % LANES, 1)
                out = jnp.where(lane_o // (2 * RIM) == j, moved, out)
            edges[place] = out

    pl.semaphore_wait(barrier, n_sec + n_gx - 2)
    for peer in sec_peers:
        pl.semaphore_signal(met_sem, inc=1, device_id={"sec": peer}, device_id_type=MESH)

    parcels = ((stage_i, soils, edges_i, edge_i), (stage_f, head, edges_f, edge_f))
    swaps = [[] for _ in range(n_sec)]
    for f, (stage, field, edges, edge) in enumerate(parcels):
        for ct in inner:
            swaps[0].append(pltpu.make_async_copy(
                stage.at[:, :, lanes_at(here, ct)], field.at[layers_of(sec), ct, own], own_sem.at[f, ct]
            ))
        swaps[0].append(pltpu.make_async_copy(edges.at[here], edge.at[sec, own], own_sem.at[f, tiles]))
    for k, peer in enumerate(sec_peers):
        for f, (stage, field, edges, edge) in enumerate(parcels):
            moves = [
                (stage.at[:, :, lanes_at(place_of(peer), ct)], field.at[layers_of(sec), ct, own]) for ct in inner
            ]
            moves.append((edges.at[place_of(peer)], edge.at[sec, own]))
            for m, (src, dst) in enumerate(moves):
                swaps[k + 1].append(pltpu.make_async_remote_copy(
                    src_ref=src,
                    dst_ref=dst,
                    send_sem=swap_send.at[k, f, m],
                    recv_sem=swap_recv.at[k, f, m],
                    device_id={"sec": peer},
                    device_id_type=MESH,
                ))
    for moves in swaps:
        for copy in moves:
            copy.start()

    def toward(d):
        return lax.rem(gx + n_gx - 1, n_gx) if d == 0 else lax.rem(gx + 1, n_gx)

    def ends(d):
        return (slice(RIM, 2 * RIM), slice(ext - RIM, ext)) if d == 0 else (slice(rows, rows + RIM), slice(0, RIM))

    def sends_to(d):
        return gx > 0 if d == 0 else gx < n_gx - 1

    def rain_copy(d):
        src, dst = ends(d)
        return pltpu.make_async_remote_copy(
            src_ref=rainx.at[:, :, src],
            dst_ref=rainx.at[:, :, dst],
            send_sem=rain_send.at[d],
            recv_sem=rain_recv.at[d],
            device_id={"gx": toward(d)},
            device_id_type=MESH,
        )

    def row_copies(k, d):
        src, dst = ends(d)
        s = sec_froms[k]
        copies = []
        for f, (_, field, _, edge) in enumerate(parcels):
            pairs = ((field.at[layers_of(s), 0:tiles, src], field.at[layers_of(s), 0:tiles, dst]),
                     (edge.at[s, src], edge.at[s, dst]))
            for m, (a, b) in enumerate(pairs):
                copies.append(pltpu.make_async_remote_copy(
                    src_ref=a,
                    dst_ref=b,
                    send_sem=row_send.at[k, f, d, m],
                    recv_sem=row_recv.at[k, f, d, m],
                    device_id={"gx": toward(d)},
                    device_id_type=MESH,
                ))
        return copies

    for d in (0, 1):
        @pl.when(sends_to(d))
        def _(d=d):
            rain_copy(d).start()

    for k in range(n_sec):
        for copy in swaps[k]:
            copy.wait()
        for d in (0, 1):
            @pl.when(sends_to(d))
            def _(d=d, k=k):
                for copy in row_copies(k, d):
                    copy.start()

    def take_rows(k):
        for d in (0, 1):
            @pl.when(sends_to(d))
            def _(d=d):
                for copy in row_copies(k, d):
                    copy.wait_send()
                for copy in row_copies(k, 1 - d):
                    copy.wait_recv()

    def packed(tile, low):
        outs = nil(ext, LANES)
        for l in range(total):
            shift = (RIM * l if low else RIM * l + RIM) % LANES
            piece = head[1 + l, tile]
            moved = pltpu.roll(piece, shift, 1) if shift else piece
            outs = jnp.where(lane // RIM == l, moved, outs)
        return outs

    def col_copy(c, d):
        return pltpu.make_async_remote_copy(
            src_ref=pack_out.at[c, d],
            dst_ref=pack_in.at[c, d],
            send_sem=col_send.at[c, d],
            recv_sem=col_recv.at[c, d],
            device_id={"sec": place_of(lax.rem(here + n_sec - 1, n_sec) if d == 0 else lax.rem(here + 1, n_sec))},
            device_id_type=MESH,
        )

    def send_cols(c):
        for d in (0, 1):
            @pl.when(here > 0 if d == 0 else here < n_sec - 1)
            def _(d=d):
                pack_out[c, d] = packed(0 if d == 0 else tiles - 1, d == 0)
                col_copy(c, d).start()

    def take_cols(c):
        @pl.when(here > 0)
        def _():
            col_copy(c, 0).wait_send()
            col_copy(c, 1).wait_recv()

        @pl.when(here < n_sec - 1)
        def _():
            col_copy(c, 1).wait_send()
            col_copy(c, 0).wait_recv()

        right, left = pack_in[c, 0], pack_in[c, 1]
        for l in range(total):
            a, b = (-RIM * l) % LANES, (LANES - RIM - RIM * l) % LANES
            ra = pltpu.roll(right, a, 1) if a else right
            rb = pltpu.roll(left, b, 1) if b else left
            head[1 + l, tiles] = jnp.where(lane < RIM, ra, jnp.where(lane >= LANES - RIM, rb, 0.0))

    def right_of(v, at):
        moved = [pltpu.roll(a, LANES - 1, 1) for a in v]
        return [jnp.where(at == LANES - 1, moved[(i + 1) % len(v)], moved[i]) for i in range(len(v))]

    def left_of(v, at):
        moved = [pltpu.roll(a, 1, 1) for a in v]
        return [jnp.where(at == 0, moved[i - 1], moved[i]) for i in range(len(v))]

    def harmonic(a, b):
        return 2.0 * a * b / jnp.maximum(a + b, 1e-30)

    half = lax.broadcasted_iota(jnp.int32, (RIM, LANES), 0) >= LOW

    def own_of(v):
        out = jnp.where(half, v[0:RIM], v[rows:rows + RIM])
        for i in range(RIM, rows, RIM):
            out = out + v[i:i + RIM]
        return out

    none = nil(RIM, LANES)
    basis = (t0, t1, t2, t3)

    def back_copies(k, peer):
        return [
            pltpu.make_async_remote_copy(
                src_ref=head.at[layers_of(peer), ct, own],
                dst_ref=out_ref.at[:, :, lanes_at(here, ct)],
                send_sem=back_send.at[k, ct],
                recv_sem=back_recv.at[k, ct],
                device_id={"sec": peer},
                device_id_type=MESH,
            )
            for ct in inner
        ]

    def soil(which, s):
        for ct in which:
            amount = nil(ext, LANES)
            for j in range(layers):
                l = 1 + s * layers + j
                sat = jax.nn.sigmoid(head[l, ct])
                cond[l, ct] = kind[l, ct] * (0.05 + sat * sat)
                cap[l, ct] = store[l, ct] * (0.1 + sat * (1.0 - sat))
                amount = amount + sat
            water[s, ct] = amount

    spot = lax.broadcasted_iota(jnp.int32, (ext, LANES), 1)
    of_cond = nil(ext, LANES)
    of_store = nil(ext, LANES)
    for k in range(kinds):
        of_cond = jnp.where(spot == k, cond_ref[k], of_cond)
        of_store = jnp.where(spot == k, store_ref[k], of_store)

    def open_edges(s):
        for edge, field in ((edge_f, head), (edge_i, soils)):
            taken = edge[s]
            for j in range(layers):
                moved = pltpu.roll(taken, LANES - RIM - 2 * RIM * j, 1)
                field[1 + s * layers + j, tiles] = jnp.where(
                    (lane < RIM) | (lane >= LANES - RIM), moved, nil(ext, LANES, dtype=field.dtype)
                )

    def look(s):
        for j in range(layers):
            l = 1 + s * layers + j
            for ct in everywhere:
                which = soils[l, ct]
                a = jnp.take_along_axis(of_cond, which, axis=1, mode="promise_in_bounds")
                b = jnp.take_along_axis(of_store, which, axis=1, mode="promise_in_bounds")
                kind[l, ct] = jnp.where(outside[ct], 0.0, a)
                store[l, ct] = jnp.where(outside[ct], 0.0, b)

    outgoing = []
    for c in range(steps):
        def couple(which, c=c):
            depth = jnp.float32(layers)
            for ct in which:
                below = nil(ext, LANES)
                slopes = [None] * n_sec
                for s in reversed(range(n_sec)):
                    amount = water[s, ct]
                    slopes[s] = amount / depth * (0.5 + 0.5 * below / (below + depth))
                    below = below + amount
                entering = rainx[c, ct]
                for s in range(n_sec):
                    enter[s, ct] = entering
                    if ct < tiles:
                        flows[s, c, :, ct * LANES:(ct + 1) * LANES] = entering[own]
                    entering = slopes[s] * entering + 0.5 * cond[(s + 1) * layers, ct]
                    leave[s, ct] = entering

        def faces(which, l, carry):
            for ct in which:
                k = cond[l, ct, work]
                face_l[l, ct, work] = harmonic(k, cond[l + 1, ct, work])
                face_r[l, ct, work] = harmonic(k, cond[l, ct, under])
            return carry

        def faces_across(l, carry):
            k = [cond[l, ct, work] for ct in everywhere]
            for ct, other in zip(everywhere, right_of(k, lane_w)):
                face_c[l, ct, work] = harmonic(k[ct], other)
            return carry

        def prepare(which, c=c):
            if c > 0:
                def each(s, carry):
                    soil(which, s)
                    return carry

                lax.fori_loop(0, n_sec, each, 0)
            couple(which)
            by_group(1, total + 1, layers, functools.partial(faces, which), 0)

        if c == 0:
            for k in range(n_sec):
                s = sec_froms[k]
                take_rows(k)
                open_edges(s)
                look(s)
                soil(everywhere, s)
            for d in (0, 1):
                @pl.when(sends_to(d))
                def _(d=d):
                    rain_copy(d).wait_send()
                    rain_copy(1 - d).wait_recv()
        else:
            send_cols(c - 1)

        prepare(inner)
        own_flow = pltpu.make_async_copy(
            flows.at[sec, c], flow_ref.at[0, c, :, pl.ds(pl.multiple_of(here * cols, LANES), cols)], flow_send.at[c, n_sec - 1]
        )
        own_flow.start()
        late = [own_flow]
        for k, peer in enumerate(sec_peers):
            copy = pltpu.make_async_remote_copy(
                src_ref=flows.at[peer, c],
                dst_ref=flow_ref.at[0, c, :, pl.ds(pl.multiple_of(here * cols, LANES), cols)],
                send_sem=flow_send.at[c, k],
                recv_sem=flow_recv.at[c, k],
                device_id={"sec": peer},
                device_id_type=MESH,
            )
            copy.start()
            late.append(copy)
        outgoing += late

        if c > 0:
            take_cols(c - 1)
        prepare([tiles])
        by_group(1, total + 1, layers, faces_across, 0)

        def rows_of(k, l, m):
            if c + 1 < steps:
                i = (l - 1) // 2
                for ct in inner:
                    for j in (0, 1):
                        put = slice(j * LOW, j * LOW + LOW)
                        rows_out[k, 0, i, ct, put] = basis[k][l + j, ct, RIM + 1:RIM + 1 + LOW]
                        rows_out[k, 1, i, ct, put] = basis[k][l + j, ct, RIM + rows - LOW:RIM + rows]

        def first(s, acc):
            for j in range(layers):
                l = 1 + s * layers + j
                fc = [face_c[l, ct, work] for ct in everywhere]
                v = [head[l, ct, work] for ct in everywhere]
                flux = [a * (b - d) for a, b, d in zip(fc, right_of(v, lane_w), v)]
                fb, back = left_of(fc, lane_w), left_of(flux, lane_w)
                for ct in everywhere:
                    up, down = face_l[l - 1, ct, work], face_l[l, ct, work]
                    fr, fa = face_r[l, ct, work], face_r[l, ct, above]
                    whole = cap[l, ct, work] + up + down + fr + fa + fc[ct] + fb[ct]
                    res = up - down + up * (head[l - 1, ct, work] - v[ct]) + down * (head[l + 1, ct, work] - v[ct])
                    res = res + fr * (head[l, ct, under] - v[ct]) + fa * (head[l, ct, above] - v[ct])
                    res = res + flux[ct] - back[ct]
                    if j == 0:
                        res = res + enter[s, ct, work]
                    if j == layers - 1:
                        res = res - leave[s, ct, work]
                    inverse = jnp.where(whole > 0.0, 1.0 / jnp.maximum(whole, 1e-30), 0.0)
                    z = res * inverse
                    diag[l, ct, work] = whole
                    dinv[l, ct, work] = 2.0 * inverse
                    t0[l, ct, work] = z
                    if ct < tiles:
                        acc = acc + own_of(res * z)
            for j in range(0, layers, 2):
                rows_of(0, 1 + s * layers + j, s)
            return acc

        def land_copy(k, d, c=c):
            return pltpu.make_async_remote_copy(
                src_ref=rows_out.at[k, d],
                dst_ref=landed.at[c, k, d],
                send_sem=land_send.at[c, k, d],
                recv_sem=land_recv.at[c, k, d],
                device_id={"gx": toward(d)},
                device_id_type=MESH,
            )

        def send_land(k):
            if c + 1 < steps:
                for d in (0, 1):
                    @pl.when(sends_to(d))
                    def _(d=d):
                        land_copy(k, d).start()

        g = [lax.fori_loop(0, n_sec, first, none)]
        send_land(0)
        h = []
        for k in range(ITERS - 1):
            def apply(i, acc, k=k):
                t = basis[k]
                for j in range(layers):
                    l = 1 + i * layers + j
                    v = [t[l, ct, work] for ct in everywhere]
                    fc = [face_c[l, ct, work] for ct in everywhere]
                    aside = right_of(v, lane_w)
                    back = left_of([a * b for a, b in zip(fc, v)], lane_w)
                    for ct in everywhere:
                        near = face_l[l - 1, ct, work] * t[l - 1, ct, work] + face_l[l, ct, work] * t[l + 1, ct, work]
                        near = near + face_r[l, ct, work] * t[l, ct, under] + face_r[l, ct, above] * t[l, ct, above]
                        near = near + (fc[ct] * aside[ct] + back[ct])
                        new = dinv[l, ct, work] * near
                        new = 0.5 * new if k == 0 else new - basis[k - 1][l, ct, work]
                        basis[k + 1][l, ct, work] = new
                        if ct < tiles:
                            acc = (acc[0] + own_of(v[ct] * near), acc[1] + own_of(diag[l, ct, work] * new * new))
                for j in range(0, layers, 2):
                    rows_of(k + 1, 1 + i * layers + j, i)
                return acc

            ah, ag = lax.fori_loop(0, n_sec, apply, (none, none))
            h.append(ah)
            g.append(ag)
            send_land(k + 1)

        def last(l, acc):
            t = basis[ITERS - 1]
            v = [t[l, ct, own] for ct in everywhere]
            aside = right_of(v, lane_o)
            for ct in inner:
                near = face_l[l, ct, own] * t[l + 1, ct, own] + face_c[l, ct, own] * aside[ct]
                near = v[ct] * (near + face_r[l, ct, own] * t[l, ct, RIM + 1:RIM + rows + 1])
                for i in range(0, rows, RIM):
                    acc = acc + near[i:i + RIM]
            return acc

        h.append(2.0 * by_group(1, total + 1, layers, last, none))

        flat = jnp.concatenate([jnp.sum(v, axis=0, keepdims=True) for v in g + h], axis=0)
        part = LANES // (2 * ITERS)
        by = LANES // 2
        while by >= part:
            flat = flat + pltpu.roll(flat, by, 1)
            by //= 2
        which = lax.broadcasted_iota(jnp.int32, flat.shape, 0)
        group = lax.broadcasted_iota(jnp.int32, flat.shape, 1) // part
        mine = sec * n_gx + gx
        stats[c, mine] = jnp.sum(jnp.where(which == group, flat, 0.0), axis=0, keepdims=True)
        if c == 0:
            pl.semaphore_wait(met_sem, n_sec - 1)
        sends = []
        for k, peer in enumerate(everyone):
            copy = pltpu.make_async_remote_copy(
                src_ref=stats.at[c, mine],
                dst_ref=stats.at[c, mine],
                send_sem=sum_send.at[c, k],
                recv_sem=sum_recv.at[c, k],
                device_id=peer,
                device_id_type=MESH,
            )
            copy.start()
            sends.append(copy)
        for copy in sends:
            copy.wait()
        summed = stats[c, 0]
        for k in range(1, n_sec * n_gx):
            summed = summed + stats[c, k]
        parts = [
            jnp.sum(jnp.where(group[0:1] == k, summed, 0.0), axis=1, keepdims=True)
            for k in range(2 * ITERS)
        ]
        x = coefficients(parts[:ITERS], parts[ITERS:])
        x = [jnp.broadcast_to(v, (rows, LANES)) for v in x]

        def update(l, carry):
            for ct in inner:
                v = head[l, ct, own]
                for k in range(ITERS):
                    v = v + x[k] * basis[k][l, ct, own]
                head[l, ct, own] = v
                if c + 1 < steps:
                    v = head[l, ct, RIM + rows:RIM + rows + 1]
                    for k in range(ITERS):
                        v = v + x[k][0:1] * basis[k][l, ct, RIM + rows:RIM + rows + 1]
                    head[l, ct, RIM + rows:RIM + rows + 1] = v
            return carry

        if c + 1 == steps:
            for i in range(1, n_sec):
                peer = sec_peers[i - 1]
                by_group(1 + peer * layers, 1 + (peer + 1) * layers, layers, update, 0)
                for copy in back_copies(i - 1, peer):
                    copy.start()
                    outgoing.append(copy)
            by_group(1 + sec * layers, 1 + (sec + 1) * layers, layers, update, 0)
        else:
            by_group(1, total + 1, layers, update, 0)
            for d in (0, 1):
                @pl.when(sends_to(d))
                def _(d=d):
                    for k in range(ITERS):
                        land_copy(k, d).wait_send()
                    for k in range(ITERS):
                        land_copy(k, 1 - d).wait_recv()

            def update_rim(i, carry):
                for d in (0, 1):
                    first_row = RIM + rows + 1 if d == 0 else RIM - LOW
                    at_rows = slice(first_row, first_row + LOW)
                    for ct in inner:
                        for j in (0, 1):
                            v = head[1 + 2 * i + j, ct, at_rows]
                            for k in range(ITERS):
                                v = v + x[k][0:LOW] * landed[c, k, d, i, ct, j * LOW:j * LOW + LOW]
                            head[1 + 2 * i + j, ct, at_rows] = v
                return carry

            by_group(0, total // 2, 2, update_rim, 0)

    for ct in inner:
        copy = pltpu.make_async_copy(
            head.at[layers_of(sec), ct, own], out_ref.at[:, :, lanes_at(here, ct)], back_send.at[n_sec - 1, ct]
        )
        copy.start()
        outgoing.append(copy)
    for copy in outgoing:
        copy.wait()


def body(n_sec, n_gx, start, soil, conductivity, storage, rain):
    layers, rows, wide = start.shape
    steps = rain.shape[0]
    cols = wide // n_sec
    tiles = cols // LANES
    total = layers * n_sec
    assert total * RIM <= LANES and cols % LANES == 0 and rows % RIM == 0 and n_sec == 4
    assert layers * 2 * RIM <= LANES and layers % 2 == 0 and n_gx & (n_gx - 1) == 0
    ext = rows + 2 * RIM
    f32, i32 = jnp.float32, jnp.int32
    field = pltpu.VMEM((total + 2, tiles + 1, ext, LANES), f32)
    per_sec = pltpu.VMEM((n_sec, tiles + 1, ext, LANES), f32)
    dma = pltpu.SemaphoreType.DMA
    hbm = pl.BlockSpec(memory_space=pl.ANY)
    smem = pl.BlockSpec(memory_space=pltpu.SMEM)
    return tuple(pl.pallas_call(
        functools.partial(kernel, n_sec, n_gx, steps, conductivity.shape[0]),
        out_shape=(
            jax.ShapeDtypeStruct(start.shape, f32),
            jax.ShapeDtypeStruct((1, steps, rows, wide), f32),
        ),
        in_specs=[hbm, hbm, smem, smem, hbm],
        out_specs=(hbm, hbm),
        scratch_shapes=[field, pltpu.VMEM((total + 2, tiles + 1, ext, LANES), i32)]
        + [field] * 13
        + [per_sec] * 3
        + [
            pltpu.VMEM((steps, tiles + 1, ext, LANES), f32),
            pltpu.VMEM((n_sec, steps, rows, cols), f32),
            pltpu.VMEM((steps - 1, 2, ext, LANES), f32),
            pltpu.VMEM((steps - 1, 2, ext, LANES), f32),
            pltpu.VMEM((n_sec, ext, LANES), f32),
            pltpu.VMEM((n_sec, ext, LANES), i32),
            pltpu.VMEM((n_sec, rows, LANES), f32),
            pltpu.VMEM((n_sec, rows, LANES), i32),
            pltpu.VMEM(start.shape, f32),
            pltpu.VMEM(start.shape, i32),
            pltpu.VMEM(rain.shape, f32),
            pltpu.VMEM((ITERS, 2, total // 2, tiles, RIM, LANES), f32),
            pltpu.VMEM((steps - 1, ITERS, 2, total // 2, tiles, RIM, LANES), f32),
            pltpu.VMEM((steps, n_sec * n_gx, 1, LANES), f32),
            pltpu.SemaphoreType.REGULAR,
            dma((2, tiles + 1)),
            dma((3,)),
            dma((n_sec - 1, 2, tiles + 1)),
            dma((n_sec - 1, 2, tiles + 1)),
            dma((n_sec, 2, 2, 2)),
            dma((n_sec, 2, 2, 2)),
            dma((2,)),
            dma((2,)),
            dma((steps - 1, 2)),
            dma((steps - 1, 2)),
            dma((steps - 1, ITERS, 2)),
            dma((steps - 1, ITERS, 2)),
            dma((steps, n_sec * n_gx)),
            dma((steps, n_sec * n_gx)),
            dma((steps, n_sec)),
            dma((steps, n_sec)),
            dma((n_sec, tiles)),
            dma((n_sec, tiles)),
        ],
        compiler_params=pltpu.CompilerParams(collective_id=0, has_side_effects=True),
    )(start, soil, conductivity, storage, rain))


def solution(mesh):
    placed = (P("sec", "gx", None), P("sec", "gx", None), P(), P(), P(None, "gx", None))
    return jax.shard_map(
        functools.partial(body, mesh.shape["sec"], mesh.shape["gx"]),
        mesh=mesh,
        in_specs=placed,
        out_specs=(P("sec", "gx", None), P("sec", None, "gx", None)),
        check_vma=False,
    )
```

```python
import functools

import jax
import jax.numpy as jnp
from jax import lax
from jax.experimental import pallas as pl
from jax.experimental.pallas import tpu as pltpu
from jax.sharding import PartitionSpec as P


MESH = pl.DeviceIdType.MESH
RIM = 8
LANES = 128
ITERS = 4
LOW = RIM // 2


def by_group(low, high, each, body, carry):
    def trip(i, carry):
        for j in range(each):
            carry = body(low + i * each + j, carry)
        return carry

    return lax.fori_loop(0, (high - low) // each, trip, carry)


def place_of(s):
    return s + s // 2 - 2 * (s // 3)


def mirrored(a, mask, count):
    out, bit = 0, 1
    while bit < count:
        out = out + lax.rem(a // bit + (mask // bit) % 2, 2) * bit
        bit *= 2
    return out


def coefficients(g, h):
    nu = [g[0], h[0]]
    for k in range(1, ITERS):
        nu.append(2.0 * g[k] - nu[0])
        nu.append(4.0 * h[k] - 2.0 * nu[1] - nu[2 * k - 1])

    def gram(i, j):
        return 0.5 * (nu[i + j] + nu[abs(i - j)])

    def gram_a(i, j):
        shifted = gram(i, 1) if j == 0 else 0.5 * (gram(i, j + 1) + gram(i, j - 1))
        return gram(i, j) - shifted

    G = [[gram(i, j) for j in range(ITERS)] for i in range(ITERS)]
    H = [[gram_a(max(i, j), min(i, j)) for j in range(ITERS)] for i in range(ITERS)]
    zero = jnp.zeros_like(g[0])

    def form(matrix, v, top):
        total = zero
        for i in range(top + 1):
            row = matrix[i][i] * v[i]
            for j in range(i):
                row = row + 2.0 * matrix[i][j] * v[j]
            total = total + row * v[i]
        return total

    z = [zero + 1.0] + [zero] * (ITERS - 1)
    p = list(z)
    x = [zero] * ITERS
    rz = nu[0]
    for k in range(ITERS):
        curve = form(H, p, k)
        alpha = jnp.where(curve > 0.0, rz / jnp.where(curve > 0.0, curve, 1.0), 0.0)
        x = [a + alpha * b for a, b in zip(x, p)]
        if k + 1 < ITERS:
            image = list(p)
            for i in range(k + 1):
                if i == 0:
                    image[1] = image[1] - p[0]
                else:
                    image[i + 1] = image[i + 1] - 0.5 * p[i]
                    image[i - 1] = image[i - 1] - 0.5 * p[i]
            z = [a - alpha * b for a, b in zip(z, image)]
            new = jnp.maximum(form(G, z, k + 1), 0.0)
            beta = jnp.where(rz > 0.0, new / jnp.where(rz > 0.0, rz, 1.0), 0.0)
            p = [a + beta * b for a, b in zip(z, p)]
            rz = new
    return x


def kernel(
    n_sec, n_gx, steps, kinds,
    start_ref, soil_ref, cond_ref, store_ref, rain_ref,
    out_ref, flow_ref,
    head, soils, kind, store, cond, cap, face_l, face_r, face_c, diag, dinv, t0, t1, t2, t3,
    water, enter, leave, rainx, flows, pack_out, pack_in, edge_f, edge_i, edges_f, edges_i,
    stage_f, stage_i, stage_r, rows_out, landed, stats, gauge, of_kind,
    met_sem, load_sem, table_sem, own_sem, swap_send, swap_recv, row_send, row_recv, rain_recv,
    col_send, col_recv, land_send, land_recv, sum_send, sum_recv, out_send, out_recv, out_own,
):
    f32 = jnp.float32
    layers, rows, wide = start_ref.shape
    cols = wide // n_sec
    tiles = cols // LANES
    total = layers * n_sec
    ext = rows + 2 * RIM
    sec, gx = lax.axis_index("sec"), lax.axis_index("gx")
    here = place_of(sec)
    own = slice(RIM, RIM + rows)
    work = slice(LOW, ext - LOW)
    above = slice(LOW - 1, ext - LOW - 1)
    under = slice(LOW + 1, ext - LOW + 1)
    everywhere = list(range(tiles + 1))
    inner = list(range(tiles))

    def lanes_at(place, tile):
        return pl.ds(pl.multiple_of(place * cols + tile * LANES, LANES), LANES)

    def layers_of(s):
        return pl.ds(1 + s * layers, layers)

    sec_peers = [lax.rem(sec + k, n_sec) for k in range(1, n_sec)]
    sec_froms = [lax.rem(sec + n_sec - k, n_sec) for k in range(n_sec)]
    gx_peers = [lax.rem(gx + k, n_gx) for k in range(1, n_gx)]
    swap_size = 2 * rows * (layers * tiles + 1)
    row_size = 2 * RIM * (layers * tiles + 1)
    rain_size = steps * (tiles + 1) * RIM
    land_size = ITERS * (total // 2) * tiles * RIM
    flow_size = steps * rows * tiles
    back_size = layers * rows * tiles

    def drain(size, sem):
        lot = gauge.at[0:size]
        pltpu.make_async_copy(lot, lot, sem).wait()

    everyone = [
        {"sec": mirrored(sec, i, n_sec), "gx": mirrored(gx, j, n_gx)}
        for j in reversed(range(n_gx)) for i in reversed(range(n_sec)) if i + j
    ]

    loads = [
        pltpu.make_async_copy(src, dst, load_sem)
        for src, dst in ((start_ref, stage_f), (soil_ref, stage_i), (rain_ref, stage_r))
    ]
    tables = [
        pltpu.make_async_copy(src, of_kind.at[f], table_sem.at[f]) for f, src in enumerate((cond_ref, store_ref))
    ]
    loads += tables
    for copy in loads:
        copy.start()
    barrier = pltpu.get_barrier_semaphore()
    for peer in sec_peers:
        pl.semaphore_signal(barrier, inc=1, device_id={"sec": peer}, device_id_type=MESH)
    for peer in gx_peers:
        pl.semaphore_signal(barrier, inc=1, device_id={"gx": peer}, device_id_type=MESH)

    def nil(*shape, dtype=f32):
        return jnp.zeros(shape, dtype)

    for ref in (head, cond, t0, t1, t2, t3, face_l):
        ref[0] = nil(tiles + 1, ext, LANES)
        ref[total + 1] = nil(tiles + 1, ext, LANES)

    def hem(l, carry):
        for ref in (t0, t1, t2, t3, face_r):
            ref[l, :, 0:RIM] = nil(tiles + 1, RIM, LANES)
            ref[l, :, ext - RIM:ext] = nil(tiles + 1, RIM, LANES)
        return carry

    lax.fori_loop(1, total + 1, hem, 0)
    for d in (0, 1):
        rim = slice(ext - RIM, ext) if d == 0 else slice(0, RIM)

        @pl.when(gx == n_gx - 1 if d == 0 else gx == 0)
        def _(d=d, rim=rim):
            def wipe(l, carry):
                head[l + 1, :, rim] = nil(tiles + 1, RIM, LANES)
                soils[l + 1, :, rim] = nil(tiles + 1, RIM, LANES, dtype=jnp.int32)
                return carry

            lax.fori_loop(0, total, wipe, 0)
            for c in range(steps):
                rainx[c, :, rim] = nil(tiles + 1, RIM, LANES)
            edge_f[:, rim] = nil(n_sec, RIM, LANES)
            edge_i[:, rim] = nil(n_sec, RIM, LANES, dtype=jnp.int32)
            for c in range(steps - 1):
                for k in range(ITERS):
                    landed[c, k, d] = nil(total // 2, tiles, RIM, LANES)

        @pl.when(here == n_sec - 1 if d == 0 else here == 0)
        def _(d=d):
            for c in range(steps - 1):
                pack_in[c, d] = nil(ext, LANES)

    lane = lax.broadcasted_iota(jnp.int32, (ext, LANES), 1)
    lane_w = lax.broadcasted_iota(jnp.int32, (rows + RIM, LANES), 1)
    lane_o = lax.broadcasted_iota(jnp.int32, (rows, LANES), 1)
    at_row = lax.broadcasted_iota(jnp.int32, (ext, LANES), 0)
    beyond = ((at_row >= rows + RIM) & (gx == n_gx - 1)) | ((at_row < RIM) & (gx == 0))
    beside = (lane >= RIM) & (lane < LANES - RIM)
    beside = beside | ((lane < RIM) & (here == n_sec - 1)) | ((lane >= LANES - RIM) & (here == 0))
    outside = [beyond] * tiles + [beyond | beside]

    drain((2 * layers + steps) * rows * wide // LANES, load_sem)

    after = lanes_at(lax.rem(here + 1, n_sec), 0)
    before = lanes_at(lax.rem(here + n_sec - 1, n_sec), tiles - 1)
    for c in range(steps):
        for ct in inner:
            rainx[c, ct, own] = stage_r[c, :, lanes_at(here, ct)]
        rainx[c, tiles, own] = jnp.where(lane_o < LANES // 2, stage_r[c, :, after], stage_r[c, :, before])
    for stage, edges in ((stage_f, edges_f), (stage_i, edges_i)):
        for place in range(n_sec):
            out = nil(rows, LANES, dtype=stage.dtype)
            for j in range(layers):
                right = nil(rows, LANES, dtype=stage.dtype)
                left = right
                if place + 1 < n_sec:
                    right = stage[j, :, (place + 1) * cols:(place + 1) * cols + LANES]
                if place > 0:
                    left = stage[j, :, place * cols - LANES:place * cols]
                both = jnp.where(lane_o < RIM, right, left)
                moved = pltpu.roll(both, (2 * RIM * j + RIM) % LANES, 1)
                out = jnp.where(lane_o // (2 * RIM) == j, moved, out)
            edges[place] = out

    pl.semaphore_wait(barrier, n_sec + n_gx - 2)
    for peer in sec_peers:
        pl.semaphore_signal(met_sem, inc=1, device_id={"sec": peer}, device_id_type=MESH)

    parcels = ((stage_i, soils, edges_i, edge_i), (stage_f, head, edges_f, edge_f))
    swaps = [[] for _ in range(n_sec)]
    for f, (stage, field, edges, edge) in enumerate(parcels):
        for ct in inner:
            swaps[0].append(pltpu.make_async_copy(
                stage.at[:, :, lanes_at(here, ct)], field.at[layers_of(sec), ct, own], own_sem
            ))
        swaps[0].append(pltpu.make_async_copy(edges.at[here], edge.at[sec, own], own_sem))
    for k, peer in enumerate(sec_peers):
        for f, (stage, field, edges, edge) in enumerate(parcels):
            moves = [
                (stage.at[:, :, lanes_at(place_of(peer), ct)], field.at[layers_of(sec), ct, own]) for ct in inner
            ]
            moves.append((edges.at[place_of(peer)], edge.at[sec, own]))
            for m, (src, dst) in enumerate(moves):
                swaps[k + 1].append(pltpu.make_async_remote_copy(
                    src_ref=src,
                    dst_ref=dst,
                    send_sem=swap_send,
                    recv_sem=swap_recv.at[k],
                    device_id={"sec": peer},
                    device_id_type=MESH,
                ))
    for moves in swaps:
        for copy in moves:
            copy.start()

    def toward(d):
        return lax.rem(gx + n_gx - 1, n_gx) if d == 0 else lax.rem(gx + 1, n_gx)

    def ends(d):
        return (slice(RIM, 2 * RIM), slice(ext - RIM, ext)) if d == 0 else (slice(rows, rows + RIM), slice(0, RIM))

    def sends_to(d):
        return gx > 0 if d == 0 else gx < n_gx - 1

    def rain_copy(d):
        src, dst = ends(d)
        return pltpu.make_async_remote_copy(
            src_ref=rainx.at[:, :, src],
            dst_ref=rainx.at[:, :, dst],
            send_sem=row_send.at[d],
            recv_sem=rain_recv.at[d],
            device_id={"gx": toward(d)},
            device_id_type=MESH,
        )

    def row_copies(k, d):
        src, dst = ends(d)
        s = sec_froms[k]
        copies = []
        for f, (_, field, _, edge) in enumerate(parcels):
            pairs = ((field.at[layers_of(s), 0:tiles, src], field.at[layers_of(s), 0:tiles, dst]),
                     (edge.at[s, src], edge.at[s, dst]))
            for m, (a, b) in enumerate(pairs):
                copies.append(pltpu.make_async_remote_copy(
                    src_ref=a,
                    dst_ref=b,
                    send_sem=row_send.at[d],
                    recv_sem=row_recv.at[k, d],
                    device_id={"gx": toward(d)},
                    device_id_type=MESH,
                ))
        return copies

    for d in (0, 1):
        @pl.when(sends_to(d))
        def _(d=d):
            rain_copy(d).start()

    for k in range(n_sec):
        drain(swap_size, own_sem if k == 0 else swap_recv.at[k - 1])
        for d in (0, 1):
            @pl.when(sends_to(d))
            def _(d=d, k=k):
                for copy in row_copies(k, d):
                    copy.start()

    def take_rows(k):
        for d in (0, 1):
            @pl.when(sends_to(d))
            def _(d=d):
                drain(row_size, row_recv.at[k, 1 - d])

    def packed(tile, low):
        outs = nil(ext, LANES)
        for l in range(total):
            shift = (RIM * l if low else RIM * l + RIM) % LANES
            piece = head[1 + l, tile]
            moved = pltpu.roll(piece, shift, 1) if shift else piece
            outs = jnp.where(lane // RIM == l, moved, outs)
        return outs

    def col_copy(c, d):
        return pltpu.make_async_remote_copy(
            src_ref=pack_out.at[c, d],
            dst_ref=pack_in.at[c, d],
            send_sem=col_send.at[d],
            recv_sem=col_recv.at[d],
            device_id={"sec": place_of(lax.rem(here + n_sec - 1, n_sec) if d == 0 else lax.rem(here + 1, n_sec))},
            device_id_type=MESH,
        )

    def send_cols(c):
        for d in (0, 1):
            @pl.when(here > 0 if d == 0 else here < n_sec - 1)
            def _(d=d):
                pack_out[c, d] = packed(0 if d == 0 else tiles - 1, d == 0)
                col_copy(c, d).start()

    def take_cols(c):
        @pl.when(here > 0)
        def _():
            col_copy(c, 0).wait_send()
            col_copy(c, 1).wait_recv()

        @pl.when(here < n_sec - 1)
        def _():
            col_copy(c, 1).wait_send()
            col_copy(c, 0).wait_recv()

        right, left = pack_in[c, 0], pack_in[c, 1]
        for l in range(total):
            a, b = (-RIM * l) % LANES, (LANES - RIM - RIM * l) % LANES
            ra = pltpu.roll(right, a, 1) if a else right
            rb = pltpu.roll(left, b, 1) if b else left
            head[1 + l, tiles] = jnp.where(lane < RIM, ra, jnp.where(lane >= LANES - RIM, rb, 0.0))

    def right_of(v, at):
        moved = [pltpu.roll(a, LANES - 1, 1) for a in v]
        return [jnp.where(at == LANES - 1, moved[(i + 1) % len(v)], moved[i]) for i in range(len(v))]

    def left_of(v, at):
        moved = [pltpu.roll(a, 1, 1) for a in v]
        return [jnp.where(at == 0, moved[i - 1], moved[i]) for i in range(len(v))]

    def harmonic(a, b):
        return 2.0 * a * b / jnp.maximum(a + b, 1e-30)

    half = lax.broadcasted_iota(jnp.int32, (RIM, LANES), 0) >= LOW

    def own_of(v):
        out = jnp.where(half, v[0:RIM], v[rows:rows + RIM])
        for i in range(RIM, rows, RIM):
            out = out + v[i:i + RIM]
        return out

    none = nil(RIM, LANES)
    basis = (t0, t1, t2, t3)

    def back_copies(peer):
        return [
            pltpu.make_async_remote_copy(
                src_ref=head.at[layers_of(peer), ct, own],
                dst_ref=out_ref.at[:, :, lanes_at(here, ct)],
                send_sem=out_send,
                recv_sem=out_recv,
                device_id={"sec": peer},
                device_id_type=MESH,
            )
            for ct in inner
        ]

    def soil(which, s):
        for ct in which:
            amount = nil(ext, LANES)
            for j in range(layers):
                l = 1 + s * layers + j
                sat = jax.nn.sigmoid(head[l, ct])
                cond[l, ct] = kind[l, ct] * (0.05 + sat * sat)
                cap[l, ct] = store[l, ct] * (0.1 + sat * (1.0 - sat))
                amount = amount + sat
            water[s, ct] = amount

    spot = lax.broadcasted_iota(jnp.int32, (ext, LANES), 1)
    of_cond = nil(ext, LANES)
    of_store = nil(ext, LANES)
    for copy in tables:
        copy.wait()
    for k in range(kinds):
        of_cond = jnp.where(spot == k, of_kind[0, k], of_cond)
        of_store = jnp.where(spot == k, of_kind[1, k], of_store)

    def open_edges(s):
        for edge, field in ((edge_f, head), (edge_i, soils)):
            taken = edge[s]
            for j in range(layers):
                moved = pltpu.roll(taken, LANES - RIM - 2 * RIM * j, 1)
                field[1 + s * layers + j, tiles] = jnp.where(
                    (lane < RIM) | (lane >= LANES - RIM), moved, nil(ext, LANES, dtype=field.dtype)
                )

    def look(s):
        for j in range(layers):
            l = 1 + s * layers + j
            for ct in everywhere:
                which = soils[l, ct]
                a = jnp.take_along_axis(of_cond, which, axis=1, mode="promise_in_bounds")
                b = jnp.take_along_axis(of_store, which, axis=1, mode="promise_in_bounds")
                kind[l, ct] = jnp.where(outside[ct], 0.0, a)
                store[l, ct] = jnp.where(outside[ct], 0.0, b)

    for c in range(steps):
        def couple(which, c=c):
            depth = jnp.float32(layers)
            for ct in which:
                below = nil(ext, LANES)
                slopes = [None] * n_sec
                for s in reversed(range(n_sec)):
                    amount = water[s, ct]
                    slopes[s] = amount / depth * (0.5 + 0.5 * below / (below + depth))
                    below = below + amount
                entering = rainx[c, ct]
                for s in range(n_sec):
                    enter[s, ct] = entering
                    if ct < tiles:
                        flows[s, c, :, ct * LANES:(ct + 1) * LANES] = entering[own]
                    entering = slopes[s] * entering + 0.5 * cond[(s + 1) * layers, ct]
                    leave[s, ct] = entering

        def faces(which, l, carry):
            for ct in which:
                k = cond[l, ct, work]
                face_l[l, ct, work] = harmonic(k, cond[l + 1, ct, work])
                face_r[l, ct, work] = harmonic(k, cond[l, ct, under])
            return carry

        def faces_across(l, carry):
            k = [cond[l, ct, work] for ct in everywhere]
            for ct, other in zip(everywhere, right_of(k, lane_w)):
                face_c[l, ct, work] = harmonic(k[ct], other)
            return carry

        def prepare(which, c=c):
            if c > 0:
                def each(s, carry):
                    soil(which, s)
                    return carry

                lax.fori_loop(0, n_sec, each, 0)
            couple(which)
            by_group(1, total + 1, layers, functools.partial(faces, which), 0)

        if c == 0:
            for k in range(n_sec):
                s = sec_froms[k]
                take_rows(k)
                open_edges(s)
                look(s)
                soil(everywhere, s)
            for d in (0, 1):
                @pl.when(sends_to(d))
                def _(d=d):
                    rain_copy(1 - d).wait_recv()
        else:
            send_cols(c - 1)

        prepare(inner)
        own_flow = pltpu.make_async_copy(
            flows.at[sec, c], flow_ref.at[0, c, :, pl.ds(pl.multiple_of(here * cols, LANES), cols)], out_own
        )
        own_flow.start()
        for k, peer in enumerate(sec_peers):
            copy = pltpu.make_async_remote_copy(
                src_ref=flows.at[peer, c],
                dst_ref=flow_ref.at[0, c, :, pl.ds(pl.multiple_of(here * cols, LANES), cols)],
                send_sem=out_send,
                recv_sem=out_recv,
                device_id={"sec": peer},
                device_id_type=MESH,
            )
            copy.start()

        if c > 0:
            take_cols(c - 1)
        prepare([tiles])
        by_group(1, total + 1, layers, faces_across, 0)

        def rows_of(k, l, m):
            if c + 1 < steps:
                i = (l - 1) // 2
                for ct in inner:
                    for j in (0, 1):
                        put = slice(j * LOW, j * LOW + LOW)
                        rows_out[k, 0, i, ct, put] = basis[k][l + j, ct, RIM + 1:RIM + 1 + LOW]
                        rows_out[k, 1, i, ct, put] = basis[k][l + j, ct, RIM + rows - LOW:RIM + rows]

        def first(s, acc):
            for j in range(layers):
                l = 1 + s * layers + j
                fc = [face_c[l, ct, work] for ct in everywhere]
                v = [head[l, ct, work] for ct in everywhere]
                flux = [a * (b - d) for a, b, d in zip(fc, right_of(v, lane_w), v)]
                fb, back = left_of(fc, lane_w), left_of(flux, lane_w)
                for ct in everywhere:
                    up, down = face_l[l - 1, ct, work], face_l[l, ct, work]
                    fr, fa = face_r[l, ct, work], face_r[l, ct, above]
                    whole = cap[l, ct, work] + up + down + fr + fa + fc[ct] + fb[ct]
                    res = up - down + up * (head[l - 1, ct, work] - v[ct]) + down * (head[l + 1, ct, work] - v[ct])
                    res = res + fr * (head[l, ct, under] - v[ct]) + fa * (head[l, ct, above] - v[ct])
                    res = res + flux[ct] - back[ct]
                    if j == 0:
                        res = res + enter[s, ct, work]
                    if j == layers - 1:
                        res = res - leave[s, ct, work]
                    inverse = jnp.where(whole > 0.0, 1.0 / jnp.maximum(whole, 1e-30), 0.0)
                    z = res * inverse
                    diag[l, ct, work] = whole
                    dinv[l, ct, work] = 2.0 * inverse
                    t0[l, ct, work] = z
                    if ct < tiles:
                        acc = acc + own_of(res * z)
            for j in range(0, layers, 2):
                rows_of(0, 1 + s * layers + j, s)
            return acc

        def land_copy(k, d, c=c):
            return pltpu.make_async_remote_copy(
                src_ref=rows_out.at[k, d],
                dst_ref=landed.at[c, k, d],
                send_sem=land_send.at[d],
                recv_sem=land_recv.at[c, d],
                device_id={"gx": toward(d)},
                device_id_type=MESH,
            )

        def send_land(k):
            if c + 1 < steps:
                for d in (0, 1):
                    @pl.when(sends_to(d))
                    def _(d=d):
                        land_copy(k, d).start()

        g = [lax.fori_loop(0, n_sec, first, none)]
        send_land(0)
        h = []
        for k in range(ITERS - 1):
            def apply(i, acc, k=k):
                t = basis[k]
                for j in range(layers):
                    l = 1 + i * layers + j
                    v = [t[l, ct, work] for ct in everywhere]
                    fc = [face_c[l, ct, work] for ct in everywhere]
                    aside = right_of(v, lane_w)
                    back = left_of([a * b for a, b in zip(fc, v)], lane_w)
                    for ct in everywhere:
                        near = face_l[l - 1, ct, work] * t[l - 1, ct, work] + face_l[l, ct, work] * t[l + 1, ct, work]
                        near = near + face_r[l, ct, work] * t[l, ct, under] + face_r[l, ct, above] * t[l, ct, above]
                        near = near + (fc[ct] * aside[ct] + back[ct])
                        new = dinv[l, ct, work] * near
                        new = 0.5 * new if k == 0 else new - basis[k - 1][l, ct, work]
                        basis[k + 1][l, ct, work] = new
                        if ct < tiles:
                            acc = (acc[0] + own_of(v[ct] * near), acc[1] + own_of(diag[l, ct, work] * new * new))
                for j in range(0, layers, 2):
                    rows_of(k + 1, 1 + i * layers + j, i)
                return acc

            ah, ag = lax.fori_loop(0, n_sec, apply, (none, none))
            h.append(ah)
            g.append(ag)
            send_land(k + 1)

        def last(l, acc):
            t = basis[ITERS - 1]
            v = [t[l, ct, own] for ct in everywhere]
            aside = right_of(v, lane_o)
            for ct in inner:
                near = face_l[l, ct, own] * t[l + 1, ct, own] + face_c[l, ct, own] * aside[ct]
                near = v[ct] * (near + face_r[l, ct, own] * t[l, ct, RIM + 1:RIM + rows + 1])
                for i in range(0, rows, RIM):
                    acc = acc + near[i:i + RIM]
            return acc

        h.append(2.0 * by_group(1, total + 1, layers, last, none))

        flat = jnp.concatenate([jnp.sum(v, axis=0, keepdims=True) for v in g + h], axis=0)
        part = LANES // (2 * ITERS)
        by = LANES // 2
        while by >= part:
            flat = flat + pltpu.roll(flat, by, 1)
            by //= 2
        which = lax.broadcasted_iota(jnp.int32, flat.shape, 0)
        group = lax.broadcasted_iota(jnp.int32, flat.shape, 1) // part
        mine = sec * n_gx + gx
        stats[c, mine] = jnp.sum(jnp.where(which == group, flat, 0.0), axis=0, keepdims=True)
        if c == 0:
            pl.semaphore_wait(met_sem, n_sec - 1)
        for k, peer in enumerate(everyone):
            copy = pltpu.make_async_remote_copy(
                src_ref=stats.at[c, mine],
                dst_ref=stats.at[c, mine],
                send_sem=sum_send,
                recv_sem=sum_recv.at[c],
                device_id=peer,
                device_id_type=MESH,
            )
            copy.start()
        drain(len(everyone), sum_recv.at[c])
        drain(len(everyone), sum_send)
        if c == 0:
            for d in (0, 1):
                @pl.when(sends_to(d))
                def _(d=d):
                    drain(n_sec * row_size + rain_size, row_send.at[d])
        summed = stats[c, 0]
        for k in range(1, n_sec * n_gx):
            summed = summed + stats[c, k]
        parts = [
            jnp.sum(jnp.where(group[0:1] == k, summed, 0.0), axis=1, keepdims=True)
            for k in range(2 * ITERS)
        ]
        x = coefficients(parts[:ITERS], parts[ITERS:])
        x = [jnp.broadcast_to(v, (rows, LANES)) for v in x]

        def update(l, carry):
            for ct in inner:
                v = head[l, ct, own]
                for k in range(ITERS):
                    v = v + x[k] * basis[k][l, ct, own]
                head[l, ct, own] = v
                if c + 1 < steps:
                    v = head[l, ct, RIM + rows:RIM + rows + 1]
                    for k in range(ITERS):
                        v = v + x[k][0:1] * basis[k][l, ct, RIM + rows:RIM + rows + 1]
                    head[l, ct, RIM + rows:RIM + rows + 1] = v
            return carry

        if c + 1 == steps:
            for i in range(1, n_sec):
                peer = sec_peers[i - 1]
                by_group(1 + peer * layers, 1 + (peer + 1) * layers, layers, update, 0)
                for copy in back_copies(peer):
                    copy.start()
            by_group(1 + sec * layers, 1 + (sec + 1) * layers, layers, update, 0)
        else:
            by_group(1, total + 1, layers, update, 0)
            for d in (0, 1):
                @pl.when(sends_to(d))
                def _(d=d):
                    drain(land_size, land_send.at[d])
                    drain(land_size, land_recv.at[c, 1 - d])

            def update_rim(i, carry):
                for d in (0, 1):
                    first_row = RIM + rows + 1 if d == 0 else RIM - LOW
                    at_rows = slice(first_row, first_row + LOW)
                    for ct in inner:
                        for j in (0, 1):
                            v = head[1 + 2 * i + j, ct, at_rows]
                            for k in range(ITERS):
                                v = v + x[k][0:LOW] * landed[c, k, d, i, ct, j * LOW:j * LOW + LOW]
                            head[1 + 2 * i + j, ct, at_rows] = v
                return carry

            by_group(0, total // 2, 2, update_rim, 0)

    for ct in inner:
        copy = pltpu.make_async_copy(
            head.at[layers_of(sec), ct, own], out_ref.at[:, :, lanes_at(here, ct)], out_own
        )
        copy.start()
    drain((n_sec - 1) * swap_size, swap_send)
    drain(flow_size + back_size, out_own)
    drain((n_sec - 1) * (flow_size + back_size), out_send)
    drain((n_sec - 1) * (flow_size + back_size), out_recv)


def body(n_sec, n_gx, start, soil, conductivity, storage, rain):
    layers, rows, wide = start.shape
    steps = rain.shape[0]
    cols = wide // n_sec
    tiles = cols // LANES
    total = layers * n_sec
    assert total * RIM <= LANES and cols % LANES == 0 and rows % RIM == 0 and n_sec == 4
    assert layers * 2 * RIM <= LANES and layers % 2 == 0 and n_gx & (n_gx - 1) == 0
    ext = rows + 2 * RIM
    f32, i32 = jnp.float32, jnp.int32
    field = pltpu.VMEM((total + 2, tiles + 1, ext, LANES), f32)
    per_sec = pltpu.VMEM((n_sec, tiles + 1, ext, LANES), f32)
    dma = pltpu.SemaphoreType.DMA
    longest = max(
        (2 * layers + steps) * rows * wide // LANES,
        2 * rows * (layers * tiles + 1) * (n_sec - 1),
        2 * RIM * (layers * tiles + 1) * n_sec + steps * (tiles + 1) * RIM,
        ITERS * (total // 2) * tiles * RIM,
        (n_sec - 1) * (steps + layers) * rows * tiles,
        n_sec * n_gx,
    )
    hbm = pl.BlockSpec(memory_space=pl.ANY)
    return tuple(pl.pallas_call(
        functools.partial(kernel, n_sec, n_gx, steps, conductivity.shape[0]),
        out_shape=(
            jax.ShapeDtypeStruct(start.shape, f32),
            jax.ShapeDtypeStruct((1, steps, rows, wide), f32),
        ),
        in_specs=[hbm] * 5,
        out_specs=(hbm, hbm),
        scratch_shapes=[field, pltpu.VMEM((total + 2, tiles + 1, ext, LANES), i32)]
        + [field] * 13
        + [per_sec] * 3
        + [
            pltpu.VMEM((steps, tiles + 1, ext, LANES), f32),
            pltpu.VMEM((n_sec, steps, rows, cols), f32),
            pltpu.VMEM((steps - 1, 2, ext, LANES), f32),
            pltpu.VMEM((steps - 1, 2, ext, LANES), f32),
            pltpu.VMEM((n_sec, ext, LANES), f32),
            pltpu.VMEM((n_sec, ext, LANES), i32),
            pltpu.VMEM((n_sec, rows, LANES), f32),
            pltpu.VMEM((n_sec, rows, LANES), i32),
            pltpu.VMEM(start.shape, f32),
            pltpu.VMEM(start.shape, i32),
            pltpu.VMEM(rain.shape, f32),
            pltpu.VMEM((ITERS, 2, total // 2, tiles, RIM, LANES), f32),
            pltpu.VMEM((steps - 1, ITERS, 2, total // 2, tiles, RIM, LANES), f32),
            pltpu.VMEM((steps, n_sec * n_gx, 1, LANES), f32),
            pltpu.VMEM((longest, LANES), f32),
            pltpu.SMEM((2, conductivity.shape[0]), f32),
            pltpu.SemaphoreType.REGULAR,
            dma,
            dma((2,)),
            dma,
            dma,
            dma((n_sec - 1,)),
            dma((2,)),
            dma((n_sec, 2)),
            dma((2,)),
            dma((2,)),
            dma((2,)),
            dma((2,)),
            dma((steps - 1, 2)),
            dma,
            dma((steps,)),
            dma,
            dma,
            dma,
        ],
        compiler_params=pltpu.CompilerParams(collective_id=0, has_side_effects=True),
    )(start, soil, conductivity, storage, rain))


def solution(mesh):
    placed = (P("sec", "gx", None), P("sec", "gx", None), P(), P(), P(None, "gx", None))
    return jax.shard_map(
        functools.partial(body, mesh.shape["sec"], mesh.shape["gx"]),
        mesh=mesh,
        in_specs=placed,
        out_specs=(P("sec", "gx", None), P("sec", None, "gx", None)),
        check_vma=False,
    )
```

```python
import functools

import jax
import jax.numpy as jnp
from jax import lax
from jax.experimental import pallas as pl
from jax.experimental.pallas import tpu as pltpu
from jax.sharding import PartitionSpec as P


MESH = pl.DeviceIdType.MESH
RIM = 8
LANES = 128
ITERS = 4
LOW = RIM // 2


def by_group(low, high, each, body, carry):
    def trip(i, carry):
        for j in range(each):
            carry = body(low + i * each + j, carry)
        return carry

    return lax.fori_loop(0, (high - low) // each, trip, carry)


def place_of(s):
    return s + s // 2 - 2 * (s // 3)


def mirrored(a, mask, count):
    out, bit = 0, 1
    while bit < count:
        out = out + lax.rem(a // bit + (mask // bit) % 2, 2) * bit
        bit *= 2
    return out


def coefficients(g, h):
    nu = [g[0], h[0]]
    for k in range(1, ITERS):
        nu.append(2.0 * g[k] - nu[0])
        nu.append(4.0 * h[k] - 2.0 * nu[1] - nu[2 * k - 1])

    def gram(i, j):
        return 0.5 * (nu[i + j] + nu[abs(i - j)])

    def gram_a(i, j):
        shifted = gram(i, 1) if j == 0 else 0.5 * (gram(i, j + 1) + gram(i, j - 1))
        return gram(i, j) - shifted

    G = [[gram(i, j) for j in range(ITERS)] for i in range(ITERS)]
    H = [[gram_a(max(i, j), min(i, j)) for j in range(ITERS)] for i in range(ITERS)]
    zero = jnp.zeros_like(g[0])

    def form(matrix, v, top):
        total = zero
        for i in range(top + 1):
            row = matrix[i][i] * v[i]
            for j in range(i):
                row = row + 2.0 * matrix[i][j] * v[j]
            total = total + row * v[i]
        return total

    z = [zero + 1.0] + [zero] * (ITERS - 1)
    p = list(z)
    x = [zero] * ITERS
    rz = nu[0]
    for k in range(ITERS):
        curve = form(H, p, k)
        alpha = jnp.where(curve > 0.0, rz / jnp.where(curve > 0.0, curve, 1.0), 0.0)
        x = [a + alpha * b for a, b in zip(x, p)]
        if k + 1 < ITERS:
            image = list(p)
            for i in range(k + 1):
                if i == 0:
                    image[1] = image[1] - p[0]
                else:
                    image[i + 1] = image[i + 1] - 0.5 * p[i]
                    image[i - 1] = image[i - 1] - 0.5 * p[i]
            z = [a - alpha * b for a, b in zip(z, image)]
            new = jnp.maximum(form(G, z, k + 1), 0.0)
            beta = jnp.where(rz > 0.0, new / jnp.where(rz > 0.0, rz, 1.0), 0.0)
            p = [a + beta * b for a, b in zip(z, p)]
            rz = new
    return x


def kernel(
    n_sec, n_gx, steps, kinds,
    start_ref, soil_ref, cond_ref, store_ref, rain_ref,
    out_ref, flow_ref,
    head, soils, kind, store, cond, cap, face_l, face_r, face_c, diag, dinv, t,
    water, enter, leave, rainx, flows, pack_out, pack_in, edge_f, edge_i, edges_f, edges_i,
    stage_f, stage_i, stage_r, rows_out, landed, stats, gauge, of_kind,
    met_sem, load_sem, table_sem, own_sem, swap_send, swap_recv, row_send, row_recv, rain_recv,
    col_send, col_recv, land_send, land_recv, sum_send, sum_recv, out_send, out_recv, out_own,
):
    f32 = jnp.float32
    layers, rows, wide = start_ref.shape
    cols = wide // n_sec
    tiles = cols // LANES
    total = layers * n_sec
    ext = rows + 2 * RIM
    sec, gx = lax.axis_index("sec"), lax.axis_index("gx")
    here = place_of(sec)
    own = slice(RIM, RIM + rows)
    work = slice(LOW, ext - LOW)
    above = slice(LOW - 1, ext - LOW - 1)
    under = slice(LOW + 1, ext - LOW + 1)
    everywhere = list(range(tiles + 1))
    inner = list(range(tiles))

    def lanes_at(place, tile):
        return pl.ds(pl.multiple_of(place * cols + tile * LANES, LANES), LANES)

    def layers_of(s):
        return pl.ds(1 + s * layers, layers)

    sec_peers = [lax.rem(sec + k, n_sec) for k in range(1, n_sec)]
    sec_froms = [lax.rem(sec + n_sec - k, n_sec) for k in range(n_sec)]
    gx_peers = [lax.rem(gx + k, n_gx) for k in range(1, n_gx)]
    swap_size = 2 * rows * (layers * tiles + 1)
    row_size = 2 * RIM * (layers * tiles + 1)
    rain_size = steps * (tiles + 1) * RIM
    land_size = ITERS * (total // 2) * tiles * RIM
    flow_size = steps * rows * tiles
    back_size = layers * rows * tiles

    def drain(size, sem):
        lot = gauge.at[0:size]
        pltpu.make_async_copy(lot, lot, sem).wait()

    parts_of = ((0, ITERS - 1), (ITERS - 1, ITERS))
    everyone = [
        {"sec": mirrored(sec, i, n_sec), "gx": mirrored(gx, j, n_gx)}
        for j in reversed(range(n_gx)) for i in reversed(range(n_sec)) if i + j
    ]

    loads = [
        pltpu.make_async_copy(src, dst, load_sem)
        for src, dst in ((start_ref, stage_f), (soil_ref, stage_i), (rain_ref, stage_r))
    ]
    tables = [
        pltpu.make_async_copy(src, of_kind.at[f], table_sem.at[f]) for f, src in enumerate((cond_ref, store_ref))
    ]
    loads += tables
    for copy in loads:
        copy.start()
    barrier = pltpu.get_barrier_semaphore()
    for peer in sec_peers:
        pl.semaphore_signal(barrier, inc=1, device_id={"sec": peer}, device_id_type=MESH)
    for peer in gx_peers:
        pl.semaphore_signal(barrier, inc=1, device_id={"gx": peer}, device_id_type=MESH)

    def nil(*shape, dtype=f32):
        return jnp.zeros(shape, dtype)

    basis = [t.at[k] for k in range(ITERS)]
    for ref in (head, cond, face_l, *basis):
        ref[0] = nil(tiles + 1, ext, LANES)
        ref[total + 1] = nil(tiles + 1, ext, LANES)

    def hem(l, carry):
        for ref in (face_r, *basis):
            ref[l, :, 0:RIM] = nil(tiles + 1, RIM, LANES)
            ref[l, :, ext - RIM:ext] = nil(tiles + 1, RIM, LANES)
        return carry

    lax.fori_loop(1, total + 1, hem, 0)
    for d in (0, 1):
        rim = slice(ext - RIM, ext) if d == 0 else slice(0, RIM)

        @pl.when(gx == n_gx - 1 if d == 0 else gx == 0)
        def _(d=d, rim=rim):
            def wipe(l, carry):
                head[l + 1, :, rim] = nil(tiles + 1, RIM, LANES)
                soils[l + 1, :, rim] = nil(tiles + 1, RIM, LANES, dtype=jnp.int32)
                return carry

            lax.fori_loop(0, total, wipe, 0)
            for c in range(steps):
                rainx[c, :, rim] = nil(tiles + 1, RIM, LANES)
            edge_f[:, rim] = nil(n_sec, RIM, LANES)
            edge_i[:, rim] = nil(n_sec, RIM, LANES, dtype=jnp.int32)
            for c in range(steps - 1):
                for k in range(ITERS):
                    landed[c, k, d] = nil(total // 2, tiles, RIM, LANES)

        @pl.when(here == n_sec - 1 if d == 0 else here == 0)
        def _(d=d):
            for c in range(steps - 1):
                pack_in[c, d] = nil(ITERS, ext, LANES)

    lane = lax.broadcasted_iota(jnp.int32, (ext, LANES), 1)
    lane_w = lax.broadcasted_iota(jnp.int32, (rows + RIM, LANES), 1)
    lane_o = lax.broadcasted_iota(jnp.int32, (rows, LANES), 1)
    at_row = lax.broadcasted_iota(jnp.int32, (ext, LANES), 0)
    beyond = ((at_row >= rows + RIM) & (gx == n_gx - 1)) | ((at_row < RIM) & (gx == 0))
    beside = (lane >= RIM) & (lane < LANES - RIM)
    beside = beside | ((lane < RIM) & (here == n_sec - 1)) | ((lane >= LANES - RIM) & (here == 0))
    outside = [beyond] * tiles + [beyond | beside]

    drain((2 * layers + steps) * rows * wide // LANES, load_sem)

    after = lanes_at(lax.rem(here + 1, n_sec), 0)
    before = lanes_at(lax.rem(here + n_sec - 1, n_sec), tiles - 1)
    for c in range(steps):
        for ct in inner:
            rainx[c, ct, own] = stage_r[c, :, lanes_at(here, ct)]
        rainx[c, tiles, own] = jnp.where(lane_o < LANES // 2, stage_r[c, :, after], stage_r[c, :, before])
    for stage, edges in ((stage_f, edges_f), (stage_i, edges_i)):
        for place in range(n_sec):
            out = nil(rows, LANES, dtype=stage.dtype)
            for j in range(layers):
                right = nil(rows, LANES, dtype=stage.dtype)
                left = right
                if place + 1 < n_sec:
                    right = stage[j, :, (place + 1) * cols:(place + 1) * cols + LANES]
                if place > 0:
                    left = stage[j, :, place * cols - LANES:place * cols]
                both = jnp.where(lane_o < RIM, right, left)
                moved = pltpu.roll(both, (2 * RIM * j + RIM) % LANES, 1)
                out = jnp.where(lane_o // (2 * RIM) == j, moved, out)
            edges[place] = out

    pl.semaphore_wait(barrier, n_sec + n_gx - 2)
    for peer in sec_peers:
        pl.semaphore_signal(met_sem, inc=1, device_id={"sec": peer}, device_id_type=MESH)

    parcels = ((stage_i, soils, edges_i, edge_i), (stage_f, head, edges_f, edge_f))
    swaps = [[] for _ in range(n_sec)]
    for f, (stage, field, edges, edge) in enumerate(parcels):
        for ct in inner:
            swaps[0].append(pltpu.make_async_copy(
                stage.at[:, :, lanes_at(here, ct)], field.at[layers_of(sec), ct, own], own_sem
            ))
        swaps[0].append(pltpu.make_async_copy(edges.at[here], edge.at[sec, own], own_sem))
    for k, peer in enumerate(sec_peers):
        for f, (stage, field, edges, edge) in enumerate(parcels):
            moves = [
                (stage.at[:, :, lanes_at(place_of(peer), ct)], field.at[layers_of(sec), ct, own]) for ct in inner
            ]
            moves.append((edges.at[place_of(peer)], edge.at[sec, own]))
            for m, (src, dst) in enumerate(moves):
                swaps[k + 1].append(pltpu.make_async_remote_copy(
                    src_ref=src,
                    dst_ref=dst,
                    send_sem=swap_send,
                    recv_sem=swap_recv.at[k],
                    device_id={"sec": peer},
                    device_id_type=MESH,
                ))
    for moves in swaps:
        for copy in moves:
            copy.start()

    def toward(d):
        return lax.rem(gx + n_gx - 1, n_gx) if d == 0 else lax.rem(gx + 1, n_gx)

    def ends(d):
        return (slice(RIM, 2 * RIM), slice(ext - RIM, ext)) if d == 0 else (slice(rows, rows + RIM), slice(0, RIM))

    def sends_to(d):
        return gx > 0 if d == 0 else gx < n_gx - 1

    def rain_copy(d):
        src, dst = ends(d)
        return pltpu.make_async_remote_copy(
            src_ref=rainx.at[:, :, src],
            dst_ref=rainx.at[:, :, dst],
            send_sem=row_send.at[d],
            recv_sem=rain_recv.at[d],
            device_id={"gx": toward(d)},
            device_id_type=MESH,
        )

    def row_copies(k, d):
        src, dst = ends(d)
        s = sec_froms[k]
        copies = []
        for f, (_, field, _, edge) in enumerate(parcels):
            pairs = ((field.at[layers_of(s), 0:tiles, src], field.at[layers_of(s), 0:tiles, dst]),
                     (edge.at[s, src], edge.at[s, dst]))
            for m, (a, b) in enumerate(pairs):
                copies.append(pltpu.make_async_remote_copy(
                    src_ref=a,
                    dst_ref=b,
                    send_sem=row_send.at[d],
                    recv_sem=row_recv.at[k, d],
                    device_id={"gx": toward(d)},
                    device_id_type=MESH,
                ))
        return copies

    for d in (0, 1):
        @pl.when(sends_to(d))
        def _(d=d):
            rain_copy(d).start()

    for k in range(n_sec):
        drain(swap_size, own_sem if k == 0 else swap_recv.at[k - 1])
        for d in (0, 1):
            @pl.when(sends_to(d))
            def _(d=d, k=k):
                for copy in row_copies(k, d):
                    copy.start()

    def take_rows(k):
        for d in (0, 1):
            @pl.when(sends_to(d))
            def _(d=d):
                drain(row_size, row_recv.at[k, 1 - d])

    def packed(k, tile, low):
        outs = nil(ext, LANES)
        for l in range(total):
            shift = (RIM * l if low else RIM * l + RIM) % LANES
            piece = t[k, 1 + l, tile]
            moved = pltpu.roll(piece, shift, 1) if shift else piece
            outs = jnp.where(lane // RIM == l, moved, outs)
        return outs

    def col_copy(c, d, part):
        low, high = parts_of[part]
        return pltpu.make_async_remote_copy(
            src_ref=pack_out.at[d, low:high],
            dst_ref=pack_in.at[c, d, low:high],
            send_sem=col_send.at[d],
            recv_sem=col_recv.at[c, d, part],
            device_id={"sec": place_of(lax.rem(here + n_sec - 1, n_sec) if d == 0 else lax.rem(here + 1, n_sec))},
            device_id_type=MESH,
        )

    def beside_to(d):
        return here > 0 if d == 0 else here < n_sec - 1

    def settle(c, part):
        low, high = parts_of[part]
        for d in (0, 1):
            @pl.when(sends_to(d))
            def _(d=d):
                drain((high - low) * land_size // ITERS, land_recv.at[c, 1 - d, part])

        def place(i, carry):
            for d in (0, 1):
                first_row = RIM + rows + 1 if d == 0 else RIM - LOW
                for k in range(low, high):
                    for ct in inner:
                        for j in (0, 1):
                            t[k, 1 + 2 * i + j, ct, first_row:first_row + LOW] = landed[
                                c, k, d, i, ct, j * LOW:j * LOW + LOW
                            ]
            return carry

        by_group(0, total // 2, 2, place, 0)
        for d in (0, 1):
            @pl.when(beside_to(d))
            def _(d=d):
                def each(k, carry):
                    pack_out[d, k] = packed(k, 0 if d == 0 else tiles - 1, d == 0)
                    return carry

                lax.fori_loop(low, high, each, 0)
                col_copy(c, d, part).start()

    def take_cols(c, part):
        low, high = parts_of[part]
        for d in (0, 1):
            @pl.when(beside_to(d))
            def _(d=d):
                col_copy(c, 1 - d, part).wait_recv()

        def each(k, carry):
            right, left = pack_in[c, 0, k], pack_in[c, 1, k]
            for l in range(total):
                a, b = (-RIM * l) % LANES, (LANES - RIM - RIM * l) % LANES
                ra = pltpu.roll(right, a, 1) if a else right
                rb = pltpu.roll(left, b, 1) if b else left
                t[k, 1 + l, tiles] = jnp.where(lane < RIM, ra, jnp.where(lane >= LANES - RIM, rb, 0.0))
            return carry

        lax.fori_loop(low, high, each, 0)

    def right_of(v, at):
        moved = [pltpu.roll(a, LANES - 1, 1) for a in v]
        return [jnp.where(at == LANES - 1, moved[(i + 1) % len(v)], moved[i]) for i in range(len(v))]

    def left_of(v, at):
        moved = [pltpu.roll(a, 1, 1) for a in v]
        return [jnp.where(at == 0, moved[i - 1], moved[i]) for i in range(len(v))]

    def harmonic(a, b):
        return 2.0 * a * b / jnp.maximum(a + b, 1e-30)

    half = lax.broadcasted_iota(jnp.int32, (RIM, LANES), 0) >= LOW

    def own_of(v):
        out = jnp.where(half, v[0:RIM], v[rows:rows + RIM])
        for i in range(RIM, rows, RIM):
            out = out + v[i:i + RIM]
        return out

    none = nil(RIM, LANES)

    def back_copies(peer):
        return [
            pltpu.make_async_remote_copy(
                src_ref=head.at[layers_of(peer), ct, own],
                dst_ref=out_ref.at[:, :, lanes_at(here, ct)],
                send_sem=out_send,
                recv_sem=out_recv,
                device_id={"sec": peer},
                device_id_type=MESH,
            )
            for ct in inner
        ]

    def soil(which, s):
        for ct in which:
            amount = nil(ext, LANES)
            for j in range(layers):
                l = 1 + s * layers + j
                sat = jax.nn.sigmoid(head[l, ct])
                cond[l, ct] = kind[l, ct] * (0.05 + sat * sat)
                cap[l, ct] = store[l, ct] * (0.1 + sat * (1.0 - sat))
                amount = amount + sat
            water[s, ct] = amount

    spot = lax.broadcasted_iota(jnp.int32, (ext, LANES), 1)
    of_cond = nil(ext, LANES)
    of_store = nil(ext, LANES)
    for copy in tables:
        copy.wait()
    for k in range(kinds):
        of_cond = jnp.where(spot == k, of_kind[0, k], of_cond)
        of_store = jnp.where(spot == k, of_kind[1, k], of_store)

    def open_edges(s):
        for edge, field in ((edge_f, head), (edge_i, soils)):
            taken = edge[s]
            for j in range(layers):
                moved = pltpu.roll(taken, LANES - RIM - 2 * RIM * j, 1)
                field[1 + s * layers + j, tiles] = jnp.where(
                    (lane < RIM) | (lane >= LANES - RIM), moved, nil(ext, LANES, dtype=field.dtype)
                )

    def look(s):
        for j in range(layers):
            l = 1 + s * layers + j
            for ct in everywhere:
                which = soils[l, ct]
                a = jnp.take_along_axis(of_cond, which, axis=1, mode="promise_in_bounds")
                b = jnp.take_along_axis(of_store, which, axis=1, mode="promise_in_bounds")
                kind[l, ct] = jnp.where(outside[ct], 0.0, a)
                store[l, ct] = jnp.where(outside[ct], 0.0, b)

    for c in range(steps):
        def couple(which, c=c):
            depth = jnp.float32(layers)
            for ct in which:
                below = nil(ext, LANES)
                slopes = [None] * n_sec
                for s in reversed(range(n_sec)):
                    amount = water[s, ct]
                    slopes[s] = amount / depth * (0.5 + 0.5 * below / (below + depth))
                    below = below + amount
                entering = rainx[c, ct]
                for s in range(n_sec):
                    enter[s, ct] = entering
                    if ct < tiles:
                        flows[s, c, :, ct * LANES:(ct + 1) * LANES] = entering[own]
                    entering = slopes[s] * entering + 0.5 * cond[(s + 1) * layers, ct]
                    leave[s, ct] = entering

        def faces(l, carry):
            k = [cond[l, ct, work] for ct in everywhere]
            for ct, other in zip(everywhere, right_of(k, lane_w)):
                face_l[l, ct, work] = harmonic(k[ct], cond[l + 1, ct, work])
                face_r[l, ct, work] = harmonic(k[ct], cond[l, ct, under])
                face_c[l, ct, work] = harmonic(k[ct], other)
            return carry

        if c == 0:
            for k in range(n_sec):
                s = sec_froms[k]
                take_rows(k)
                open_edges(s)
                look(s)
                soil(everywhere, s)
            for d in (0, 1):
                @pl.when(sends_to(d))
                def _(d=d):
                    rain_copy(1 - d).wait_recv()
        else:
            def each(s, carry):
                soil(everywhere, s)
                return carry

            lax.fori_loop(0, n_sec, each, 0)
        couple(everywhere)
        own_flow = pltpu.make_async_copy(
            flows.at[sec, c], flow_ref.at[0, c, :, pl.ds(pl.multiple_of(here * cols, LANES), cols)], out_own
        )
        own_flow.start()
        for k, peer in enumerate(sec_peers):
            copy = pltpu.make_async_remote_copy(
                src_ref=flows.at[peer, c],
                dst_ref=flow_ref.at[0, c, :, pl.ds(pl.multiple_of(here * cols, LANES), cols)],
                send_sem=out_send,
                recv_sem=out_recv,
                device_id={"sec": peer},
                device_id_type=MESH,
            )
            copy.start()

        by_group(1, total + 1, layers, faces, 0)

        def rows_of(k, l, m):
            if c + 1 < steps:
                i = (l - 1) // 2
                for ct in inner:
                    for j in (0, 1):
                        put = slice(j * LOW, j * LOW + LOW)
                        rows_out[k, 0, i, ct, put] = basis[k][l + j, ct, RIM + 1:RIM + 1 + LOW]
                        rows_out[k, 1, i, ct, put] = basis[k][l + j, ct, RIM + rows - LOW:RIM + rows]

        def first(s, acc):
            for j in range(layers):
                l = 1 + s * layers + j
                fc = [face_c[l, ct, work] for ct in everywhere]
                v = [head[l, ct, work] for ct in everywhere]
                flux = [a * (b - d) for a, b, d in zip(fc, right_of(v, lane_w), v)]
                fb, back = left_of(fc, lane_w), left_of(flux, lane_w)
                for ct in everywhere:
                    up, down = face_l[l - 1, ct, work], face_l[l, ct, work]
                    fr, fa = face_r[l, ct, work], face_r[l, ct, above]
                    whole = cap[l, ct, work] + up + down + fr + fa + fc[ct] + fb[ct]
                    res = up - down + up * (head[l - 1, ct, work] - v[ct]) + down * (head[l + 1, ct, work] - v[ct])
                    res = res + fr * (head[l, ct, under] - v[ct]) + fa * (head[l, ct, above] - v[ct])
                    res = res + flux[ct] - back[ct]
                    if j == 0:
                        res = res + enter[s, ct, work]
                    if j == layers - 1:
                        res = res - leave[s, ct, work]
                    inverse = jnp.where(whole > 0.0, 1.0 / jnp.maximum(whole, 1e-30), 0.0)
                    z = res * inverse
                    diag[l, ct, work] = whole
                    dinv[l, ct, work] = 2.0 * inverse
                    basis[0][l, ct, work] = z
                    if ct < tiles:
                        acc = acc + own_of(res * z)
            for j in range(0, layers, 2):
                rows_of(0, 1 + s * layers + j, s)
            return acc

        def land_copy(k, d, c=c):
            return pltpu.make_async_remote_copy(
                src_ref=rows_out.at[k, d],
                dst_ref=landed.at[c, k, d],
                send_sem=land_send.at[d],
                recv_sem=land_recv.at[c, d, 0 if k < ITERS - 1 else 1],
                device_id={"gx": toward(d)},
                device_id_type=MESH,
            )

        def send_land(k):
            if c + 1 < steps:
                for d in (0, 1):
                    @pl.when(sends_to(d))
                    def _(d=d):
                        land_copy(k, d).start()

        g = [lax.fori_loop(0, n_sec, first, none)]
        send_land(0)
        h = []
        for k in range(ITERS - 1):
            def apply(i, acc, k=k):
                v_of = basis[k]
                for j in range(layers):
                    l = 1 + i * layers + j
                    v = [v_of[l, ct, work] for ct in everywhere]
                    fc = [face_c[l, ct, work] for ct in everywhere]
                    aside = right_of(v, lane_w)
                    back = left_of([a * b for a, b in zip(fc, v)], lane_w)
                    for ct in everywhere:
                        near = face_l[l - 1, ct, work] * v_of[l - 1, ct, work] + face_l[l, ct, work] * v_of[l + 1, ct, work]
                        near = near + face_r[l, ct, work] * v_of[l, ct, under] + face_r[l, ct, above] * v_of[l, ct, above]
                        near = near + (fc[ct] * aside[ct] + back[ct])
                        new = dinv[l, ct, work] * near
                        new = 0.5 * new if k == 0 else new - basis[k - 1][l, ct, work]
                        basis[k + 1][l, ct, work] = new
                        if ct < tiles:
                            acc = (acc[0] + own_of(v[ct] * near), acc[1] + own_of(diag[l, ct, work] * new * new))
                for j in range(0, layers, 2):
                    rows_of(k + 1, 1 + i * layers + j, i)
                return acc

            ah, ag = lax.fori_loop(0, n_sec, apply, (none, none))
            h.append(ah)
            g.append(ag)
            send_land(k + 1)

        def last(l, acc):
            v_of = basis[ITERS - 1]
            v = [v_of[l, ct, own] for ct in everywhere]
            aside = right_of(v, lane_o)
            for ct in inner:
                near = face_l[l, ct, own] * v_of[l + 1, ct, own] + face_c[l, ct, own] * aside[ct]
                near = v[ct] * (near + face_r[l, ct, own] * v_of[l, ct, RIM + 1:RIM + rows + 1])
                for i in range(0, rows, RIM):
                    acc = acc + near[i:i + RIM]
            return acc

        h.append(2.0 * by_group(1, total + 1, layers, last, none))

        flat = jnp.concatenate([jnp.sum(v, axis=0, keepdims=True) for v in g + h], axis=0)
        part = LANES // (2 * ITERS)
        by = LANES // 2
        while by >= part:
            flat = flat + pltpu.roll(flat, by, 1)
            by //= 2
        which = lax.broadcasted_iota(jnp.int32, flat.shape, 0)
        group = lax.broadcasted_iota(jnp.int32, flat.shape, 1) // part
        mine = sec * n_gx + gx
        stats[c, mine] = jnp.sum(jnp.where(which == group, flat, 0.0), axis=0, keepdims=True)
        if c == 0:
            pl.semaphore_wait(met_sem, n_sec - 1)
        for k, peer in enumerate(everyone):
            copy = pltpu.make_async_remote_copy(
                src_ref=stats.at[c, mine],
                dst_ref=stats.at[c, mine],
                send_sem=sum_send,
                recv_sem=sum_recv.at[c],
                device_id=peer,
                device_id_type=MESH,
            )
            copy.start()
        if c + 1 < steps:
            settle(c, 0)
            settle(c, 1)
            take_cols(c, 0)
            take_cols(c, 1)
            for d in (0, 1):
                @pl.when(sends_to(d))
                def _(d=d):
                    drain(land_size, land_send.at[d])

                @pl.when(beside_to(d))
                def _(d=d):
                    drain(ITERS * ext, col_send.at[d])
        drain(len(everyone), sum_recv.at[c])
        drain(len(everyone), sum_send)
        if c == 0:
            for d in (0, 1):
                @pl.when(sends_to(d))
                def _(d=d):
                    drain(n_sec * row_size + rain_size, row_send.at[d])
        summed = stats[c, 0]
        for k in range(1, n_sec * n_gx):
            summed = summed + stats[c, k]
        parts = [
            jnp.sum(jnp.where(group[0:1] == k, summed, 0.0), axis=1, keepdims=True)
            for k in range(2 * ITERS)
        ]
        x = coefficients(parts[:ITERS], parts[ITERS:])
        x = [jnp.broadcast_to(v, (ext, LANES)) for v in x]

        def update(which, at_rows, count, l, carry):
            for ct in which:
                v = head[l, ct, at_rows]
                for k in range(ITERS):
                    v = v + x[k][0:count] * t[k, l, ct, at_rows]
                head[l, ct, at_rows] = v
            return carry

        if c + 1 == steps:
            final = functools.partial(update, inner, own, rows)
            for i in range(1, n_sec):
                peer = sec_peers[i - 1]
                by_group(1 + peer * layers, 1 + (peer + 1) * layers, layers, final, 0)
                for copy in back_copies(peer):
                    copy.start()
            by_group(1 + sec * layers, 1 + (sec + 1) * layers, layers, final, 0)
        else:
            by_group(1, total + 1, layers, functools.partial(update, everywhere, slice(0, ext), ext), 0)

    for ct in inner:
        copy = pltpu.make_async_copy(
            head.at[layers_of(sec), ct, own], out_ref.at[:, :, lanes_at(here, ct)], out_own
        )
        copy.start()
    drain((n_sec - 1) * swap_size, swap_send)
    drain(flow_size + back_size, out_own)
    drain((n_sec - 1) * (flow_size + back_size), out_send)
    drain((n_sec - 1) * (flow_size + back_size), out_recv)


def body(n_sec, n_gx, start, soil, conductivity, storage, rain):
    layers, rows, wide = start.shape
    steps = rain.shape[0]
    cols = wide // n_sec
    tiles = cols // LANES
    total = layers * n_sec
    assert total * RIM <= LANES and cols % LANES == 0 and rows % RIM == 0 and n_sec == 4
    assert layers * 2 * RIM <= LANES and layers % 2 == 0 and n_gx & (n_gx - 1) == 0
    ext = rows + 2 * RIM
    f32, i32 = jnp.float32, jnp.int32
    field = pltpu.VMEM((total + 2, tiles + 1, ext, LANES), f32)
    per_sec = pltpu.VMEM((n_sec, tiles + 1, ext, LANES), f32)
    dma = pltpu.SemaphoreType.DMA
    longest = max(
        (2 * layers + steps) * rows * wide // LANES,
        2 * rows * (layers * tiles + 1) * (n_sec - 1),
        2 * RIM * (layers * tiles + 1) * n_sec + steps * (tiles + 1) * RIM,
        ITERS * (total // 2) * tiles * RIM,
        ITERS * ext,
        (n_sec - 1) * (steps + layers) * rows * tiles,
        n_sec * n_gx,
    )
    hbm = pl.BlockSpec(memory_space=pl.ANY)
    return tuple(pl.pallas_call(
        functools.partial(kernel, n_sec, n_gx, steps, conductivity.shape[0]),
        out_shape=(
            jax.ShapeDtypeStruct(start.shape, f32),
            jax.ShapeDtypeStruct((1, steps, rows, wide), f32),
        ),
        in_specs=[hbm] * 5,
        out_specs=(hbm, hbm),
        scratch_shapes=[field, pltpu.VMEM((total + 2, tiles + 1, ext, LANES), i32)]
        + [field] * 9
        + [pltpu.VMEM((ITERS, total + 2, tiles + 1, ext, LANES), f32)]
        + [per_sec] * 3
        + [
            pltpu.VMEM((steps, tiles + 1, ext, LANES), f32),
            pltpu.VMEM((n_sec, steps, rows, cols), f32),
            pltpu.VMEM((2, ITERS, ext, LANES), f32),
            pltpu.VMEM((steps - 1, 2, ITERS, ext, LANES), f32),
            pltpu.VMEM((n_sec, ext, LANES), f32),
            pltpu.VMEM((n_sec, ext, LANES), i32),
            pltpu.VMEM((n_sec, rows, LANES), f32),
            pltpu.VMEM((n_sec, rows, LANES), i32),
            pltpu.VMEM(start.shape, f32),
            pltpu.VMEM(start.shape, i32),
            pltpu.VMEM(rain.shape, f32),
            pltpu.VMEM((ITERS, 2, total // 2, tiles, RIM, LANES), f32),
            pltpu.VMEM((steps - 1, ITERS, 2, total // 2, tiles, RIM, LANES), f32),
            pltpu.VMEM((steps, n_sec * n_gx, 1, LANES), f32),
            pltpu.VMEM((longest, LANES), f32),
            pltpu.SMEM((2, conductivity.shape[0]), f32),
            pltpu.SemaphoreType.REGULAR,
            dma,
            dma((2,)),
            dma,
            dma,
            dma((n_sec - 1,)),
            dma((2,)),
            dma((n_sec, 2)),
            dma((2,)),
            dma((2,)),
            dma((steps - 1, 2, 2)),
            dma((2,)),
            dma((steps - 1, 2, 2)),
            dma,
            dma((steps,)),
            dma,
            dma,
            dma,
        ],
        compiler_params=pltpu.CompilerParams(collective_id=0, has_side_effects=True),
    )(start, soil, conductivity, storage, rain))


def solution(mesh):
    placed = (P("sec", "gx", None), P("sec", "gx", None), P(), P(), P(None, "gx", None))
    return jax.shard_map(
        functools.partial(body, mesh.shape["sec"], mesh.shape["gx"]),
        mesh=mesh,
        in_specs=placed,
        out_specs=(P("sec", "gx", None), P("sec", None, "gx", None)),
        check_vma=False,
    )
```

```python
import functools

import jax
import jax.numpy as jnp
from jax import lax
from jax.experimental import pallas as pl
from jax.experimental.pallas import tpu as pltpu
from jax.sharding import PartitionSpec as P


MESH = pl.DeviceIdType.MESH
RIM = 8
LANES = 128
ITERS = 4
LOW = RIM // 2
SHIPPED = (((0, 0), (1, 1)), ((2, 0),), ((3, 0),))


def by_group(low, high, each, body, carry):
    def trip(i, carry):
        for j in range(each):
            carry = body(low + i * each + j, carry)
        return carry

    return lax.fori_loop(0, (high - low) // each, trip, carry)


def place_of(s):
    return s + s // 2 - 2 * (s // 3)


def mirrored(a, mask, count):
    out, bit = 0, 1
    while bit < count:
        out = out + lax.rem(a // bit + (mask // bit) % 2, 2) * bit
        bit *= 2
    return out


def coefficients(g, h):
    nu = [g[0], h[0]]
    for k in range(1, ITERS):
        nu.append(2.0 * g[k] - nu[0])
        nu.append(4.0 * h[k] - 2.0 * nu[1] - nu[2 * k - 1])

    def gram(i, j):
        return 0.5 * (nu[i + j] + nu[abs(i - j)])

    def gram_a(i, j):
        shifted = gram(i, 1) if j == 0 else 0.5 * (gram(i, j + 1) + gram(i, j - 1))
        return gram(i, j) - shifted

    G = [[gram(i, j) for j in range(ITERS)] for i in range(ITERS)]
    H = [[gram_a(max(i, j), min(i, j)) for j in range(ITERS)] for i in range(ITERS)]
    zero = jnp.zeros_like(g[0])

    def form(matrix, v, top):
        total = zero
        for i in range(top + 1):
            row = matrix[i][i] * v[i]
            for j in range(i):
                row = row + 2.0 * matrix[i][j] * v[j]
            total = total + row * v[i]
        return total

    z = [zero + 1.0] + [zero] * (ITERS - 1)
    p = list(z)
    x = [zero] * ITERS
    rz = nu[0]
    for k in range(ITERS):
        curve = form(H, p, k)
        alpha = jnp.where(curve > 0.0, rz / jnp.where(curve > 0.0, curve, 1.0), 0.0)
        x = [a + alpha * b for a, b in zip(x, p)]
        if k + 1 < ITERS:
            image = list(p)
            for i in range(k + 1):
                if i == 0:
                    image[1] = image[1] - p[0]
                else:
                    image[i + 1] = image[i + 1] - 0.5 * p[i]
                    image[i - 1] = image[i - 1] - 0.5 * p[i]
            z = [a - alpha * b for a, b in zip(z, image)]
            new = jnp.maximum(form(G, z, k + 1), 0.0)
            beta = jnp.where(rz > 0.0, new / jnp.where(rz > 0.0, rz, 1.0), 0.0)
            p = [a + beta * b for a, b in zip(z, p)]
            rz = new
    return x


def kernel(
    n_sec, n_gx, steps, kinds,
    start_ref, soil_ref, cond_ref, store_ref, rain_ref,
    out_ref, flow_ref,
    head, soils, kind, store, cond, cap, face_l, face_r, face_c, diag, dinv, t,
    water, enter, leave, rainx, flows, pack_out, pack_in, side, edge_f, edge_i, edges_f, edges_i,
    stage_f, stage_i, stage_r, rows_out, landed, stats, gauge, of_kind,
    met_sem, load_sem, table_sem, own_sem, swap_send, swap_recv, row_send, row_recv, rain_recv,
    col_send, col_recv, land_send, land_recv, sum_send, sum_recv, out_send, out_recv, out_own,
):
    f32 = jnp.float32
    layers, rows, wide = start_ref.shape
    cols = wide // n_sec
    tiles = cols // LANES
    total = layers * n_sec
    ext = rows + 2 * RIM
    sec, gx = lax.axis_index("sec"), lax.axis_index("gx")
    here = place_of(sec)
    own = slice(RIM, RIM + rows)
    work = slice(LOW, ext - LOW)
    above = slice(LOW - 1, ext - LOW - 1)
    under = slice(LOW + 1, ext - LOW + 1)
    everywhere = list(range(tiles + 1))
    inner = list(range(tiles))

    def lanes_at(place, tile):
        return pl.ds(pl.multiple_of(place * cols + tile * LANES, LANES), LANES)

    def layers_of(s):
        return pl.ds(1 + s * layers, layers)

    sec_peers = [lax.rem(sec + k, n_sec) for k in range(1, n_sec)]
    sec_froms = [lax.rem(sec + n_sec - k, n_sec) for k in range(n_sec)]
    gx_peers = [lax.rem(gx + k, n_gx) for k in range(1, n_gx)]
    swap_size = 2 * rows * (layers * tiles + 1)
    row_size = 2 * RIM * (layers * tiles + 1)
    rain_size = steps * (tiles + 1) * RIM
    land_size = (total // 2) * tiles * RIM
    flow_size = steps * rows * tiles
    back_size = layers * rows * tiles

    def drain(size, sem):
        lot = gauge.at[0:size]
        pltpu.make_async_copy(lot, lot, sem).wait()

    parts_of = ((0, ITERS - 1), (ITERS - 1, ITERS))
    everyone = [
        {"sec": mirrored(sec, i, n_sec), "gx": mirrored(gx, j, n_gx)}
        for j in reversed(range(n_gx)) for i in reversed(range(n_sec)) if i + j
    ]

    loads = [
        pltpu.make_async_copy(src, dst, load_sem)
        for src, dst in ((start_ref, stage_f), (soil_ref, stage_i), (rain_ref, stage_r))
    ]
    tables = [
        pltpu.make_async_copy(src, of_kind.at[f], table_sem.at[f]) for f, src in enumerate((cond_ref, store_ref))
    ]
    loads += tables
    for copy in loads:
        copy.start()
    barrier = pltpu.get_barrier_semaphore()
    for peer in sec_peers:
        pl.semaphore_signal(barrier, inc=1, device_id={"sec": peer}, device_id_type=MESH)
    for peer in gx_peers:
        pl.semaphore_signal(barrier, inc=1, device_id={"gx": peer}, device_id_type=MESH)

    def nil(*shape, dtype=f32):
        return jnp.zeros(shape, dtype)

    basis = [t.at[k] for k in range(ITERS)]
    for ref in (head, cond, face_l, *basis):
        ref[0] = nil(tiles + 1, ext, LANES)
        ref[total + 1] = nil(tiles + 1, ext, LANES)

    def hem(l, carry):
        for ref in (face_r, *basis):
            ref[l, :, 0:RIM] = nil(tiles + 1, RIM, LANES)
            ref[l, :, ext - RIM:ext] = nil(tiles + 1, RIM, LANES)
        return carry

    lax.fori_loop(1, total + 1, hem, 0)
    for d in (0, 1):
        rim = slice(ext - RIM, ext) if d == 0 else slice(0, RIM)

        @pl.when(gx == n_gx - 1 if d == 0 else gx == 0)
        def _(d=d, rim=rim):
            def wipe(l, carry):
                head[l + 1, :, rim] = nil(tiles + 1, RIM, LANES)
                soils[l + 1, :, rim] = nil(tiles + 1, RIM, LANES, dtype=jnp.int32)
                return carry

            lax.fori_loop(0, total, wipe, 0)
            for c in range(steps):
                rainx[c, :, rim] = nil(tiles + 1, RIM, LANES)
            edge_f[:, rim] = nil(n_sec, RIM, LANES)
            edge_i[:, rim] = nil(n_sec, RIM, LANES, dtype=jnp.int32)
            for c in range(steps - 1):
                for k in range(len(SHIPPED)):
                    landed[c, k, d] = nil(total // 2, tiles, RIM, LANES)

        @pl.when(here == n_sec - 1 if d == 0 else here == 0)
        def _(d=d):
            for c in range(steps - 1):
                pack_in[c, d] = nil(ITERS, ext, LANES)

    lane = lax.broadcasted_iota(jnp.int32, (ext, LANES), 1)
    lane_w = lax.broadcasted_iota(jnp.int32, (rows + RIM, LANES), 1)
    lane_o = lax.broadcasted_iota(jnp.int32, (rows, LANES), 1)
    at_row = lax.broadcasted_iota(jnp.int32, (ext, LANES), 0)
    beyond = ((at_row >= rows + RIM) & (gx == n_gx - 1)) | ((at_row < RIM) & (gx == 0))
    beside = (lane >= RIM) & (lane < LANES - RIM)
    beside = beside | ((lane < RIM) & (here == n_sec - 1)) | ((lane >= LANES - RIM) & (here == 0))
    outside = [beyond] * tiles + [beyond | beside]

    drain((2 * layers + steps) * rows * wide // LANES, load_sem)

    after = lanes_at(lax.rem(here + 1, n_sec), 0)
    before = lanes_at(lax.rem(here + n_sec - 1, n_sec), tiles - 1)
    for c in range(steps):
        for ct in inner:
            rainx[c, ct, own] = stage_r[c, :, lanes_at(here, ct)]
        rainx[c, tiles, own] = jnp.where(lane_o < LANES // 2, stage_r[c, :, after], stage_r[c, :, before])
    for stage, edges in ((stage_f, edges_f), (stage_i, edges_i)):
        for place in range(n_sec):
            out = nil(rows, LANES, dtype=stage.dtype)
            for j in range(layers):
                right = nil(rows, LANES, dtype=stage.dtype)
                left = right
                if place + 1 < n_sec:
                    right = stage[j, :, (place + 1) * cols:(place + 1) * cols + LANES]
                if place > 0:
                    left = stage[j, :, place * cols - LANES:place * cols]
                both = jnp.where(lane_o < RIM, right, left)
                moved = pltpu.roll(both, (2 * RIM * j + RIM) % LANES, 1)
                out = jnp.where(lane_o // (2 * RIM) == j, moved, out)
            edges[place] = out

    pl.semaphore_wait(barrier, n_sec + n_gx - 2)
    for peer in sec_peers:
        pl.semaphore_signal(met_sem, inc=1, device_id={"sec": peer}, device_id_type=MESH)

    parcels = ((stage_i, soils, edges_i, edge_i), (stage_f, head, edges_f, edge_f))
    swaps = [[] for _ in range(n_sec)]
    for f, (stage, field, edges, edge) in enumerate(parcels):
        for ct in inner:
            swaps[0].append(pltpu.make_async_copy(
                stage.at[:, :, lanes_at(here, ct)], field.at[layers_of(sec), ct, own], own_sem
            ))
        swaps[0].append(pltpu.make_async_copy(edges.at[here], edge.at[sec, own], own_sem))
    for k, peer in enumerate(sec_peers):
        for f, (stage, field, edges, edge) in enumerate(parcels):
            moves = [
                (stage.at[:, :, lanes_at(place_of(peer), ct)], field.at[layers_of(sec), ct, own]) for ct in inner
            ]
            moves.append((edges.at[place_of(peer)], edge.at[sec, own]))
            for m, (src, dst) in enumerate(moves):
                swaps[k + 1].append(pltpu.make_async_remote_copy(
                    src_ref=src,
                    dst_ref=dst,
                    send_sem=swap_send,
                    recv_sem=swap_recv.at[k],
                    device_id={"sec": peer},
                    device_id_type=MESH,
                ))
    for moves in swaps:
        for copy in moves:
            copy.start()

    def toward(d):
        return lax.rem(gx + n_gx - 1, n_gx) if d == 0 else lax.rem(gx + 1, n_gx)

    def ends(d):
        return (slice(RIM, 2 * RIM), slice(ext - RIM, ext)) if d == 0 else (slice(rows, rows + RIM), slice(0, RIM))

    def sends_to(d):
        return gx > 0 if d == 0 else gx < n_gx - 1

    def rain_copy(d):
        src, dst = ends(d)
        return pltpu.make_async_remote_copy(
            src_ref=rainx.at[:, :, src],
            dst_ref=rainx.at[:, :, dst],
            send_sem=row_send.at[d],
            recv_sem=rain_recv.at[d],
            device_id={"gx": toward(d)},
            device_id_type=MESH,
        )

    def row_copies(k, d):
        src, dst = ends(d)
        s = sec_froms[k]
        copies = []
        for f, (_, field, _, edge) in enumerate(parcels):
            pairs = ((field.at[layers_of(s), 0:tiles, src], field.at[layers_of(s), 0:tiles, dst]),
                     (edge.at[s, src], edge.at[s, dst]))
            for m, (a, b) in enumerate(pairs):
                copies.append(pltpu.make_async_remote_copy(
                    src_ref=a,
                    dst_ref=b,
                    send_sem=row_send.at[d],
                    recv_sem=row_recv.at[k, d],
                    device_id={"gx": toward(d)},
                    device_id_type=MESH,
                ))
        return copies

    for d in (0, 1):
        @pl.when(sends_to(d))
        def _(d=d):
            rain_copy(d).start()

    for k in range(n_sec):
        drain(swap_size, own_sem if k == 0 else swap_recv.at[k - 1])
        for d in (0, 1):
            @pl.when(sends_to(d))
            def _(d=d, k=k):
                for copy in row_copies(k, d):
                    copy.start()

    def take_rows(k):
        for d in (0, 1):
            @pl.when(sends_to(d))
            def _(d=d):
                drain(row_size, row_recv.at[k, 1 - d])

    def packed(field, tile, low):
        outs = nil(ext, LANES)
        for l in range(total):
            shift = (RIM * l if low else RIM * l + RIM) % LANES
            piece = field[1 + l, tile]
            moved = pltpu.roll(piece, shift, 1) if shift else piece
            outs = jnp.where(lane // RIM == l, moved, outs)
        return outs

    def col_copy(c, d, part):
        low, high = parts_of[part]
        return pltpu.make_async_remote_copy(
            src_ref=pack_out.at[d, low:high],
            dst_ref=pack_in.at[c, d, low:high],
            send_sem=col_send.at[d],
            recv_sem=col_recv.at[c, d, part],
            device_id={"sec": place_of(lax.rem(here + n_sec - 1, n_sec) if d == 0 else lax.rem(here + 1, n_sec))},
            device_id_type=MESH,
        )

    def beside_to(d):
        return here > 0 if d == 0 else here < n_sec - 1

    def rows_for(k, d, landing):
        if d == 0:
            start = RIM + LOW - k + (rows if landing else 0)
        else:
            start = RIM - LOW + (0 if landing else rows)
        return slice(start, start + k + 1)

    def settle(c, part):
        low, high = parts_of[part]
        lots = [p for p, slots in enumerate(SHIPPED) if low <= slots[0][0] < high]
        for d in (0, 1):
            @pl.when(sends_to(d))
            def _(d=d):
                for p in lots:
                    drain(land_size, land_recv.at[c, 1 - d, p])

        def place(i, carry):
            for d in (0, 1):
                for p in lots:
                    for k, spot in SHIPPED[p]:
                        for ct in inner:
                            for j in (0, 1):
                                t[k, 1 + 2 * i + j, ct, rows_for(k, d, True)] = landed[
                                    c, p, d, i, ct, j * LOW + spot:j * LOW + spot + k + 1
                                ]
            return carry

        by_group(0, total // 2, 2, place, 0)
        for d in (0, 1):
            @pl.when(beside_to(d))
            def _(d=d):
                def each(k, carry):
                    pack_out[d, k] = packed(t.at[k], 0 if d == 0 else tiles - 1, d == 0)
                    return carry

                lax.fori_loop(low, high, each, 0)
                col_copy(c, d, part).start()

    def take_cols(c):
        for d in (0, 1):
            @pl.when(beside_to(d))
            def _(d=d):
                for part in range(len(parts_of)):
                    col_copy(c, 1 - d, part).wait_recv()

    def side_heads(c, x):
        sides = []
        for d in (0, 1):
            v = side[d]
            for k in range(ITERS):
                v = v + x[k] * pack_in[c, d, k]
            side[d] = v
            sides.append(v)
        right, left = sides
        for l in range(total):
            a, b = (-RIM * l) % LANES, (LANES - RIM - RIM * l) % LANES
            ra = pltpu.roll(right, a, 1) if a else right
            rb = pltpu.roll(left, b, 1) if b else left
            head[1 + l, tiles] = jnp.where(lane < RIM, ra, jnp.where(lane >= LANES - RIM, rb, 0.0))

    def right_of(v, at):
        moved = [pltpu.roll(a, LANES - 1, 1) for a in v]
        return [jnp.where(at == LANES - 1, moved[(i + 1) % len(v)], moved[i]) for i in range(len(v))]

    def left_of(v, at):
        moved = [pltpu.roll(a, 1, 1) for a in v]
        return [jnp.where(at == 0, moved[i - 1], moved[i]) for i in range(len(v))]

    def harmonic(a, b):
        return 2.0 * a * b / jnp.maximum(a + b, 1e-30)

    half = lax.broadcasted_iota(jnp.int32, (RIM, LANES), 0) >= LOW

    def own_of(v):
        out = jnp.where(half, v[0:RIM], v[rows:rows + RIM])
        for i in range(RIM, rows, RIM):
            out = out + v[i:i + RIM]
        return out

    none = nil(RIM, LANES)

    def back_copies(peer):
        return [
            pltpu.make_async_remote_copy(
                src_ref=head.at[layers_of(peer), ct, own],
                dst_ref=out_ref.at[:, :, lanes_at(here, ct)],
                send_sem=out_send,
                recv_sem=out_recv,
                device_id={"sec": peer},
                device_id_type=MESH,
            )
            for ct in inner
        ]

    def soil(which, s):
        for ct in which:
            amount = nil(ext, LANES)
            for j in range(layers):
                l = 1 + s * layers + j
                sat = jax.nn.sigmoid(head[l, ct])
                cond[l, ct] = kind[l, ct] * (0.05 + sat * sat)
                cap[l, ct] = store[l, ct] * (0.1 + sat * (1.0 - sat))
                amount = amount + sat
            water[s, ct] = amount

    spot = lax.broadcasted_iota(jnp.int32, (ext, LANES), 1)
    of_cond = nil(ext, LANES)
    of_store = nil(ext, LANES)
    for copy in tables:
        copy.wait()
    for k in range(kinds):
        of_cond = jnp.where(spot == k, of_kind[0, k], of_cond)
        of_store = jnp.where(spot == k, of_kind[1, k], of_store)

    def open_edges(s):
        for edge, field in ((edge_f, head), (edge_i, soils)):
            taken = edge[s]
            for j in range(layers):
                moved = pltpu.roll(taken, LANES - RIM - 2 * RIM * j, 1)
                field[1 + s * layers + j, tiles] = jnp.where(
                    (lane < RIM) | (lane >= LANES - RIM), moved, nil(ext, LANES, dtype=field.dtype)
                )

    def look(s):
        for j in range(layers):
            l = 1 + s * layers + j
            for ct in everywhere:
                which = soils[l, ct]
                a = jnp.take_along_axis(of_cond, which, axis=1, mode="promise_in_bounds")
                b = jnp.take_along_axis(of_store, which, axis=1, mode="promise_in_bounds")
                kind[l, ct] = jnp.where(outside[ct], 0.0, a)
                store[l, ct] = jnp.where(outside[ct], 0.0, b)

    for c in range(steps):
        def couple(which, c=c):
            depth = jnp.float32(layers)
            for ct in which:
                below = nil(ext, LANES)
                slopes = [None] * n_sec
                for s in reversed(range(n_sec)):
                    amount = water[s, ct]
                    slopes[s] = amount / depth * (0.5 + 0.5 * below / (below + depth))
                    below = below + amount
                entering = rainx[c, ct]
                for s in range(n_sec):
                    enter[s, ct] = entering
                    if ct < tiles:
                        flows[s, c, :, ct * LANES:(ct + 1) * LANES] = entering[own]
                    entering = slopes[s] * entering + 0.5 * cond[(s + 1) * layers, ct]
                    leave[s, ct] = entering

        def faces(l, carry):
            k = [cond[l, ct, work] for ct in everywhere]
            for ct, other in zip(everywhere, right_of(k, lane_w)):
                face_l[l, ct, work] = harmonic(k[ct], cond[l + 1, ct, work])
                face_r[l, ct, work] = harmonic(k[ct], cond[l, ct, under])
                face_c[l, ct, work] = harmonic(k[ct], other)
            return carry

        if c == 0:
            for k in range(n_sec):
                s = sec_froms[k]
                take_rows(k)
                open_edges(s)
                look(s)
                soil(everywhere, s)
            for d in (0, 1):
                @pl.when(sends_to(d))
                def _(d=d):
                    rain_copy(1 - d).wait_recv()
        else:
            def each(s, carry):
                soil(everywhere, s)
                return carry

            lax.fori_loop(0, n_sec, each, 0)
        couple(everywhere)
        own_flow = pltpu.make_async_copy(
            flows.at[sec, c], flow_ref.at[0, c, :, pl.ds(pl.multiple_of(here * cols, LANES), cols)], out_own
        )
        own_flow.start()
        for k, peer in enumerate(sec_peers):
            copy = pltpu.make_async_remote_copy(
                src_ref=flows.at[peer, c],
                dst_ref=flow_ref.at[0, c, :, pl.ds(pl.multiple_of(here * cols, LANES), cols)],
                send_sem=out_send,
                recv_sem=out_recv,
                device_id={"sec": peer},
                device_id_type=MESH,
            )
            copy.start()

        by_group(1, total + 1, layers, faces, 0)

        def rows_of(k, l):
            if c + 1 < steps:
                i = (l - 1) // 2
                p = next(p for p, slots in enumerate(SHIPPED) if k in dict(slots))
                spot = dict(SHIPPED[p])[k]
                for ct in inner:
                    for j in (0, 1):
                        for d in (0, 1):
                            rows_out[p, d, i, ct, j * LOW + spot:j * LOW + spot + k + 1] = basis[k][
                                l + j, ct, rows_for(k, d, False)
                            ]

        def first(s, acc):
            for j in range(layers):
                l = 1 + s * layers + j
                fc = [face_c[l, ct, work] for ct in everywhere]
                v = [head[l, ct, work] for ct in everywhere]
                flux = [a * (b - d) for a, b, d in zip(fc, right_of(v, lane_w), v)]
                fb, back = left_of(fc, lane_w), left_of(flux, lane_w)
                for ct in everywhere:
                    up, down = face_l[l - 1, ct, work], face_l[l, ct, work]
                    fr, fa = face_r[l, ct, work], face_r[l, ct, above]
                    whole = cap[l, ct, work] + up + down + fr + fa + fc[ct] + fb[ct]
                    res = up - down + up * (head[l - 1, ct, work] - v[ct]) + down * (head[l + 1, ct, work] - v[ct])
                    res = res + fr * (head[l, ct, under] - v[ct]) + fa * (head[l, ct, above] - v[ct])
                    res = res + flux[ct] - back[ct]
                    if j == 0:
                        res = res + enter[s, ct, work]
                    if j == layers - 1:
                        res = res - leave[s, ct, work]
                    inverse = jnp.where(whole > 0.0, 1.0 / jnp.maximum(whole, 1e-30), 0.0)
                    z = res * inverse
                    diag[l, ct, work] = whole
                    dinv[l, ct, work] = 2.0 * inverse
                    basis[0][l, ct, work] = z
                    if ct < tiles:
                        acc = acc + own_of(res * z)
            for j in range(0, layers, 2):
                rows_of(0, 1 + s * layers + j)
            return acc

        def land_copy(p, d, c=c):
            return pltpu.make_async_remote_copy(
                src_ref=rows_out.at[p, d],
                dst_ref=landed.at[c, p, d],
                send_sem=land_send.at[d],
                recv_sem=land_recv.at[c, d, p],
                device_id={"gx": toward(d)},
                device_id_type=MESH,
            )

        def send_land(k):
            for p, slots in enumerate(SHIPPED):
                if c + 1 < steps and slots[-1][0] == k:
                    for d in (0, 1):
                        @pl.when(sends_to(d))
                        def _(d=d, p=p):
                            land_copy(p, d).start()

        g = [lax.fori_loop(0, n_sec, first, none)]
        send_land(0)
        h = []
        for k in range(ITERS - 1):
            def apply(i, acc, k=k):
                v_of = basis[k]
                for j in range(layers):
                    l = 1 + i * layers + j
                    v = [v_of[l, ct, work] for ct in everywhere]
                    fc = [face_c[l, ct, work] for ct in everywhere]
                    aside = right_of(v, lane_w)
                    back = left_of([a * b for a, b in zip(fc, v)], lane_w)
                    for ct in everywhere:
                        near = face_l[l - 1, ct, work] * v_of[l - 1, ct, work] + face_l[l, ct, work] * v_of[l + 1, ct, work]
                        near = near + face_r[l, ct, work] * v_of[l, ct, under] + face_r[l, ct, above] * v_of[l, ct, above]
                        near = near + (fc[ct] * aside[ct] + back[ct])
                        new = dinv[l, ct, work] * near
                        new = 0.5 * new if k == 0 else new - basis[k - 1][l, ct, work]
                        basis[k + 1][l, ct, work] = new
                        if ct < tiles:
                            acc = (acc[0] + own_of(v[ct] * near), acc[1] + own_of(diag[l, ct, work] * new * new))
                for j in range(0, layers, 2):
                    rows_of(k + 1, 1 + i * layers + j)
                return acc

            ah, ag = lax.fori_loop(0, n_sec, apply, (none, none))
            h.append(ah)
            g.append(ag)
            send_land(k + 1)

        def last(l, acc):
            v_of = basis[ITERS - 1]
            v = [v_of[l, ct, own] for ct in everywhere]
            aside = right_of(v, lane_o)
            for ct in inner:
                near = face_l[l, ct, own] * v_of[l + 1, ct, own] + face_c[l, ct, own] * aside[ct]
                near = v[ct] * (near + face_r[l, ct, own] * v_of[l, ct, RIM + 1:RIM + rows + 1])
                for i in range(0, rows, RIM):
                    acc = acc + near[i:i + RIM]
            return acc

        h.append(2.0 * by_group(1, total + 1, layers, last, none))

        flat = jnp.concatenate([jnp.sum(v, axis=0, keepdims=True) for v in g + h], axis=0)
        part = LANES // (2 * ITERS)
        by = LANES // 2
        while by >= part:
            flat = flat + pltpu.roll(flat, by, 1)
            by //= 2
        which = lax.broadcasted_iota(jnp.int32, flat.shape, 0)
        group = lax.broadcasted_iota(jnp.int32, flat.shape, 1) // part
        mine = sec * n_gx + gx
        stats[c, mine] = jnp.sum(jnp.where(which == group, flat, 0.0), axis=0, keepdims=True)
        if c == 0:
            pl.semaphore_wait(met_sem, n_sec - 1)
        for k, peer in enumerate(everyone):
            copy = pltpu.make_async_remote_copy(
                src_ref=stats.at[c, mine],
                dst_ref=stats.at[c, mine],
                send_sem=sum_send,
                recv_sem=sum_recv.at[c],
                device_id=peer,
                device_id_type=MESH,
            )
            copy.start()
        if c + 1 < steps:
            settle(c, 0)
            if c == 0:
                side[0] = packed(head, tiles, True)
                side[1] = packed(head, tiles, False)
            settle(c, 1)
            take_cols(c)
            for d in (0, 1):
                @pl.when(sends_to(d))
                def _(d=d):
                    drain(len(SHIPPED) * land_size, land_send.at[d])

                @pl.when(beside_to(d))
                def _(d=d):
                    drain(ITERS * ext, col_send.at[d])
        drain(len(everyone), sum_recv.at[c])
        drain(len(everyone), sum_send)
        if c == 0:
            for d in (0, 1):
                @pl.when(sends_to(d))
                def _(d=d):
                    drain(n_sec * row_size + rain_size, row_send.at[d])
        summed = stats[c, 0]
        for k in range(1, n_sec * n_gx):
            summed = summed + stats[c, k]
        parts = [
            jnp.sum(jnp.where(group[0:1] == k, summed, 0.0), axis=1, keepdims=True)
            for k in range(2 * ITERS)
        ]
        x = coefficients(parts[:ITERS], parts[ITERS:])
        x = [jnp.broadcast_to(v, (ext, LANES)) for v in x]

        def update(which, at_rows, count, l, carry):
            for ct in which:
                v = head[l, ct, at_rows]
                for k in range(ITERS):
                    v = v + x[k][0:count] * t[k, l, ct, at_rows]
                head[l, ct, at_rows] = v
            return carry

        if c + 1 == steps:
            final = functools.partial(update, inner, own, rows)
            for i in range(1, n_sec):
                peer = sec_peers[i - 1]
                by_group(1 + peer * layers, 1 + (peer + 1) * layers, layers, final, 0)
                for copy in back_copies(peer):
                    copy.start()
            by_group(1 + sec * layers, 1 + (sec + 1) * layers, layers, final, 0)
        else:
            by_group(1, total + 1, layers, functools.partial(update, inner, slice(0, ext), ext), 0)
            side_heads(c, x)

    for ct in inner:
        copy = pltpu.make_async_copy(
            head.at[layers_of(sec), ct, own], out_ref.at[:, :, lanes_at(here, ct)], out_own
        )
        copy.start()
    drain((n_sec - 1) * swap_size, swap_send)
    drain(flow_size + back_size, out_own)
    drain((n_sec - 1) * (flow_size + back_size), out_send)
    drain((n_sec - 1) * (flow_size + back_size), out_recv)


def hand_over(*refs):
    a, b, out_a, out_b, hold_a, hold_b, sem = refs
    trips = ((a, hold_a, out_a), (b, hold_b, out_b))
    come = [pltpu.make_async_copy(src, hold, sem.at[0, i]) for i, (src, hold, _) in enumerate(trips)]
    go = [pltpu.make_async_copy(hold, dst, sem.at[1, i]) for i, (_, hold, dst) in enumerate(trips)]
    for copy in come:
        copy.start()
    for i in range(2):
        come[i].wait()
        go[i].start()
    for copy in go:
        copy.wait()


def body(n_sec, n_gx, start, soil, conductivity, storage, rain):
    layers, rows, wide = start.shape
    steps = rain.shape[0]
    cols = wide // n_sec
    tiles = cols // LANES
    total = layers * n_sec
    assert total * RIM <= LANES and cols % LANES == 0 and rows % RIM == 0 and n_sec == 4
    assert ITERS == LOW and sum(len(slots) for slots in SHIPPED) == ITERS
    assert layers * 2 * RIM <= LANES and layers % 2 == 0 and n_gx & (n_gx - 1) == 0
    ext = rows + 2 * RIM
    f32, i32 = jnp.float32, jnp.int32
    field = pltpu.VMEM((total + 2, tiles + 1, ext, LANES), f32)
    per_sec = pltpu.VMEM((n_sec, tiles + 1, ext, LANES), f32)
    dma = pltpu.SemaphoreType.DMA
    longest = max(
        (2 * layers + steps) * rows * wide // LANES,
        2 * rows * (layers * tiles + 1) * (n_sec - 1),
        2 * RIM * (layers * tiles + 1) * n_sec + steps * (tiles + 1) * RIM,
        len(SHIPPED) * (total // 2) * tiles * RIM,
        ITERS * ext,
        (n_sec - 1) * (steps + layers) * rows * tiles,
        n_sec * n_gx,
    )
    hbm = pl.BlockSpec(memory_space=pl.ANY)
    made = pl.pallas_call(
        functools.partial(kernel, n_sec, n_gx, steps, conductivity.shape[0]),
        out_shape=(
            jax.ShapeDtypeStruct(start.shape, f32),
            jax.ShapeDtypeStruct((1, steps, rows, wide), f32),
        ),
        in_specs=[hbm] * 5,
        out_specs=(hbm, hbm),
        scratch_shapes=[field, pltpu.VMEM((total + 2, tiles + 1, ext, LANES), i32)]
        + [field] * 9
        + [pltpu.VMEM((ITERS, total + 2, tiles + 1, ext, LANES), f32)]
        + [per_sec] * 3
        + [
            pltpu.VMEM((steps, tiles + 1, ext, LANES), f32),
            pltpu.VMEM((n_sec, steps, rows, cols), f32),
            pltpu.VMEM((2, ITERS, ext, LANES), f32),
            pltpu.VMEM((steps - 1, 2, ITERS, ext, LANES), f32),
            pltpu.VMEM((2, ext, LANES), f32),
            pltpu.VMEM((n_sec, ext, LANES), f32),
            pltpu.VMEM((n_sec, ext, LANES), i32),
            pltpu.VMEM((n_sec, rows, LANES), f32),
            pltpu.VMEM((n_sec, rows, LANES), i32),
            pltpu.VMEM(start.shape, f32),
            pltpu.VMEM(start.shape, i32),
            pltpu.VMEM(rain.shape, f32),
            pltpu.VMEM((len(SHIPPED), 2, total // 2, tiles, RIM, LANES), f32),
            pltpu.VMEM((steps - 1, len(SHIPPED), 2, total // 2, tiles, RIM, LANES), f32),
            pltpu.VMEM((steps, n_sec * n_gx, 1, LANES), f32),
            pltpu.VMEM((longest, LANES), f32),
            pltpu.SMEM((2, conductivity.shape[0]), f32),
            pltpu.SemaphoreType.REGULAR,
            dma,
            dma((2,)),
            dma,
            dma,
            dma((n_sec - 1,)),
            dma((2,)),
            dma((n_sec, 2)),
            dma((2,)),
            dma((2,)),
            dma((steps - 1, 2, 2)),
            dma((2,)),
            dma((steps - 1, 2, len(SHIPPED))),
            dma,
            dma((steps,)),
            dma,
            dma,
            dma,
        ],
        compiler_params=pltpu.CompilerParams(collective_id=0, has_side_effects=True),
    )(start, soil, conductivity, storage, rain)
    return tuple(pl.pallas_call(
        hand_over,
        out_shape=tuple(jax.ShapeDtypeStruct(a.shape, a.dtype) for a in made),
        in_specs=[hbm] * 2,
        out_specs=(hbm,) * 2,
        scratch_shapes=[pltpu.VMEM(a.shape, a.dtype) for a in made] + [dma((2, 2))],
    )(*made))


def solution(mesh):
    placed = (P("sec", "gx", None), P("sec", "gx", None), P(), P(), P(None, "gx", None))
    return jax.shard_map(
        functools.partial(body, mesh.shape["sec"], mesh.shape["gx"]),
        mesh=mesh,
        in_specs=placed,
        out_specs=(P("sec", "gx", None), P("sec", None, "gx", None)),
        check_vma=False,
    )
```

```python
import functools

import jax
import jax.numpy as jnp
from jax import lax
from jax.experimental import pallas as pl
from jax.experimental.pallas import tpu as pltpu
from jax.sharding import PartitionSpec as P


MESH = pl.DeviceIdType.MESH
RIM = 8
LANES = 128
ITERS = 4
LOW = RIM // 2
SHIPPED = (((0, 0), (1, 1)), ((2, 0),), ((3, 0),))


def by_group(low, high, each, body, carry):
    def trip(i, carry):
        for j in range(each):
            carry = body(low + i * each + j, carry)
        return carry

    return lax.fori_loop(0, (high - low) // each, trip, carry)


def place_of(s):
    return s + s // 2 - 2 * (s // 3)


def mirrored(a, mask, count):
    out, bit = 0, 1
    while bit < count:
        out = out + lax.rem(a // bit + (mask // bit) % 2, 2) * bit
        bit *= 2
    return out


def coefficients(g, h):
    nu = [g[0], h[0]]
    for k in range(1, ITERS):
        nu.append(2.0 * g[k] - nu[0])
        nu.append(4.0 * h[k] - 2.0 * nu[1] - nu[2 * k - 1])

    def gram(i, j):
        return 0.5 * (nu[i + j] + nu[abs(i - j)])

    def gram_a(i, j):
        shifted = gram(i, 1) if j == 0 else 0.5 * (gram(i, j + 1) + gram(i, j - 1))
        return gram(i, j) - shifted

    G = [[gram(i, j) for j in range(ITERS)] for i in range(ITERS)]
    H = [[gram_a(max(i, j), min(i, j)) for j in range(ITERS)] for i in range(ITERS)]
    zero = jnp.zeros_like(g[0])

    def form(matrix, v, top):
        total = zero
        for i in range(top + 1):
            row = matrix[i][i] * v[i]
            for j in range(i):
                row = row + 2.0 * matrix[i][j] * v[j]
            total = total + row * v[i]
        return total

    z = [zero + 1.0] + [zero] * (ITERS - 1)
    p = list(z)
    x = [zero] * ITERS
    rz = nu[0]
    for k in range(ITERS):
        curve = form(H, p, k)
        alpha = jnp.where(curve > 0.0, rz / jnp.where(curve > 0.0, curve, 1.0), 0.0)
        x = [a + alpha * b for a, b in zip(x, p)]
        if k + 1 < ITERS:
            image = list(p)
            for i in range(k + 1):
                if i == 0:
                    image[1] = image[1] - p[0]
                else:
                    image[i + 1] = image[i + 1] - 0.5 * p[i]
                    image[i - 1] = image[i - 1] - 0.5 * p[i]
            z = [a - alpha * b for a, b in zip(z, image)]
            new = jnp.maximum(form(G, z, k + 1), 0.0)
            beta = jnp.where(rz > 0.0, new / jnp.where(rz > 0.0, rz, 1.0), 0.0)
            p = [a + beta * b for a, b in zip(z, p)]
            rz = new
    return x


def kernel(
    n_sec, n_gx, steps, kinds,
    start_ref, soil_ref, cond_ref, store_ref, rain_ref,
    out_ref, flow_ref,
    head, soils, kind, store, cond, cap, face_l, face_r, face_c, diag, dinv, t,
    water, enter, leave, rainx, flows, pack_out, pack_in, side, edge_f, edge_i, edges_f, edges_i,
    stage_f, stage_i, stage_r, rows_out, landed, stats, gauge, of_kind,
    met_sem, load_sem, table_sem, own_sem, swap_send, swap_recv, row_send, row_recv, rain_recv,
    col_send, col_recv, land_send, land_recv, sum_send, sum_recv, out_send, out_recv, out_own,
):
    f32 = jnp.float32
    layers, rows, wide = start_ref.shape
    cols = wide // n_sec
    tiles = cols // LANES
    total = layers * n_sec
    ext = rows + 2 * RIM
    sec, gx = lax.axis_index("sec"), lax.axis_index("gx")
    here = place_of(sec)
    own = slice(RIM, RIM + rows)
    work = slice(LOW, ext - LOW)
    above = slice(LOW - 1, ext - LOW - 1)
    under = slice(LOW + 1, ext - LOW + 1)
    everywhere = list(range(tiles + 1))
    inner = list(range(tiles))

    def lanes_at(place, tile):
        return pl.ds(pl.multiple_of(place * cols + tile * LANES, LANES), LANES)

    def layers_of(s):
        return pl.ds(1 + s * layers, layers)

    sec_peers = [lax.rem(sec + k, n_sec) for k in range(1, n_sec)]
    sec_froms = [lax.rem(sec + n_sec - k, n_sec) for k in range(n_sec)]
    gx_peers = [lax.rem(gx + k, n_gx) for k in range(1, n_gx)]
    swap_size = rows * (layers * tiles + 1)
    row_size = RIM * (layers * tiles + 1)
    rain_size = steps * (tiles + 1) * RIM
    land_size = (total // 2) * tiles * RIM
    flow_size = steps * rows * tiles
    back_size = layers * rows * tiles

    def drain(size, sem):
        lot = gauge.at[0:size]
        pltpu.make_async_copy(lot, lot, sem).wait()

    everyone = [
        {"sec": mirrored(sec, i, n_sec), "gx": mirrored(gx, j, n_gx)}
        for j in reversed(range(n_gx)) for i in reversed(range(n_sec)) if i + j
    ]

    loads = [
        pltpu.make_async_copy(src, dst, load_sem)
        for src, dst in ((start_ref, stage_f), (soil_ref, stage_i), (rain_ref, stage_r))
    ]
    tables = [
        pltpu.make_async_copy(src, of_kind.at[f], table_sem.at[f]) for f, src in enumerate((cond_ref, store_ref))
    ]
    loads += tables
    for copy in loads:
        copy.start()
    barrier = pltpu.get_barrier_semaphore()
    for peer in sec_peers:
        pl.semaphore_signal(barrier, inc=1, device_id={"sec": peer}, device_id_type=MESH)
    for peer in gx_peers:
        pl.semaphore_signal(barrier, inc=1, device_id={"gx": peer}, device_id_type=MESH)

    def nil(*shape, dtype=f32):
        return jnp.zeros(shape, dtype)

    basis = [t.at[k] for k in range(ITERS)]
    for ref in (head, cond, face_l, *basis):
        ref[0] = nil(tiles + 1, ext, LANES)
        ref[total + 1] = nil(tiles + 1, ext, LANES)

    def hem(l, carry):
        for ref in (face_r, *basis):
            ref[l, :, 0:RIM] = nil(tiles + 1, RIM, LANES)
            ref[l, :, ext - RIM:ext] = nil(tiles + 1, RIM, LANES)
        return carry

    lax.fori_loop(1, total + 1, hem, 0)
    for d in (0, 1):
        rim = slice(ext - RIM, ext) if d == 0 else slice(0, RIM)

        @pl.when(gx == n_gx - 1 if d == 0 else gx == 0)
        def _(d=d, rim=rim):
            def wipe(l, carry):
                head[l + 1, :, rim] = nil(tiles + 1, RIM, LANES)
                soils[l + 1, :, rim] = nil(tiles + 1, RIM, LANES, dtype=jnp.int32)
                return carry

            lax.fori_loop(0, total, wipe, 0)
            for c in range(steps):
                rainx[c, :, rim] = nil(tiles + 1, RIM, LANES)
            edge_f[:, rim] = nil(n_sec, RIM, LANES)
            edge_i[:, rim] = nil(n_sec, RIM, LANES, dtype=jnp.int32)
            for c in range(steps - 1):
                for k in (0, 1):
                    pack_in[c, k, :, rim] = nil(ITERS, RIM, LANES)
                for k in range(len(SHIPPED)):
                    landed[c, k, d] = nil(total // 2, tiles, RIM, LANES)

        @pl.when(here == n_sec - 1 if d == 0 else here == 0)
        def _(d=d):
            for c in range(steps - 1):
                pack_in[c, d] = nil(ITERS, ext, LANES)

    lane = lax.broadcasted_iota(jnp.int32, (ext, LANES), 1)
    lane_w = lax.broadcasted_iota(jnp.int32, (rows + RIM, LANES), 1)
    lane_o = lax.broadcasted_iota(jnp.int32, (rows, LANES), 1)
    at_row = lax.broadcasted_iota(jnp.int32, (ext, LANES), 0)
    beyond = ((at_row >= rows + RIM) & (gx == n_gx - 1)) | ((at_row < RIM) & (gx == 0))
    beside = (lane >= RIM) & (lane < LANES - RIM)
    beside = beside | ((lane < RIM) & (here == n_sec - 1)) | ((lane >= LANES - RIM) & (here == 0))
    outside = [beyond] * tiles + [beyond | beside]

    drain((2 * layers + steps) * rows * wide // LANES, load_sem)

    after = lanes_at(lax.rem(here + 1, n_sec), 0)
    before = lanes_at(lax.rem(here + n_sec - 1, n_sec), tiles - 1)
    for c in range(steps):
        for ct in inner:
            rainx[c, ct, own] = stage_r[c, :, lanes_at(here, ct)]
        rainx[c, tiles, own] = jnp.where(lane_o < LANES // 2, stage_r[c, :, after], stage_r[c, :, before])
    for stage, edges in ((stage_f, edges_f), (stage_i, edges_i)):
        for place in range(n_sec):
            out = nil(rows, LANES, dtype=stage.dtype)
            for j in range(layers):
                right = nil(rows, LANES, dtype=stage.dtype)
                left = right
                if place + 1 < n_sec:
                    right = stage[j, :, (place + 1) * cols:(place + 1) * cols + LANES]
                if place > 0:
                    left = stage[j, :, place * cols - LANES:place * cols]
                both = jnp.where(lane_o < RIM, right, left)
                moved = pltpu.roll(both, (2 * RIM * j + RIM) % LANES, 1)
                out = jnp.where(lane_o // (2 * RIM) == j, moved, out)
            edges[place] = out

    pl.semaphore_wait(barrier, n_sec + n_gx - 2)
    for peer in sec_peers:
        pl.semaphore_signal(met_sem, inc=1, device_id={"sec": peer}, device_id_type=MESH)

    parcels = ((stage_i, soils, edges_i, edge_i), (stage_f, head, edges_f, edge_f))
    swaps = []
    for f, (stage, field, edges, edge) in enumerate(parcels):
        for ct in inner:
            swaps.append(pltpu.make_async_copy(
                stage.at[:, :, lanes_at(here, ct)], field.at[layers_of(sec), ct, own], own_sem.at[f]
            ))
        swaps.append(pltpu.make_async_copy(edges.at[here], edge.at[sec, own], own_sem.at[f]))
        for k, peer in enumerate(sec_peers):
            moves = [
                (stage.at[:, :, lanes_at(place_of(peer), ct)], field.at[layers_of(sec), ct, own]) for ct in inner
            ]
            moves.append((edges.at[place_of(peer)], edge.at[sec, own]))
            for src, dst in moves:
                swaps.append(pltpu.make_async_remote_copy(
                    src_ref=src,
                    dst_ref=dst,
                    send_sem=swap_send,
                    recv_sem=swap_recv.at[k, f],
                    device_id={"sec": peer},
                    device_id_type=MESH,
                ))
    for copy in swaps:
        copy.start()

    def toward(d):
        return lax.rem(gx + n_gx - 1, n_gx) if d == 0 else lax.rem(gx + 1, n_gx)

    def ends(d):
        return (slice(RIM, 2 * RIM), slice(ext - RIM, ext)) if d == 0 else (slice(rows, rows + RIM), slice(0, RIM))

    def sends_to(d):
        return gx > 0 if d == 0 else gx < n_gx - 1

    def rain_copy(d):
        src, dst = ends(d)
        return pltpu.make_async_remote_copy(
            src_ref=rainx.at[:, :, src],
            dst_ref=rainx.at[:, :, dst],
            send_sem=row_send.at[d],
            recv_sem=rain_recv.at[d],
            device_id={"gx": toward(d)},
            device_id_type=MESH,
        )

    def row_copies(k, f, d):
        src, dst = ends(d)
        s = sec_froms[k]
        _, field, _, edge = parcels[f]
        pairs = ((field.at[layers_of(s), 0:tiles, src], field.at[layers_of(s), 0:tiles, dst]),
                 (edge.at[s, src], edge.at[s, dst]))
        return [
            pltpu.make_async_remote_copy(
                src_ref=a,
                dst_ref=b,
                send_sem=row_send.at[d],
                recv_sem=row_recv.at[k, f, d],
                device_id={"gx": toward(d)},
                device_id_type=MESH,
            )
            for a, b in pairs
        ]

    for d in (0, 1):
        @pl.when(sends_to(d))
        def _(d=d):
            rain_copy(d).start()

    def pass_rows(k, f):
        drain(swap_size, own_sem.at[f] if k == 0 else swap_recv.at[k - 1, f])
        for d in (0, 1):
            @pl.when(sends_to(d))
            def _(d=d):
                for copy in row_copies(k, f, d):
                    copy.start()

    def take_rows(k, f):
        for d in (0, 1):
            @pl.when(sends_to(d))
            def _(d=d):
                drain(row_size, row_recv.at[k, f, 1 - d])

    for k in range(n_sec):
        pass_rows(k, 0)
    for k in range(n_sec):
        pass_rows(k, 1)

    def packed(field, tile, low, at_rows, lane):
        outs = nil(*lane.shape)
        for l in range(total):
            shift = (RIM * l if low else RIM * l + RIM) % LANES
            piece = field[1 + l, tile, at_rows]
            moved = pltpu.roll(piece, shift, 1) if shift else piece
            outs = jnp.where(lane // RIM == l, moved, outs)
        return outs

    def beside_to(d):
        return here > 0 if d == 0 else here < n_sec - 1

    def col_copy(c, d, way):
        peer = {"sec": place_of(lax.rem(here + n_sec - 1, n_sec) if d == 0 else lax.rem(here + 1, n_sec))}
        src, dst = (slice(0, rows), own)
        if way > 0:
            peer["gx"] = toward(way - 1)
            src, dst = (slice(0, RIM), slice(ext - RIM, ext)) if way == 1 else (slice(rows - RIM, rows), slice(0, RIM))
        return pltpu.make_async_remote_copy(
            src_ref=pack_out.at[d, :, src],
            dst_ref=pack_in.at[c, d, :, dst],
            send_sem=col_send.at[d, way],
            recv_sem=col_recv.at[c, d, way],
            device_id=peer,
            device_id_type=MESH,
        )

    def send_cols(c):
        def each(k, carry):
            for d in (0, 1):
                pack_out[d, k] = packed(t.at[k], 0 if d == 0 else tiles - 1, d == 0, own, lane_o)
            return carry

        lax.fori_loop(0, ITERS, each, 0)
        for way in (1, 2, 0):
            for d in (0, 1):
                @pl.when(beside_to(d) & sends_to(way - 1) if way else beside_to(d))
                def _(d=d, way=way):
                    col_copy(c, d, way).start()

    def take_cols(c):
        for way in (0, 1, 2):
            for d in (0, 1):
                @pl.when(beside_to(d) & sends_to(way - 1) if way else beside_to(d))
                def _(d=d, way=way):
                    col_copy(c, d, way).wait_send()

                @pl.when(beside_to(d) & sends_to(2 - way) if way else beside_to(d))
                def _(d=d, way=way):
                    col_copy(c, 1 - d, way).wait_recv()

    def rows_for(k, d, landing):
        if d == 0:
            start = RIM + LOW - k + (rows if landing else 0)
        else:
            start = RIM - LOW + (0 if landing else rows)
        return slice(start, start + k + 1)

    def settle(c):
        lots = range(len(SHIPPED))
        for d in (0, 1):
            @pl.when(sends_to(d))
            def _(d=d):
                for p in lots:
                    drain(land_size, land_recv.at[c, 1 - d, p])
                drain(len(SHIPPED) * land_size, land_send.at[d])

        def place(i, carry):
            for d in (0, 1):
                for p in lots:
                    for k, spot in SHIPPED[p]:
                        for ct in inner:
                            for j in (0, 1):
                                t[k, 1 + 2 * i + j, ct, rows_for(k, d, True)] = landed[
                                    c, p, d, i, ct, j * LOW + spot:j * LOW + spot + k + 1
                                ]
            return carry

        by_group(0, total // 2, 2, place, 0)

    def side_heads(c, x):
        sides = []
        for d in (0, 1):
            v = side[d]
            for k in range(ITERS):
                v = v + x[k] * pack_in[c, d, k]
            side[d] = v
            sides.append(v)
        right, left = sides
        for l in range(total):
            a, b = (-RIM * l) % LANES, (LANES - RIM - RIM * l) % LANES
            ra = pltpu.roll(right, a, 1) if a else right
            rb = pltpu.roll(left, b, 1) if b else left
            head[1 + l, tiles] = jnp.where(lane < RIM, ra, jnp.where(lane >= LANES - RIM, rb, 0.0))

    def right_of(v, at):
        moved = [pltpu.roll(a, LANES - 1, 1) for a in v]
        return [jnp.where(at == LANES - 1, moved[(i + 1) % len(v)], moved[i]) for i in range(len(v))]

    def left_of(v, at):
        moved = [pltpu.roll(a, 1, 1) for a in v]
        return [jnp.where(at == 0, moved[i - 1], moved[i]) for i in range(len(v))]

    def harmonic(a, b):
        return 2.0 * a * b / jnp.maximum(a + b, 1e-30)

    half = lax.broadcasted_iota(jnp.int32, (RIM, LANES), 0) >= LOW

    def own_of(v):
        out = jnp.where(half, v[0:RIM], v[rows:rows + RIM])
        for i in range(RIM, rows, RIM):
            out = out + v[i:i + RIM]
        return out

    none = nil(RIM, LANES)

    def back_copies(peer):
        return [
            pltpu.make_async_remote_copy(
                src_ref=head.at[layers_of(peer), ct, own],
                dst_ref=out_ref.at[:, :, lanes_at(here, ct)],
                send_sem=out_send,
                recv_sem=out_recv,
                device_id={"sec": peer},
                device_id_type=MESH,
            )
            for ct in inner
        ]

    def soil(which, s):
        for ct in which:
            amount = nil(ext, LANES)
            for j in range(layers):
                l = 1 + s * layers + j
                sat = jax.nn.sigmoid(head[l, ct])
                cond[l, ct] = kind[l, ct] * (0.05 + sat * sat)
                cap[l, ct] = store[l, ct] * (0.1 + sat * (1.0 - sat))
                amount = amount + sat
            water[s, ct] = amount

    spot = lax.broadcasted_iota(jnp.int32, (ext, LANES), 1)
    of_cond = nil(ext, LANES)
    of_store = nil(ext, LANES)
    for copy in tables:
        copy.wait()
    for k in range(kinds):
        of_cond = jnp.where(spot == k, of_kind[0, k], of_cond)
        of_store = jnp.where(spot == k, of_kind[1, k], of_store)

    def open_edges(s, f):
        _, field, _, edge = parcels[f]
        taken = edge[s]
        for j in range(layers):
            moved = pltpu.roll(taken, LANES - RIM - 2 * RIM * j, 1)
            field[1 + s * layers + j, tiles] = jnp.where(
                (lane < RIM) | (lane >= LANES - RIM), moved, nil(ext, LANES, dtype=field.dtype)
            )

    def look(s):
        for j in range(layers):
            l = 1 + s * layers + j
            for ct in everywhere:
                which = soils[l, ct]
                a = jnp.take_along_axis(of_cond, which, axis=1, mode="promise_in_bounds")
                b = jnp.take_along_axis(of_store, which, axis=1, mode="promise_in_bounds")
                kind[l, ct] = jnp.where(outside[ct], 0.0, a)
                store[l, ct] = jnp.where(outside[ct], 0.0, b)

    for c in range(steps):
        def couple(which, c=c):
            depth = jnp.float32(layers)
            for ct in which:
                below = nil(ext, LANES)
                slopes = [None] * n_sec
                for s in reversed(range(n_sec)):
                    amount = water[s, ct]
                    slopes[s] = amount / depth * (0.5 + 0.5 * below / (below + depth))
                    below = below + amount
                entering = rainx[c, ct]
                for s in range(n_sec):
                    enter[s, ct] = entering
                    if ct < tiles:
                        flows[s, c, :, ct * LANES:(ct + 1) * LANES] = entering[own]
                    entering = slopes[s] * entering + 0.5 * cond[(s + 1) * layers, ct]
                    leave[s, ct] = entering

        def faces(l, carry):
            k = [cond[l, ct, work] for ct in everywhere]
            for ct, other in zip(everywhere, right_of(k, lane_w)):
                face_l[l, ct, work] = harmonic(k[ct], cond[l + 1, ct, work])
                face_r[l, ct, work] = harmonic(k[ct], cond[l, ct, under])
                face_c[l, ct, work] = harmonic(k[ct], other)
            return carry

        if c == 0:
            for k in range(n_sec):
                take_rows(k, 0)
                open_edges(sec_froms[k], 0)
                look(sec_froms[k])
            for k in range(n_sec):
                take_rows(k, 1)
                open_edges(sec_froms[k], 1)
                soil(everywhere, sec_froms[k])
            for d in (0, 1):
                @pl.when(sends_to(d))
                def _(d=d):
                    rain_copy(1 - d).wait_recv()
        else:
            def each(s, carry):
                soil(everywhere, s)
                return carry

            lax.fori_loop(0, n_sec, each, 0)
        couple(everywhere)
        own_flow = pltpu.make_async_copy(
            flows.at[sec, c], flow_ref.at[0, c, :, pl.ds(pl.multiple_of(here * cols, LANES), cols)], out_own
        )
        own_flow.start()
        for k, peer in enumerate(sec_peers):
            copy = pltpu.make_async_remote_copy(
                src_ref=flows.at[peer, c],
                dst_ref=flow_ref.at[0, c, :, pl.ds(pl.multiple_of(here * cols, LANES), cols)],
                send_sem=out_send,
                recv_sem=out_recv,
                device_id={"sec": peer},
                device_id_type=MESH,
            )
            copy.start()

        by_group(1, total + 1, layers, faces, 0)

        def rows_of(k, l):
            if c + 1 < steps:
                i = (l - 1) // 2
                p = next(p for p, slots in enumerate(SHIPPED) if k in dict(slots))
                spot = dict(SHIPPED[p])[k]
                for ct in inner:
                    for j in (0, 1):
                        for d in (0, 1):
                            rows_out[p, d, i, ct, j * LOW + spot:j * LOW + spot + k + 1] = basis[k][
                                l + j, ct, rows_for(k, d, False)
                            ]

        def first(s, acc):
            for j in range(layers):
                l = 1 + s * layers + j
                fc = [face_c[l, ct, work] for ct in everywhere]
                v = [head[l, ct, work] for ct in everywhere]
                flux = [a * (b - d) for a, b, d in zip(fc, right_of(v, lane_w), v)]
                fb, back = left_of(fc, lane_w), left_of(flux, lane_w)
                for ct in everywhere:
                    up, down = face_l[l - 1, ct, work], face_l[l, ct, work]
                    fr, fa = face_r[l, ct, work], face_r[l, ct, above]
                    whole = cap[l, ct, work] + up + down + fr + fa + fc[ct] + fb[ct]
                    res = up - down + up * (head[l - 1, ct, work] - v[ct]) + down * (head[l + 1, ct, work] - v[ct])
                    res = res + fr * (head[l, ct, under] - v[ct]) + fa * (head[l, ct, above] - v[ct])
                    res = res + flux[ct] - back[ct]
                    if j == 0:
                        res = res + enter[s, ct, work]
                    if j == layers - 1:
                        res = res - leave[s, ct, work]
                    inverse = jnp.where(whole > 0.0, 1.0 / jnp.maximum(whole, 1e-30), 0.0)
                    z = res * inverse
                    diag[l, ct, work] = whole
                    dinv[l, ct, work] = 2.0 * inverse
                    basis[0][l, ct, work] = z
                    if ct < tiles:
                        acc = acc + own_of(res * z)
            for j in range(0, layers, 2):
                rows_of(0, 1 + s * layers + j)
            return acc

        def land_copy(p, d, c=c):
            return pltpu.make_async_remote_copy(
                src_ref=rows_out.at[p, d],
                dst_ref=landed.at[c, p, d],
                send_sem=land_send.at[d],
                recv_sem=land_recv.at[c, d, p],
                device_id={"gx": toward(d)},
                device_id_type=MESH,
            )

        def send_land(k):
            for p, slots in enumerate(SHIPPED):
                if c + 1 < steps and slots[-1][0] == k:
                    for d in (0, 1):
                        @pl.when(sends_to(d))
                        def _(d=d, p=p):
                            land_copy(p, d).start()

        g = [lax.fori_loop(0, n_sec, first, none)]
        send_land(0)
        h = []
        for k in range(ITERS - 1):
            def apply(i, acc, k=k):
                v_of = basis[k]
                for j in range(layers):
                    l = 1 + i * layers + j
                    v = [v_of[l, ct, work] for ct in everywhere]
                    fc = [face_c[l, ct, work] for ct in everywhere]
                    aside = right_of(v, lane_w)
                    back = left_of([a * b for a, b in zip(fc, v)], lane_w)
                    for ct in everywhere:
                        near = face_l[l - 1, ct, work] * v_of[l - 1, ct, work] + face_l[l, ct, work] * v_of[l + 1, ct, work]
                        near = near + face_r[l, ct, work] * v_of[l, ct, under] + face_r[l, ct, above] * v_of[l, ct, above]
                        near = near + (fc[ct] * aside[ct] + back[ct])
                        new = dinv[l, ct, work] * near
                        new = 0.5 * new if k == 0 else new - basis[k - 1][l, ct, work]
                        basis[k + 1][l, ct, work] = new
                        if ct < tiles:
                            acc = (acc[0] + own_of(v[ct] * near), acc[1] + own_of(diag[l, ct, work] * new * new))
                for j in range(0, layers, 2):
                    rows_of(k + 1, 1 + i * layers + j)
                return acc

            ah, ag = lax.fori_loop(0, n_sec, apply, (none, none))
            h.append(ah)
            g.append(ag)
            send_land(k + 1)

        def last(l, acc):
            v_of = basis[ITERS - 1]
            v = [v_of[l, ct, own] for ct in everywhere]
            aside = right_of(v, lane_o)
            for ct in inner:
                near = face_l[l, ct, own] * v_of[l + 1, ct, own] + face_c[l, ct, own] * aside[ct]
                near = v[ct] * (near + face_r[l, ct, own] * v_of[l, ct, RIM + 1:RIM + rows + 1])
                for i in range(0, rows, RIM):
                    acc = acc + near[i:i + RIM]
            return acc

        h.append(2.0 * by_group(1, total + 1, layers, last, none))

        flat = jnp.concatenate([jnp.sum(v, axis=0, keepdims=True) for v in g + h], axis=0)
        part = LANES // (2 * ITERS)
        by = LANES // 2
        while by >= part:
            flat = flat + pltpu.roll(flat, by, 1)
            by //= 2
        which = lax.broadcasted_iota(jnp.int32, flat.shape, 0)
        group = lax.broadcasted_iota(jnp.int32, flat.shape, 1) // part
        mine = sec * n_gx + gx
        stats[c, mine] = jnp.sum(jnp.where(which == group, flat, 0.0), axis=0, keepdims=True)
        if c == 0:
            pl.semaphore_wait(met_sem, n_sec - 1)
        for k, peer in enumerate(everyone):
            copy = pltpu.make_async_remote_copy(
                src_ref=stats.at[c, mine],
                dst_ref=stats.at[c, mine],
                send_sem=sum_send,
                recv_sem=sum_recv.at[c],
                device_id=peer,
                device_id_type=MESH,
            )
            copy.start()
        if c + 1 < steps:
            send_cols(c)
            if c == 0:
                side[0] = packed(head, tiles, True, slice(0, ext), lane)
                side[1] = packed(head, tiles, False, slice(0, ext), lane)
            settle(c)
            take_cols(c)
        drain(len(everyone), sum_recv.at[c])
        drain(len(everyone), sum_send)
        if c == 0:
            for d in (0, 1):
                @pl.when(sends_to(d))
                def _(d=d):
                    drain(2 * n_sec * row_size + rain_size, row_send.at[d])
        summed = stats[c, 0]
        for k in range(1, n_sec * n_gx):
            summed = summed + stats[c, k]
        parts = [
            jnp.sum(jnp.where(group[0:1] == k, summed, 0.0), axis=1, keepdims=True)
            for k in range(2 * ITERS)
        ]
        x = coefficients(parts[:ITERS], parts[ITERS:])
        x = [jnp.broadcast_to(v, (ext, LANES)) for v in x]

        def update(which, at_rows, count, l, carry):
            for ct in which:
                v = head[l, ct, at_rows]
                for k in range(ITERS):
                    v = v + x[k][0:count] * t[k, l, ct, at_rows]
                head[l, ct, at_rows] = v
            return carry

        if c + 1 == steps:
            final = functools.partial(update, inner, own, rows)
            for i in range(1, n_sec):
                peer = sec_peers[i - 1]
                by_group(1 + peer * layers, 1 + (peer + 1) * layers, layers, final, 0)
                for copy in back_copies(peer):
                    copy.start()
            by_group(1 + sec * layers, 1 + (sec + 1) * layers, layers, final, 0)
        else:
            by_group(1, total + 1, layers, functools.partial(update, inner, slice(0, ext), ext), 0)
            side_heads(c, x)

    for ct in inner:
        copy = pltpu.make_async_copy(
            head.at[layers_of(sec), ct, own], out_ref.at[:, :, lanes_at(here, ct)], out_own
        )
        copy.start()
    drain(2 * (n_sec - 1) * swap_size, swap_send)
    drain(flow_size + back_size, out_own)
    drain((n_sec - 1) * (flow_size + back_size), out_send)
    drain((n_sec - 1) * (flow_size + back_size), out_recv)


def hand_over(*refs):
    a, b, out_a, out_b, hold_a, hold_b, sem = refs
    trips = ((a, hold_a, out_a), (b, hold_b, out_b))
    come = [pltpu.make_async_copy(src, hold, sem.at[0, i]) for i, (src, hold, _) in enumerate(trips)]
    go = [pltpu.make_async_copy(hold, dst, sem.at[1, i]) for i, (_, hold, dst) in enumerate(trips)]
    for copy in come:
        copy.start()
    for i in range(2):
        come[i].wait()
        go[i].start()
    for copy in go:
        copy.wait()


def body(n_sec, n_gx, start, soil, conductivity, storage, rain):
    layers, rows, wide = start.shape
    steps = rain.shape[0]
    cols = wide // n_sec
    tiles = cols // LANES
    total = layers * n_sec
    assert total * RIM <= LANES and cols % LANES == 0 and rows % RIM == 0 and n_sec == 4
    assert ITERS == LOW and sum(len(slots) for slots in SHIPPED) == ITERS
    assert layers * 2 * RIM <= LANES and layers % 2 == 0 and n_gx & (n_gx - 1) == 0
    ext = rows + 2 * RIM
    f32, i32 = jnp.float32, jnp.int32
    field = pltpu.VMEM((total + 2, tiles + 1, ext, LANES), f32)
    per_sec = pltpu.VMEM((n_sec, tiles + 1, ext, LANES), f32)
    dma = pltpu.SemaphoreType.DMA
    longest = max(
        (2 * layers + steps) * rows * wide // LANES,
        2 * rows * (layers * tiles + 1) * (n_sec - 1),
        2 * RIM * (layers * tiles + 1) * n_sec + steps * (tiles + 1) * RIM,
        len(SHIPPED) * (total // 2) * tiles * RIM,
        ITERS * ext,
        (n_sec - 1) * (steps + layers) * rows * tiles,
        n_sec * n_gx,
    )
    hbm = pl.BlockSpec(memory_space=pl.ANY)
    made = pl.pallas_call(
        functools.partial(kernel, n_sec, n_gx, steps, conductivity.shape[0]),
        out_shape=(
            jax.ShapeDtypeStruct(start.shape, f32),
            jax.ShapeDtypeStruct((1, steps, rows, wide), f32),
        ),
        in_specs=[hbm] * 5,
        out_specs=(hbm, hbm),
        scratch_shapes=[field, pltpu.VMEM((total + 2, tiles + 1, ext, LANES), i32)]
        + [field] * 9
        + [pltpu.VMEM((ITERS, total + 2, tiles + 1, ext, LANES), f32)]
        + [per_sec] * 3
        + [
            pltpu.VMEM((steps, tiles + 1, ext, LANES), f32),
            pltpu.VMEM((n_sec, steps, rows, cols), f32),
            pltpu.VMEM((2, ITERS, rows, LANES), f32),
            pltpu.VMEM((steps - 1, 2, ITERS, ext, LANES), f32),
            pltpu.VMEM((2, ext, LANES), f32),
            pltpu.VMEM((n_sec, ext, LANES), f32),
            pltpu.VMEM((n_sec, ext, LANES), i32),
            pltpu.VMEM((n_sec, rows, LANES), f32),
            pltpu.VMEM((n_sec, rows, LANES), i32),
            pltpu.VMEM(start.shape, f32),
            pltpu.VMEM(start.shape, i32),
            pltpu.VMEM(rain.shape, f32),
            pltpu.VMEM((len(SHIPPED), 2, total // 2, tiles, RIM, LANES), f32),
            pltpu.VMEM((steps - 1, len(SHIPPED), 2, total // 2, tiles, RIM, LANES), f32),
            pltpu.VMEM((steps, n_sec * n_gx, 1, LANES), f32),
            pltpu.VMEM((longest, LANES), f32),
            pltpu.SMEM((2, conductivity.shape[0]), f32),
            pltpu.SemaphoreType.REGULAR,
            dma,
            dma((2,)),
            dma((2,)),
            dma,
            dma((n_sec - 1, 2)),
            dma((2,)),
            dma((n_sec, 2, 2)),
            dma((2,)),
            dma((2, 3)),
            dma((steps - 1, 2, 3)),
            dma((2,)),
            dma((steps - 1, 2, len(SHIPPED))),
            dma,
            dma((steps,)),
            dma,
            dma,
            dma,
        ],
        compiler_params=pltpu.CompilerParams(collective_id=0, has_side_effects=True),
    )(start, soil, conductivity, storage, rain)
    return tuple(pl.pallas_call(
        hand_over,
        out_shape=tuple(jax.ShapeDtypeStruct(a.shape, a.dtype) for a in made),
        in_specs=[hbm] * 2,
        out_specs=(hbm,) * 2,
        scratch_shapes=[pltpu.VMEM(a.shape, a.dtype) for a in made] + [dma((2, 2))],
    )(*made))


def solution(mesh):
    placed = (P("sec", "gx", None), P("sec", "gx", None), P(), P(), P(None, "gx", None))
    return jax.shard_map(
        functools.partial(body, mesh.shape["sec"], mesh.shape["gx"]),
        mesh=mesh,
        in_specs=placed,
        out_specs=(P("sec", "gx", None), P("sec", None, "gx", None)),
        check_vma=False,
    )
```

```python
import functools

import jax
import jax.numpy as jnp
from jax import lax
from jax.experimental import pallas as pl
from jax.experimental.pallas import tpu as pltpu
from jax.sharding import PartitionSpec as P


MESH = pl.DeviceIdType.MESH
RIM = 8
LANES = 128
ITERS = 4
LOW = RIM // 2
SHIPPED = (((0, 0), (1, 1)), ((2, 0),), ((3, 0),))


def by_group(low, high, each, body, carry):
    def trip(i, carry):
        for j in range(each):
            carry = body(low + i * each + j, carry)
        return carry

    return lax.fori_loop(0, (high - low) // each, trip, carry)


def place_of(s):
    return s + s // 2 - 2 * (s // 3)


def mirrored(a, mask, count):
    out, bit = 0, 1
    while bit < count:
        out = out + lax.rem(a // bit + (mask // bit) % 2, 2) * bit
        bit *= 2
    return out


def coefficients(g, h):
    nu = [g[0], h[0]]
    for k in range(1, ITERS):
        nu.append(2.0 * g[k] - nu[0])
        nu.append(4.0 * h[k] - 2.0 * nu[1] - nu[2 * k - 1])

    def gram(i, j):
        return 0.5 * (nu[i + j] + nu[abs(i - j)])

    def gram_a(i, j):
        shifted = gram(i, 1) if j == 0 else 0.5 * (gram(i, j + 1) + gram(i, j - 1))
        return gram(i, j) - shifted

    G = [[gram(i, j) for j in range(ITERS)] for i in range(ITERS)]
    H = [[gram_a(max(i, j), min(i, j)) for j in range(ITERS)] for i in range(ITERS)]
    zero = jnp.zeros_like(g[0])

    def form(matrix, v, top):
        total = zero
        for i in range(top + 1):
            row = matrix[i][i] * v[i]
            for j in range(i):
                row = row + 2.0 * matrix[i][j] * v[j]
            total = total + row * v[i]
        return total

    z = [zero + 1.0] + [zero] * (ITERS - 1)
    p = list(z)
    x = [zero] * ITERS
    rz = nu[0]
    for k in range(ITERS):
        curve = form(H, p, k)
        alpha = jnp.where(curve > 0.0, rz / jnp.where(curve > 0.0, curve, 1.0), 0.0)
        x = [a + alpha * b for a, b in zip(x, p)]
        if k + 1 < ITERS:
            image = list(p)
            for i in range(k + 1):
                if i == 0:
                    image[1] = image[1] - p[0]
                else:
                    image[i + 1] = image[i + 1] - 0.5 * p[i]
                    image[i - 1] = image[i - 1] - 0.5 * p[i]
            z = [a - alpha * b for a, b in zip(z, image)]
            new = jnp.maximum(form(G, z, k + 1), 0.0)
            beta = jnp.where(rz > 0.0, new / jnp.where(rz > 0.0, rz, 1.0), 0.0)
            p = [a + beta * b for a, b in zip(z, p)]
            rz = new
    return x


def kernel(
    n_sec, n_gx, steps, kinds,
    start_ref, soil_ref, cond_ref, store_ref, rain_ref,
    out_ref, flow_ref,
    head, soils, kind, store, cond, cap, face_l, face_r, face_c, diag, dinv, t,
    water, enter, leave, rainx, flows, pack_out, pack_in, side, edge_f, edge_i, edges_f, edges_i,
    stage_f, stage_i, stage_r, rows_out, landed, stats, gauge, of_kind,
    met_sem, load_sem, table_sem, own_sem, swap_send, swap_recv, row_send, row_recv, rain_recv,
    col_send, col_recv, land_send, land_recv, sum_send, sum_recv, out_send, out_recv, out_own,
):
    f32 = jnp.float32
    layers, rows, wide = start_ref.shape
    cols = wide // n_sec
    tiles = cols // LANES
    total = layers * n_sec
    ext = rows + 2 * RIM
    sec, gx = lax.axis_index("sec"), lax.axis_index("gx")
    here = place_of(sec)
    own = slice(RIM, RIM + rows)
    work = slice(LOW, ext - LOW)
    above = slice(LOW - 1, ext - LOW - 1)
    under = slice(LOW + 1, ext - LOW + 1)
    everywhere = list(range(tiles + 1))
    inner = list(range(tiles))

    def lanes_at(place, tile):
        return pl.ds(pl.multiple_of(place * cols + tile * LANES, LANES), LANES)

    def layers_of(s):
        return pl.ds(1 + s * layers, layers)

    sec_peers = [lax.rem(sec + k, n_sec) for k in range(1, n_sec)]
    sec_froms = [lax.rem(sec + n_sec - k, n_sec) for k in range(n_sec)]
    gx_peers = [lax.rem(gx + k, n_gx) for k in range(1, n_gx)]
    swap_size = rows * (layers * tiles + 1)
    row_size = RIM * (layers * tiles + 1)
    rain_size = steps * (tiles + 1) * RIM
    land_size = (total // 2) * tiles * RIM
    flow_size = steps * rows * tiles
    back_size = layers * rows * tiles

    def drain(size, sem):
        lot = gauge.at[0:size]
        pltpu.make_async_copy(lot, lot, sem).wait()

    everyone = [
        {"sec": mirrored(sec, i, n_sec), "gx": mirrored(gx, j, n_gx)}
        for j in reversed(range(n_gx)) for i in reversed(range(n_sec)) if i + j
    ]

    loads = [
        pltpu.make_async_copy(src, dst, load_sem)
        for src, dst in ((start_ref, stage_f), (soil_ref, stage_i), (rain_ref, stage_r))
    ]
    tables = [
        pltpu.make_async_copy(src, of_kind.at[f], table_sem.at[f]) for f, src in enumerate((cond_ref, store_ref))
    ]
    loads += tables
    for copy in loads:
        copy.start()
    barrier = pltpu.get_barrier_semaphore()
    for peer in sec_peers:
        pl.semaphore_signal(barrier, inc=1, device_id={"sec": peer}, device_id_type=MESH)
    for peer in gx_peers:
        pl.semaphore_signal(barrier, inc=1, device_id={"gx": peer}, device_id_type=MESH)

    def nil(*shape, dtype=f32):
        return jnp.zeros(shape, dtype)

    basis = [t.at[k] for k in range(ITERS)]
    lane = lax.broadcasted_iota(jnp.int32, (ext, LANES), 1)
    lane_w = lax.broadcasted_iota(jnp.int32, (rows + RIM, LANES), 1)
    lane_o = lax.broadcasted_iota(jnp.int32, (rows, LANES), 1)
    at_row = lax.broadcasted_iota(jnp.int32, (ext, LANES), 0)
    beyond = ((at_row >= rows + RIM) & (gx == n_gx - 1)) | ((at_row < RIM) & (gx == 0))
    beside = (lane >= RIM) & (lane < LANES - RIM)
    beside = beside | ((lane < RIM) & (here == n_sec - 1)) | ((lane >= LANES - RIM) & (here == 0))
    outside = [beyond] * tiles + [beyond | beside]

    drain((2 * layers + steps) * rows * wide // LANES, load_sem)

    for stage, edges in ((stage_f, edges_f), (stage_i, edges_i)):
        for place in range(n_sec):
            out = nil(rows, LANES, dtype=stage.dtype)
            for j in range(layers):
                right = nil(rows, LANES, dtype=stage.dtype)
                left = right
                if place + 1 < n_sec:
                    right = stage[j, :, (place + 1) * cols:(place + 1) * cols + LANES]
                if place > 0:
                    left = stage[j, :, place * cols - LANES:place * cols]
                both = jnp.where(lane_o < RIM, right, left)
                moved = pltpu.roll(both, (2 * RIM * j + RIM) % LANES, 1)
                out = jnp.where(lane_o // (2 * RIM) == j, moved, out)
            edges[place] = out

    pl.semaphore_wait(barrier, n_sec + n_gx - 2)
    for peer in sec_peers:
        pl.semaphore_signal(met_sem, inc=1, device_id={"sec": peer}, device_id_type=MESH)

    parcels = ((stage_i, soils, edges_i, edge_i), (stage_f, head, edges_f, edge_f))
    swaps = []
    for f, (stage, field, edges, edge) in enumerate(parcels):
        for ct in inner:
            swaps.append(pltpu.make_async_copy(
                stage.at[:, :, lanes_at(here, ct)], field.at[layers_of(sec), ct, own], own_sem.at[f]
            ))
        swaps.append(pltpu.make_async_copy(edges.at[here], edge.at[sec, own], own_sem.at[f]))
        for k, peer in enumerate(sec_peers):
            moves = [
                (stage.at[:, :, lanes_at(place_of(peer), ct)], field.at[layers_of(sec), ct, own]) for ct in inner
            ]
            moves.append((edges.at[place_of(peer)], edge.at[sec, own]))
            for src, dst in moves:
                swaps.append(pltpu.make_async_remote_copy(
                    src_ref=src,
                    dst_ref=dst,
                    send_sem=swap_send,
                    recv_sem=swap_recv.at[k, f],
                    device_id={"sec": peer},
                    device_id_type=MESH,
                ))
    for copy in swaps:
        copy.start()

    for ref in (head, cond, face_l, *basis):
        ref[0] = nil(tiles + 1, ext, LANES)
        ref[total + 1] = nil(tiles + 1, ext, LANES)

    def hem(l, carry):
        for ref in (face_r, *basis):
            ref[l, :, 0:RIM] = nil(tiles + 1, RIM, LANES)
            ref[l, :, ext - RIM:ext] = nil(tiles + 1, RIM, LANES)
        return carry

    lax.fori_loop(1, total + 1, hem, 0)
    for d in (0, 1):
        rim = slice(ext - RIM, ext) if d == 0 else slice(0, RIM)

        @pl.when(gx == n_gx - 1 if d == 0 else gx == 0)
        def _(d=d, rim=rim):
            def wipe(l, carry):
                head[l + 1, :, rim] = nil(tiles + 1, RIM, LANES)
                soils[l + 1, :, rim] = nil(tiles + 1, RIM, LANES, dtype=jnp.int32)
                return carry

            lax.fori_loop(0, total, wipe, 0)
            for c in range(steps):
                rainx[c, :, rim] = nil(tiles + 1, RIM, LANES)
            edge_f[:, rim] = nil(n_sec, RIM, LANES)
            edge_i[:, rim] = nil(n_sec, RIM, LANES, dtype=jnp.int32)
            for c in range(steps - 1):
                for k in (0, 1):
                    pack_in[c, k, :, rim] = nil(ITERS, RIM, LANES)
                for k in range(len(SHIPPED)):
                    landed[c, k, d] = nil(total // 2, tiles, RIM, LANES)

        @pl.when(here == n_sec - 1 if d == 0 else here == 0)
        def _(d=d):
            for c in range(steps - 1):
                pack_in[c, d] = nil(ITERS, ext, LANES)

    after = lanes_at(lax.rem(here + 1, n_sec), 0)
    before = lanes_at(lax.rem(here + n_sec - 1, n_sec), tiles - 1)
    for c in range(steps):
        for ct in inner:
            rainx[c, ct, own] = stage_r[c, :, lanes_at(here, ct)]
        rainx[c, tiles, own] = jnp.where(lane_o < LANES // 2, stage_r[c, :, after], stage_r[c, :, before])
    def toward(d):
        return lax.rem(gx + n_gx - 1, n_gx) if d == 0 else lax.rem(gx + 1, n_gx)

    def ends(d):
        return (slice(RIM, 2 * RIM), slice(ext - RIM, ext)) if d == 0 else (slice(rows, rows + RIM), slice(0, RIM))

    def sends_to(d):
        return gx > 0 if d == 0 else gx < n_gx - 1

    def rain_copy(d):
        src, dst = ends(d)
        return pltpu.make_async_remote_copy(
            src_ref=rainx.at[:, :, src],
            dst_ref=rainx.at[:, :, dst],
            send_sem=row_send.at[d],
            recv_sem=rain_recv.at[d],
            device_id={"gx": toward(d)},
            device_id_type=MESH,
        )

    def row_copies(k, f, d):
        src, dst = ends(d)
        s = sec_froms[k]
        _, field, _, edge = parcels[f]
        pairs = ((field.at[layers_of(s), 0:tiles, src], field.at[layers_of(s), 0:tiles, dst]),
                 (edge.at[s, src], edge.at[s, dst]))
        return [
            pltpu.make_async_remote_copy(
                src_ref=a,
                dst_ref=b,
                send_sem=row_send.at[d],
                recv_sem=row_recv.at[k, f, d],
                device_id={"gx": toward(d)},
                device_id_type=MESH,
            )
            for a, b in pairs
        ]

    for d in (0, 1):
        @pl.when(sends_to(d))
        def _(d=d):
            rain_copy(d).start()

    def pass_rows(k, f):
        drain(swap_size, own_sem.at[f] if k == 0 else swap_recv.at[k - 1, f])
        for d in (0, 1):
            @pl.when(sends_to(d))
            def _(d=d):
                for copy in row_copies(k, f, d):
                    copy.start()

    def take_rows(k, f):
        for d in (0, 1):
            @pl.when(sends_to(d))
            def _(d=d):
                drain(row_size, row_recv.at[k, f, 1 - d])

    for k in range(n_sec):
        pass_rows(k, 0)
    for k in range(n_sec):
        pass_rows(k, 1)

    def packed(field, tile, low, at_rows, lane):
        outs = nil(*lane.shape)
        for l in range(total):
            shift = (RIM * l if low else RIM * l + RIM) % LANES
            piece = field[1 + l, tile, at_rows]
            moved = pltpu.roll(piece, shift, 1) if shift else piece
            outs = jnp.where(lane // RIM == l, moved, outs)
        return outs

    def beside_to(d):
        return here > 0 if d == 0 else here < n_sec - 1

    def col_copy(c, d, way):
        peer = {"sec": place_of(lax.rem(here + n_sec - 1, n_sec) if d == 0 else lax.rem(here + 1, n_sec))}
        src, dst = (slice(0, rows), own)
        if way > 0:
            peer["gx"] = toward(way - 1)
            src, dst = (slice(0, RIM), slice(ext - RIM, ext)) if way == 1 else (slice(rows - RIM, rows), slice(0, RIM))
        return pltpu.make_async_remote_copy(
            src_ref=pack_out.at[d, :, src],
            dst_ref=pack_in.at[c, d, :, dst],
            send_sem=col_send.at[d, way],
            recv_sem=col_recv.at[c, d, way],
            device_id=peer,
            device_id_type=MESH,
        )

    def send_cols(c):
        def each(k, carry):
            for d in (0, 1):
                pack_out[d, k] = packed(t.at[k], 0 if d == 0 else tiles - 1, d == 0, own, lane_o)
            return carry

        lax.fori_loop(0, ITERS, each, 0)
        for way in (1, 2, 0):
            for d in (0, 1):
                @pl.when(beside_to(d) & sends_to(way - 1) if way else beside_to(d))
                def _(d=d, way=way):
                    col_copy(c, d, way).start()

    def take_cols(c):
        for way in (0, 1, 2):
            for d in (0, 1):
                @pl.when(beside_to(d) & sends_to(way - 1) if way else beside_to(d))
                def _(d=d, way=way):
                    col_copy(c, d, way).wait_send()

                @pl.when(beside_to(d) & sends_to(2 - way) if way else beside_to(d))
                def _(d=d, way=way):
                    col_copy(c, 1 - d, way).wait_recv()

    def rows_for(k, d, landing):
        if d == 0:
            start = RIM + LOW - k + (rows if landing else 0)
        else:
            start = RIM - LOW + (0 if landing else rows)
        return slice(start, start + k + 1)

    def settle(c):
        lots = range(len(SHIPPED))
        for d in (0, 1):
            @pl.when(sends_to(d))
            def _(d=d):
                for p in lots:
                    drain(land_size, land_recv.at[c, 1 - d, p])
                drain(len(SHIPPED) * land_size, land_send.at[d])

        def place(i, carry):
            for d in (0, 1):
                for p in lots:
                    for k, spot in SHIPPED[p]:
                        for ct in inner:
                            for j in (0, 1):
                                t[k, 1 + 2 * i + j, ct, rows_for(k, d, True)] = landed[
                                    c, p, d, i, ct, j * LOW + spot:j * LOW + spot + k + 1
                                ]
            return carry

        by_group(0, total // 2, 2, place, 0)

    def side_heads(c, x):
        sides = []
        for d in (0, 1):
            v = side[d]
            for k in range(ITERS):
                v = v + x[k] * pack_in[c, d, k]
            side[d] = v
            sides.append(v)
        right, left = sides
        for l in range(total):
            a, b = (-RIM * l) % LANES, (LANES - RIM - RIM * l) % LANES
            ra = pltpu.roll(right, a, 1) if a else right
            rb = pltpu.roll(left, b, 1) if b else left
            head[1 + l, tiles] = jnp.where(lane < RIM, ra, jnp.where(lane >= LANES - RIM, rb, 0.0))

    def right_of(v, at):
        moved = [pltpu.roll(a, LANES - 1, 1) for a in v]
        return [jnp.where(at == LANES - 1, moved[(i + 1) % len(v)], moved[i]) for i in range(len(v))]

    def left_of(v, at):
        moved = [pltpu.roll(a, 1, 1) for a in v]
        return [jnp.where(at == 0, moved[i - 1], moved[i]) for i in range(len(v))]

    def harmonic(a, b):
        return 2.0 * a * b / jnp.maximum(a + b, 1e-30)

    half = lax.broadcasted_iota(jnp.int32, (RIM, LANES), 0) >= LOW

    def own_of(v):
        out = jnp.where(half, v[0:RIM], v[rows:rows + RIM])
        for i in range(RIM, rows, RIM):
            out = out + v[i:i + RIM]
        return out

    none = nil(RIM, LANES)

    def back_copies(peer):
        return [
            pltpu.make_async_remote_copy(
                src_ref=head.at[layers_of(peer), ct, own],
                dst_ref=out_ref.at[:, :, lanes_at(here, ct)],
                send_sem=out_send,
                recv_sem=out_recv,
                device_id={"sec": peer},
                device_id_type=MESH,
            )
            for ct in inner
        ]

    def soil(which, s):
        for ct in which:
            amount = nil(ext, LANES)
            for j in range(layers):
                l = 1 + s * layers + j
                sat = jax.nn.sigmoid(head[l, ct])
                cond[l, ct] = kind[l, ct] * (0.05 + sat * sat)
                cap[l, ct] = store[l, ct] * (0.1 + sat * (1.0 - sat))
                amount = amount + sat
            water[s, ct] = amount

    spot = lax.broadcasted_iota(jnp.int32, (ext, LANES), 1)
    of_cond = nil(ext, LANES)
    of_store = nil(ext, LANES)
    for copy in tables:
        copy.wait()
    for k in range(kinds):
        of_cond = jnp.where(spot == k, of_kind[0, k], of_cond)
        of_store = jnp.where(spot == k, of_kind[1, k], of_store)

    def open_edges(s, f):
        _, field, _, edge = parcels[f]
        taken = edge[s]
        for j in range(layers):
            moved = pltpu.roll(taken, LANES - RIM - 2 * RIM * j, 1)
            field[1 + s * layers + j, tiles] = jnp.where(
                (lane < RIM) | (lane >= LANES - RIM), moved, nil(ext, LANES, dtype=field.dtype)
            )

    def look(s):
        for j in range(layers):
            l = 1 + s * layers + j
            for ct in everywhere:
                which = soils[l, ct]
                a = jnp.take_along_axis(of_cond, which, axis=1, mode="promise_in_bounds")
                b = jnp.take_along_axis(of_store, which, axis=1, mode="promise_in_bounds")
                kind[l, ct] = jnp.where(outside[ct], 0.0, a)
                store[l, ct] = jnp.where(outside[ct], 0.0, b)

    for c in range(steps):
        def couple(which, c=c):
            depth = jnp.float32(layers)
            for ct in which:
                below = nil(ext, LANES)
                slopes = [None] * n_sec
                for s in reversed(range(n_sec)):
                    amount = water[s, ct]
                    slopes[s] = amount / depth * (0.5 + 0.5 * below / (below + depth))
                    below = below + amount
                entering = rainx[c, ct]
                for s in range(n_sec):
                    enter[s, ct] = entering
                    if ct < tiles:
                        flows[s, c, :, ct * LANES:(ct + 1) * LANES] = entering[own]
                    entering = slopes[s] * entering + 0.5 * cond[(s + 1) * layers, ct]
                    leave[s, ct] = entering

        def faces(l, carry):
            k = [cond[l, ct, work] for ct in everywhere]
            for ct, other in zip(everywhere, right_of(k, lane_w)):
                face_l[l, ct, work] = harmonic(k[ct], cond[l + 1, ct, work])
                face_r[l, ct, work] = harmonic(k[ct], cond[l, ct, under])
                face_c[l, ct, work] = harmonic(k[ct], other)
            return carry

        if c == 0:
            for k in range(n_sec):
                take_rows(k, 0)
                open_edges(sec_froms[k], 0)
                look(sec_froms[k])
            for k in range(n_sec):
                take_rows(k, 1)
                open_edges(sec_froms[k], 1)
                soil(everywhere, sec_froms[k])
            for d in (0, 1):
                @pl.when(sends_to(d))
                def _(d=d):
                    rain_copy(1 - d).wait_recv()
        else:
            def each(s, carry):
                soil(everywhere, s)
                return carry

            lax.fori_loop(0, n_sec, each, 0)
        couple(everywhere)
        own_flow = pltpu.make_async_copy(
            flows.at[sec, c], flow_ref.at[0, c, :, pl.ds(pl.multiple_of(here * cols, LANES), cols)], out_own
        )
        own_flow.start()
        for k, peer in enumerate(sec_peers):
            copy = pltpu.make_async_remote_copy(
                src_ref=flows.at[peer, c],
                dst_ref=flow_ref.at[0, c, :, pl.ds(pl.multiple_of(here * cols, LANES), cols)],
                send_sem=out_send,
                recv_sem=out_recv,
                device_id={"sec": peer},
                device_id_type=MESH,
            )
            copy.start()

        by_group(1, total + 1, layers, faces, 0)

        def rows_of(k, l):
            if c + 1 < steps:
                i = (l - 1) // 2
                p = next(p for p, slots in enumerate(SHIPPED) if k in dict(slots))
                spot = dict(SHIPPED[p])[k]
                for ct in inner:
                    for j in (0, 1):
                        for d in (0, 1):
                            rows_out[p, d, i, ct, j * LOW + spot:j * LOW + spot + k + 1] = basis[k][
                                l + j, ct, rows_for(k, d, False)
                            ]

        def first(s, acc):
            for j in range(layers):
                l = 1 + s * layers + j
                fc = [face_c[l, ct, work] for ct in everywhere]
                v = [head[l, ct, work] for ct in everywhere]
                flux = [a * (b - d) for a, b, d in zip(fc, right_of(v, lane_w), v)]
                fb, back = left_of(fc, lane_w), left_of(flux, lane_w)
                for ct in everywhere:
                    up, down = face_l[l - 1, ct, work], face_l[l, ct, work]
                    fr, fa = face_r[l, ct, work], face_r[l, ct, above]
                    whole = cap[l, ct, work] + up + down + fr + fa + fc[ct] + fb[ct]
                    res = up - down + up * (head[l - 1, ct, work] - v[ct]) + down * (head[l + 1, ct, work] - v[ct])
                    res = res + fr * (head[l, ct, under] - v[ct]) + fa * (head[l, ct, above] - v[ct])
                    res = res + flux[ct] - back[ct]
                    if j == 0:
                        res = res + enter[s, ct, work]
                    if j == layers - 1:
                        res = res - leave[s, ct, work]
                    inverse = jnp.where(whole > 0.0, 1.0 / jnp.maximum(whole, 1e-30), 0.0)
                    z = res * inverse
                    diag[l, ct, work] = whole
                    dinv[l, ct, work] = 2.0 * inverse
                    basis[0][l, ct, work] = z
                    if ct < tiles:
                        acc = acc + own_of(res * z)
            for j in range(0, layers, 2):
                rows_of(0, 1 + s * layers + j)
            return acc

        def land_copy(p, d, c=c):
            return pltpu.make_async_remote_copy(
                src_ref=rows_out.at[p, d],
                dst_ref=landed.at[c, p, d],
                send_sem=land_send.at[d],
                recv_sem=land_recv.at[c, d, p],
                device_id={"gx": toward(d)},
                device_id_type=MESH,
            )

        def send_land(k):
            for p, slots in enumerate(SHIPPED):
                if c + 1 < steps and slots[-1][0] == k:
                    for d in (0, 1):
                        @pl.when(sends_to(d))
                        def _(d=d, p=p):
                            land_copy(p, d).start()

        g = [lax.fori_loop(0, n_sec, first, none)]
        send_land(0)
        h = []
        for k in range(ITERS - 1):
            def apply(i, acc, k=k):
                v_of = basis[k]
                for j in range(2 * layers):
                    l = 1 + i * 2 * layers + j
                    v = [v_of[l, ct, work] for ct in everywhere]
                    fc = [face_c[l, ct, work] for ct in everywhere]
                    aside = right_of(v, lane_w)
                    back = left_of([a * b for a, b in zip(fc, v)], lane_w)
                    for ct in everywhere:
                        near = face_l[l - 1, ct, work] * v_of[l - 1, ct, work] + face_l[l, ct, work] * v_of[l + 1, ct, work]
                        near = near + face_r[l, ct, work] * v_of[l, ct, under] + face_r[l, ct, above] * v_of[l, ct, above]
                        near = near + (fc[ct] * aside[ct] + back[ct])
                        new = dinv[l, ct, work] * near
                        new = 0.5 * new if k == 0 else new - basis[k - 1][l, ct, work]
                        basis[k + 1][l, ct, work] = new
                        if ct < tiles:
                            acc = (acc[0] + own_of(v[ct] * near), acc[1] + own_of(diag[l, ct, work] * new * new))
                for j in range(0, 2 * layers, 2):
                    rows_of(k + 1, 1 + i * 2 * layers + j)
                return acc

            ah, ag = lax.fori_loop(0, n_sec // 2, apply, (none, none))
            h.append(ah)
            g.append(ag)
            send_land(k + 1)

        def last(l, acc):
            v_of = basis[ITERS - 1]
            v = [v_of[l, ct, own] for ct in everywhere]
            aside = right_of(v, lane_o)
            for ct in inner:
                near = face_l[l, ct, own] * v_of[l + 1, ct, own] + face_c[l, ct, own] * aside[ct]
                near = v[ct] * (near + face_r[l, ct, own] * v_of[l, ct, RIM + 1:RIM + rows + 1])
                for i in range(0, rows, RIM):
                    acc = acc + near[i:i + RIM]
            return acc

        h.append(2.0 * by_group(1, total + 1, layers, last, none))

        flat = jnp.concatenate([jnp.sum(v, axis=0, keepdims=True) for v in g + h], axis=0)
        part = LANES // (2 * ITERS)
        by = LANES // 2
        while by >= part:
            flat = flat + pltpu.roll(flat, by, 1)
            by //= 2
        which = lax.broadcasted_iota(jnp.int32, flat.shape, 0)
        group = lax.broadcasted_iota(jnp.int32, flat.shape, 1) // part
        mine = sec * n_gx + gx
        stats[c, mine] = jnp.sum(jnp.where(which == group, flat, 0.0), axis=0, keepdims=True)
        if c == 0:
            pl.semaphore_wait(met_sem, n_sec - 1)
        for k, peer in enumerate(everyone):
            copy = pltpu.make_async_remote_copy(
                src_ref=stats.at[c, mine],
                dst_ref=stats.at[c, mine],
                send_sem=sum_send,
                recv_sem=sum_recv.at[c],
                device_id=peer,
                device_id_type=MESH,
            )
            copy.start()
        if c + 1 < steps:
            send_cols(c)
            if c == 0:
                side[0] = packed(head, tiles, True, slice(0, ext), lane)
                side[1] = packed(head, tiles, False, slice(0, ext), lane)
            settle(c)
            take_cols(c)
        drain(len(everyone), sum_recv.at[c])
        drain(len(everyone), sum_send)
        if c == 0:
            for d in (0, 1):
                @pl.when(sends_to(d))
                def _(d=d):
                    drain(2 * n_sec * row_size + rain_size, row_send.at[d])
        summed = stats[c, 0]
        for k in range(1, n_sec * n_gx):
            summed = summed + stats[c, k]
        parts = [
            jnp.sum(jnp.where(group[0:1] == k, summed, 0.0), axis=1, keepdims=True)
            for k in range(2 * ITERS)
        ]
        x = coefficients(parts[:ITERS], parts[ITERS:])
        x = [jnp.broadcast_to(v, (ext, LANES)) for v in x]

        def update(which, at_rows, count, l, carry):
            for ct in which:
                v = head[l, ct, at_rows]
                for k in range(ITERS):
                    v = v + x[k][0:count] * t[k, l, ct, at_rows]
                head[l, ct, at_rows] = v
            return carry

        if c + 1 == steps:
            final = functools.partial(update, inner, own, rows)
            for i in range(1, n_sec):
                peer = sec_peers[i - 1]
                by_group(1 + peer * layers, 1 + (peer + 1) * layers, layers, final, 0)
                for copy in back_copies(peer):
                    copy.start()
            by_group(1 + sec * layers, 1 + (sec + 1) * layers, layers, final, 0)
        else:
            by_group(1, total + 1, layers, functools.partial(update, inner, slice(0, ext), ext), 0)
            side_heads(c, x)

    for ct in inner:
        copy = pltpu.make_async_copy(
            head.at[layers_of(sec), ct, own], out_ref.at[:, :, lanes_at(here, ct)], out_own
        )
        copy.start()
    drain(2 * (n_sec - 1) * swap_size, swap_send)
    drain(flow_size + back_size, out_own)
    drain((n_sec - 1) * (flow_size + back_size), out_send)
    drain((n_sec - 1) * (flow_size + back_size), out_recv)


def hand_over(*refs):
    a, b, out_a, out_b, hold_a, hold_b, sem = refs
    trips = ((a, hold_a, out_a), (b, hold_b, out_b))
    come = [pltpu.make_async_copy(src, hold, sem.at[0, i]) for i, (src, hold, _) in enumerate(trips)]
    go = [pltpu.make_async_copy(hold, dst, sem.at[1, i]) for i, (_, hold, dst) in enumerate(trips)]
    for copy in come:
        copy.start()
    for i in range(2):
        come[i].wait()
        go[i].start()
    for copy in go:
        copy.wait()


def body(n_sec, n_gx, start, soil, conductivity, storage, rain):
    layers, rows, wide = start.shape
    steps = rain.shape[0]
    cols = wide // n_sec
    tiles = cols // LANES
    total = layers * n_sec
    assert total * RIM <= LANES and cols % LANES == 0 and rows % RIM == 0 and n_sec == 4
    assert ITERS == LOW and sum(len(slots) for slots in SHIPPED) == ITERS
    assert layers * 2 * RIM <= LANES and layers % 2 == 0 and n_gx & (n_gx - 1) == 0
    ext = rows + 2 * RIM
    f32, i32 = jnp.float32, jnp.int32
    field = pltpu.VMEM((total + 2, tiles + 1, ext, LANES), f32)
    per_sec = pltpu.VMEM((n_sec, tiles + 1, ext, LANES), f32)
    dma = pltpu.SemaphoreType.DMA
    longest = max(
        (2 * layers + steps) * rows * wide // LANES,
        2 * rows * (layers * tiles + 1) * (n_sec - 1),
        2 * RIM * (layers * tiles + 1) * n_sec + steps * (tiles + 1) * RIM,
        len(SHIPPED) * (total // 2) * tiles * RIM,
        ITERS * ext,
        (n_sec - 1) * (steps + layers) * rows * tiles,
        n_sec * n_gx,
    )
    hbm = pl.BlockSpec(memory_space=pl.ANY)
    made = pl.pallas_call(
        functools.partial(kernel, n_sec, n_gx, steps, conductivity.shape[0]),
        out_shape=(
            jax.ShapeDtypeStruct(start.shape, f32),
            jax.ShapeDtypeStruct((1, steps, rows, wide), f32),
        ),
        in_specs=[hbm] * 5,
        out_specs=(hbm, hbm),
        scratch_shapes=[field, pltpu.VMEM((total + 2, tiles + 1, ext, LANES), i32)]
        + [field] * 9
        + [pltpu.VMEM((ITERS, total + 2, tiles + 1, ext, LANES), f32)]
        + [per_sec] * 3
        + [
            pltpu.VMEM((steps, tiles + 1, ext, LANES), f32),
            pltpu.VMEM((n_sec, steps, rows, cols), f32),
            pltpu.VMEM((2, ITERS, rows, LANES), f32),
            pltpu.VMEM((steps - 1, 2, ITERS, ext, LANES), f32),
            pltpu.VMEM((2, ext, LANES), f32),
            pltpu.VMEM((n_sec, ext, LANES), f32),
            pltpu.VMEM((n_sec, ext, LANES), i32),
            pltpu.VMEM((n_sec, rows, LANES), f32),
            pltpu.VMEM((n_sec, rows, LANES), i32),
            pltpu.VMEM(start.shape, f32),
            pltpu.VMEM(start.shape, i32),
            pltpu.VMEM(rain.shape, f32),
            pltpu.VMEM((len(SHIPPED), 2, total // 2, tiles, RIM, LANES), f32),
            pltpu.VMEM((steps - 1, len(SHIPPED), 2, total // 2, tiles, RIM, LANES), f32),
            pltpu.VMEM((steps, n_sec * n_gx, 1, LANES), f32),
            pltpu.VMEM((longest, LANES), f32),
            pltpu.SMEM((2, conductivity.shape[0]), f32),
            pltpu.SemaphoreType.REGULAR,
            dma,
            dma((2,)),
            dma((2,)),
            dma,
            dma((n_sec - 1, 2)),
            dma((2,)),
            dma((n_sec, 2, 2)),
            dma((2,)),
            dma((2, 3)),
            dma((steps - 1, 2, 3)),
            dma((2,)),
            dma((steps - 1, 2, len(SHIPPED))),
            dma,
            dma((steps,)),
            dma,
            dma,
            dma,
        ],
        compiler_params=pltpu.CompilerParams(collective_id=0, has_side_effects=True),
    )(start, soil, conductivity, storage, rain)
    return tuple(pl.pallas_call(
        hand_over,
        out_shape=tuple(jax.ShapeDtypeStruct(a.shape, a.dtype) for a in made),
        in_specs=[hbm] * 2,
        out_specs=(hbm,) * 2,
        scratch_shapes=[pltpu.VMEM(a.shape, a.dtype) for a in made] + [dma((2, 2))],
    )(*made))


def solution(mesh):
    placed = (P("sec", "gx", None), P("sec", "gx", None), P(), P(), P(None, "gx", None))
    return jax.shard_map(
        functools.partial(body, mesh.shape["sec"], mesh.shape["gx"]),
        mesh=mesh,
        in_specs=placed,
        out_specs=(P("sec", "gx", None), P("sec", None, "gx", None)),
        check_vma=False,
    )
```

```python
import functools

import jax
import jax.numpy as jnp
from jax import lax
from jax.experimental import pallas as pl
from jax.experimental.pallas import tpu as pltpu
from jax.sharding import PartitionSpec as P


MESH = pl.DeviceIdType.MESH
RIM = 8
LANES = 128
ITERS = 4
LOW = RIM // 2
SHIPPED = (((0, 0), (1, 1)), ((2, 0),), ((3, 0),))


def by_group(low, high, each, body, carry):
    def trip(i, carry):
        for j in range(each):
            carry = body(low + i * each + j, carry)
        return carry

    return lax.fori_loop(0, (high - low) // each, trip, carry)


def place_of(s):
    return s + s // 2 - 2 * (s // 3)


def mirrored(a, mask, count):
    out, bit = 0, 1
    while bit < count:
        out = out + lax.rem(a // bit + (mask // bit) % 2, 2) * bit
        bit *= 2
    return out


def coefficients(g, h):
    nu = [g[0], h[0]]
    for k in range(1, ITERS):
        nu.append(2.0 * g[k] - nu[0])
        nu.append(4.0 * h[k] - 2.0 * nu[1] - nu[2 * k - 1])

    def gram(i, j):
        return 0.5 * (nu[i + j] + nu[abs(i - j)])

    def gram_a(i, j):
        shifted = gram(i, 1) if j == 0 else 0.5 * (gram(i, j + 1) + gram(i, j - 1))
        return gram(i, j) - shifted

    G = [[gram(i, j) for j in range(ITERS)] for i in range(ITERS)]
    H = [[gram_a(max(i, j), min(i, j)) for j in range(ITERS)] for i in range(ITERS)]
    zero = jnp.zeros_like(g[0])

    def form(matrix, v, top):
        total = zero
        for i in range(top + 1):
            row = matrix[i][i] * v[i]
            for j in range(i):
                row = row + 2.0 * matrix[i][j] * v[j]
            total = total + row * v[i]
        return total

    z = [zero + 1.0] + [zero] * (ITERS - 1)
    p = list(z)
    x = [zero] * ITERS
    rz = nu[0]
    for k in range(ITERS):
        curve = form(H, p, k)
        alpha = jnp.where(curve > 0.0, rz / jnp.where(curve > 0.0, curve, 1.0), 0.0)
        x = [a + alpha * b for a, b in zip(x, p)]
        if k + 1 < ITERS:
            image = list(p)
            for i in range(k + 1):
                if i == 0:
                    image[1] = image[1] - p[0]
                else:
                    image[i + 1] = image[i + 1] - 0.5 * p[i]
                    image[i - 1] = image[i - 1] - 0.5 * p[i]
            z = [a - alpha * b for a, b in zip(z, image)]
            new = jnp.maximum(form(G, z, k + 1), 0.0)
            beta = jnp.where(rz > 0.0, new / jnp.where(rz > 0.0, rz, 1.0), 0.0)
            p = [a + beta * b for a, b in zip(z, p)]
            rz = new
    return x


def kernel(
    n_sec, n_gx, steps, kinds,
    start_ref, soil_ref, cond_ref, store_ref, rain_ref,
    out_ref, flow_ref,
    head, soils, kind, store, cond, cap, face_l, face_r, face_c, diag, dinv, t,
    water, enter, leave, rainx, flows, pack_out, pack_in, side, edge_f, edge_i, edges_f, edges_i,
    stage_f, stage_i, stage_r, rows_out, landed, stats, gauge, of_kind,
    met_sem, load_sem, table_sem, own_sem, swap_send, swap_recv, row_send, row_recv, rain_recv,
    col_send, col_recv, land_send, land_recv, sum_send, sum_recv, out_send, out_recv, out_own,
):
    f32 = jnp.float32
    layers, rows, wide = start_ref.shape
    cols = wide // n_sec
    tiles = cols // LANES
    total = layers * n_sec
    ext = rows + 2 * RIM
    sec, gx = lax.axis_index("sec"), lax.axis_index("gx")
    here = place_of(sec)
    own = slice(RIM, RIM + rows)
    work = slice(LOW, ext - LOW)
    above = slice(LOW - 1, ext - LOW - 1)
    under = slice(LOW + 1, ext - LOW + 1)
    everywhere = list(range(tiles + 1))
    inner = list(range(tiles))

    def lanes_at(place, tile):
        return pl.ds(pl.multiple_of(place * cols + tile * LANES, LANES), LANES)

    def layers_of(s):
        return pl.ds(1 + s * layers, layers)

    sec_peers = [lax.rem(sec + k, n_sec) for k in range(1, n_sec)]
    sec_froms = [lax.rem(sec + n_sec - k, n_sec) for k in range(n_sec)]
    gx_peers = [lax.rem(gx + k, n_gx) for k in range(1, n_gx)]
    swap_size = rows * (layers * tiles + 1)
    row_size = RIM * (layers * tiles + 1)
    rain_size = steps * (tiles + 1) * RIM
    land_size = (total // 2) * tiles * RIM
    flow_size = steps * rows * tiles
    back_size = layers * rows * tiles

    def drain(size, sem):
        lot = gauge.at[0:size]
        pltpu.make_async_copy(lot, lot, sem).wait()

    everyone = [
        {"sec": mirrored(sec, i, n_sec), "gx": mirrored(gx, j, n_gx)}
        for j in reversed(range(n_gx)) for i in reversed(range(n_sec)) if i + j
    ]

    loads = [
        pltpu.make_async_copy(src, dst, load_sem)
        for src, dst in ((start_ref, stage_f), (soil_ref, stage_i), (rain_ref, stage_r))
    ]
    tables = [
        pltpu.make_async_copy(src, of_kind.at[f], table_sem.at[f]) for f, src in enumerate((cond_ref, store_ref))
    ]
    loads += tables
    for copy in loads:
        copy.start()
    barrier = pltpu.get_barrier_semaphore()
    for peer in sec_peers:
        pl.semaphore_signal(barrier, inc=1, device_id={"sec": peer}, device_id_type=MESH)
    for peer in gx_peers:
        pl.semaphore_signal(barrier, inc=1, device_id={"gx": peer}, device_id_type=MESH)

    def nil(*shape, dtype=f32):
        return jnp.zeros(shape, dtype)

    basis = [t.at[k] for k in range(ITERS)]
    lane = lax.broadcasted_iota(jnp.int32, (ext, LANES), 1)
    lane_w = lax.broadcasted_iota(jnp.int32, (rows + RIM, LANES), 1)
    lane_o = lax.broadcasted_iota(jnp.int32, (rows, LANES), 1)
    at_row = lax.broadcasted_iota(jnp.int32, (ext, LANES), 0)
    beyond = ((at_row >= rows + RIM) & (gx == n_gx - 1)) | ((at_row < RIM) & (gx == 0))
    beside = (lane >= RIM) & (lane < LANES - RIM)
    beside = beside | ((lane < RIM) & (here == n_sec - 1)) | ((lane >= LANES - RIM) & (here == 0))
    outside = [beyond] * tiles + [beyond | beside]

    drain((2 * layers + steps) * rows * wide // LANES, load_sem)

    for stage, edges in ((stage_f, edges_f), (stage_i, edges_i)):
        for place in range(n_sec):
            out = nil(rows, LANES, dtype=stage.dtype)
            for j in range(layers):
                right = nil(rows, LANES, dtype=stage.dtype)
                left = right
                if place + 1 < n_sec:
                    right = stage[j, :, (place + 1) * cols:(place + 1) * cols + LANES]
                if place > 0:
                    left = stage[j, :, place * cols - LANES:place * cols]
                both = jnp.where(lane_o < RIM, right, left)
                moved = pltpu.roll(both, (2 * RIM * j + RIM) % LANES, 1)
                out = jnp.where(lane_o // (2 * RIM) == j, moved, out)
            edges[place] = out

    pl.semaphore_wait(barrier, n_sec + n_gx - 2)
    for peer in sec_peers:
        pl.semaphore_signal(met_sem, inc=1, device_id={"sec": peer}, device_id_type=MESH)

    parcels = ((stage_i, soils, edges_i, edge_i), (stage_f, head, edges_f, edge_f))
    swaps = []
    for f, (stage, field, edges, edge) in enumerate(parcels):
        for ct in inner:
            swaps.append(pltpu.make_async_copy(
                stage.at[:, :, lanes_at(here, ct)], field.at[layers_of(sec), ct, own], own_sem.at[f]
            ))
        swaps.append(pltpu.make_async_copy(edges.at[here], edge.at[sec, own], own_sem.at[f]))
        for k, peer in enumerate(sec_peers):
            moves = [
                (stage.at[:, :, lanes_at(place_of(peer), ct)], field.at[layers_of(sec), ct, own]) for ct in inner
            ]
            moves.append((edges.at[place_of(peer)], edge.at[sec, own]))
            for src, dst in moves:
                swaps.append(pltpu.make_async_remote_copy(
                    src_ref=src,
                    dst_ref=dst,
                    send_sem=swap_send,
                    recv_sem=swap_recv.at[k, f],
                    device_id={"sec": peer},
                    device_id_type=MESH,
                ))
    for copy in swaps:
        copy.start()

    for ref in (head, cond, face_l, *basis):
        ref[0] = nil(tiles + 1, ext, LANES)
        ref[total + 1] = nil(tiles + 1, ext, LANES)

    def hem(l, carry):
        for ref in (face_r, *basis):
            ref[l, :, 0:RIM] = nil(tiles + 1, RIM, LANES)
            ref[l, :, ext - RIM:ext] = nil(tiles + 1, RIM, LANES)
        return carry

    lax.fori_loop(1, total + 1, hem, 0)
    for d in (0, 1):
        rim = slice(ext - RIM, ext) if d == 0 else slice(0, RIM)

        @pl.when(gx == n_gx - 1 if d == 0 else gx == 0)
        def _(d=d, rim=rim):
            def wipe(l, carry):
                head[l + 1, :, rim] = nil(tiles + 1, RIM, LANES)
                soils[l + 1, :, rim] = nil(tiles + 1, RIM, LANES, dtype=jnp.int32)
                return carry

            lax.fori_loop(0, total, wipe, 0)
            for c in range(steps):
                rainx[c, :, rim] = nil(tiles + 1, RIM, LANES)
            edge_f[:, rim] = nil(n_sec, RIM, LANES)
            edge_i[:, rim] = nil(n_sec, RIM, LANES, dtype=jnp.int32)
            for c in range(steps - 1):
                for k in (0, 1):
                    pack_in[c, k, :, rim] = nil(ITERS, RIM, LANES)
                for k in range(len(SHIPPED)):
                    landed[c, k, d] = nil(total // 2, tiles, RIM, LANES)

        @pl.when(here == n_sec - 1 if d == 0 else here == 0)
        def _(d=d):
            for c in range(steps - 1):
                pack_in[c, d] = nil(ITERS, ext, LANES)

    after = lanes_at(lax.rem(here + 1, n_sec), 0)
    before = lanes_at(lax.rem(here + n_sec - 1, n_sec), tiles - 1)
    for c in range(steps):
        for ct in inner:
            rainx[c, ct, own] = stage_r[c, :, lanes_at(here, ct)]
        rainx[c, tiles, own] = jnp.where(lane_o < LANES // 2, stage_r[c, :, after], stage_r[c, :, before])
    def toward(d):
        return lax.rem(gx + n_gx - 1, n_gx) if d == 0 else lax.rem(gx + 1, n_gx)

    def ends(d):
        return (slice(RIM, 2 * RIM), slice(ext - RIM, ext)) if d == 0 else (slice(rows, rows + RIM), slice(0, RIM))

    def sends_to(d):
        return gx > 0 if d == 0 else gx < n_gx - 1

    def rain_copy(d):
        src, dst = ends(d)
        return pltpu.make_async_remote_copy(
            src_ref=rainx.at[:, :, src],
            dst_ref=rainx.at[:, :, dst],
            send_sem=row_send.at[d],
            recv_sem=rain_recv.at[d],
            device_id={"gx": toward(d)},
            device_id_type=MESH,
        )

    def row_copies(k, f, d):
        src, dst = ends(d)
        s = sec_froms[k]
        _, field, _, edge = parcels[f]
        pairs = ((field.at[layers_of(s), 0:tiles, src], field.at[layers_of(s), 0:tiles, dst]),
                 (edge.at[s, src], edge.at[s, dst]))
        return [
            pltpu.make_async_remote_copy(
                src_ref=a,
                dst_ref=b,
                send_sem=row_send.at[d],
                recv_sem=row_recv.at[k, f, d],
                device_id={"gx": toward(d)},
                device_id_type=MESH,
            )
            for a, b in pairs
        ]

    for d in (0, 1):
        @pl.when(sends_to(d))
        def _(d=d):
            rain_copy(d).start()

    def pass_rows(k, f):
        drain(swap_size, own_sem.at[f] if k == 0 else swap_recv.at[k - 1, f])
        for d in (0, 1):
            @pl.when(sends_to(d))
            def _(d=d):
                for copy in row_copies(k, f, d):
                    copy.start()

    def take_rows(k, f):
        for d in (0, 1):
            @pl.when(sends_to(d))
            def _(d=d):
                drain(row_size, row_recv.at[k, f, 1 - d])

    for k in range(n_sec):
        pass_rows(k, 0)
    for k in range(n_sec):
        pass_rows(k, 1)

    def packed(field, tile, low, at_rows, lane):
        outs = nil(*lane.shape)
        for l in range(total):
            shift = (RIM * l if low else RIM * l + RIM) % LANES
            piece = field[1 + l, tile, at_rows]
            moved = pltpu.roll(piece, shift, 1) if shift else piece
            outs = jnp.where(lane // RIM == l, moved, outs)
        return outs

    def beside_to(d):
        return here > 0 if d == 0 else here < n_sec - 1

    def col_copy(c, d, way):
        peer = {"sec": place_of(lax.rem(here + n_sec - 1, n_sec) if d == 0 else lax.rem(here + 1, n_sec))}
        src, dst = (slice(0, rows), own)
        if way > 0:
            peer["gx"] = toward(way - 1)
            src, dst = (slice(0, RIM), slice(ext - RIM, ext)) if way == 1 else (slice(rows - RIM, rows), slice(0, RIM))
        return pltpu.make_async_remote_copy(
            src_ref=pack_out.at[d, :, src],
            dst_ref=pack_in.at[c, d, :, dst],
            send_sem=col_send.at[d, way],
            recv_sem=col_recv.at[c, d, way],
            device_id=peer,
            device_id_type=MESH,
        )

    def send_cols(c):
        def each(k, carry):
            for d in (0, 1):
                pack_out[d, k] = packed(t.at[k], 0 if d == 0 else tiles - 1, d == 0, own, lane_o)
            return carry

        lax.fori_loop(0, ITERS, each, 0)
        for way in (1, 2, 0):
            for d in (0, 1):
                @pl.when(beside_to(d) & sends_to(way - 1) if way else beside_to(d))
                def _(d=d, way=way):
                    col_copy(c, d, way).start()

    def take_cols(c):
        for way in (0, 1, 2):
            for d in (0, 1):
                @pl.when(beside_to(d) & sends_to(way - 1) if way else beside_to(d))
                def _(d=d, way=way):
                    col_copy(c, d, way).wait_send()

                @pl.when(beside_to(d) & sends_to(2 - way) if way else beside_to(d))
                def _(d=d, way=way):
                    col_copy(c, 1 - d, way).wait_recv()

    def rows_for(k, d, landing):
        if d == 0:
            start = RIM + LOW - k + (rows if landing else 0)
        else:
            start = RIM - LOW + (0 if landing else rows)
        return slice(start, start + k + 1)

    def settle(c):
        lots = range(len(SHIPPED))
        for d in (0, 1):
            @pl.when(sends_to(d))
            def _(d=d):
                for p in lots:
                    drain(land_size, land_recv.at[c, 1 - d, p])
                drain(len(SHIPPED) * land_size, land_send.at[d])

        def place(i, carry):
            for d in (0, 1):
                for p in lots:
                    for k, spot in SHIPPED[p]:
                        for ct in inner:
                            for j in (0, 1):
                                t[k, 1 + 2 * i + j, ct, rows_for(k, d, True)] = landed[
                                    c, p, d, i, ct, j * LOW + spot:j * LOW + spot + k + 1
                                ]
            return carry

        by_group(0, total // 2, 2, place, 0)

    def side_heads(c, x):
        sides = []
        for d in (0, 1):
            v = side[d]
            for k in range(ITERS):
                v = v + x[k] * pack_in[c, d, k]
            side[d] = v
            sides.append(v)
        right, left = sides
        for l in range(total):
            a, b = (-RIM * l) % LANES, (LANES - RIM - RIM * l) % LANES
            ra = pltpu.roll(right, a, 1) if a else right
            rb = pltpu.roll(left, b, 1) if b else left
            head[1 + l, tiles] = jnp.where(lane < RIM, ra, jnp.where(lane >= LANES - RIM, rb, 0.0))

    def right_of(v, at):
        moved = [pltpu.roll(a, LANES - 1, 1) for a in v]
        return [jnp.where(at == LANES - 1, moved[(i + 1) % len(v)], moved[i]) for i in range(len(v))]

    def left_of(v, at):
        moved = [pltpu.roll(a, 1, 1) for a in v]
        return [jnp.where(at == 0, moved[i - 1], moved[i]) for i in range(len(v))]

    def harmonic(a, b):
        return 2.0 * a * b / jnp.maximum(a + b, 1e-30)

    half = lax.broadcasted_iota(jnp.int32, (RIM, LANES), 0) >= LOW

    def own_of(v):
        out = jnp.where(half, v[0:RIM], v[rows:rows + RIM])
        for i in range(RIM, rows, RIM):
            out = out + v[i:i + RIM]
        return out

    none = nil(RIM, LANES)

    def back_copies(peer):
        return [
            pltpu.make_async_remote_copy(
                src_ref=head.at[layers_of(peer), ct, own],
                dst_ref=out_ref.at[:, :, lanes_at(here, ct)],
                send_sem=out_send,
                recv_sem=out_recv,
                device_id={"sec": peer},
                device_id_type=MESH,
            )
            for ct in inner
        ]

    def soil(which, s):
        for ct in which:
            amount = nil(ext, LANES)
            for j in range(layers):
                l = 1 + s * layers + j
                sat = jax.nn.sigmoid(head[l, ct])
                cond[l, ct] = kind[l, ct] * (0.05 + sat * sat)
                cap[l, ct] = store[l, ct] * (0.1 + sat * (1.0 - sat))
                amount = amount + sat
            water[s, ct] = amount

    spot = lax.broadcasted_iota(jnp.int32, (ext, LANES), 1)
    of_cond = nil(ext, LANES)
    of_store = nil(ext, LANES)
    for copy in tables:
        copy.wait()
    for k in range(kinds):
        of_cond = jnp.where(spot == k, of_kind[0, k], of_cond)
        of_store = jnp.where(spot == k, of_kind[1, k], of_store)

    def open_edges(s, f):
        _, field, _, edge = parcels[f]
        taken = edge[s]
        for j in range(layers):
            moved = pltpu.roll(taken, LANES - RIM - 2 * RIM * j, 1)
            field[1 + s * layers + j, tiles] = jnp.where(
                (lane < RIM) | (lane >= LANES - RIM), moved, nil(ext, LANES, dtype=field.dtype)
            )

    def look(s):
        for j in range(layers):
            l = 1 + s * layers + j
            for ct in everywhere:
                which = soils[l, ct]
                a = jnp.take_along_axis(of_cond, which, axis=1, mode="promise_in_bounds")
                b = jnp.take_along_axis(of_store, which, axis=1, mode="promise_in_bounds")
                kind[l, ct] = jnp.where(outside[ct], 0.0, a)
                store[l, ct] = jnp.where(outside[ct], 0.0, b)

    for c in range(steps):
        def couple(which, c=c):
            depth = jnp.float32(layers)
            for ct in which:
                below = nil(ext, LANES)
                slopes = [None] * n_sec
                for s in reversed(range(n_sec)):
                    amount = water[s, ct]
                    slopes[s] = amount / depth * (0.5 + 0.5 * below / (below + depth))
                    below = below + amount
                entering = rainx[c, ct]
                for s in range(n_sec):
                    enter[s, ct] = entering
                    if ct < tiles:
                        flows[s, c, :, ct * LANES:(ct + 1) * LANES] = entering[own]
                    entering = slopes[s] * entering + 0.5 * cond[(s + 1) * layers, ct]
                    leave[s, ct] = entering

        def faces(l, carry):
            k = [cond[l, ct, work] for ct in everywhere]
            for ct, other in zip(everywhere, right_of(k, lane_w)):
                face_l[l, ct, work] = harmonic(k[ct], cond[l + 1, ct, work])
                face_r[l, ct, work] = harmonic(k[ct], cond[l, ct, under])
                face_c[l, ct, work] = harmonic(k[ct], other)
            return carry

        if c == 0:
            for k in range(n_sec):
                take_rows(k, 0)
                open_edges(sec_froms[k], 0)
                look(sec_froms[k])
            for k in range(n_sec):
                take_rows(k, 1)
                open_edges(sec_froms[k], 1)
                soil(everywhere, sec_froms[k])
            for d in (0, 1):
                @pl.when(sends_to(d))
                def _(d=d):
                    rain_copy(1 - d).wait_recv()
        else:
            def each(s, carry):
                soil(everywhere, s)
                return carry

            lax.fori_loop(0, n_sec, each, 0)
        couple(everywhere)
        own_flow = pltpu.make_async_copy(
            flows.at[sec, c], flow_ref.at[0, c, :, pl.ds(pl.multiple_of(here * cols, LANES), cols)], out_own
        )
        own_flow.start()
        for k, peer in enumerate(sec_peers):
            copy = pltpu.make_async_remote_copy(
                src_ref=flows.at[peer, c],
                dst_ref=flow_ref.at[0, c, :, pl.ds(pl.multiple_of(here * cols, LANES), cols)],
                send_sem=out_send,
                recv_sem=out_recv,
                device_id={"sec": peer},
                device_id_type=MESH,
            )
            copy.start()

        by_group(1, total + 1, 2 * layers, faces, 0)

        def rows_of(k, l):
            if c + 1 < steps:
                i = (l - 1) // 2
                p = next(p for p, slots in enumerate(SHIPPED) if k in dict(slots))
                spot = dict(SHIPPED[p])[k]
                for ct in inner:
                    for j in (0, 1):
                        for d in (0, 1):
                            rows_out[p, d, i, ct, j * LOW + spot:j * LOW + spot + k + 1] = basis[k][
                                l + j, ct, rows_for(k, d, False)
                            ]

        def first(s, acc):
            for j in range(layers):
                l = 1 + s * layers + j
                fc = [face_c[l, ct, work] for ct in everywhere]
                v = [head[l, ct, work] for ct in everywhere]
                flux = [a * (b - d) for a, b, d in zip(fc, right_of(v, lane_w), v)]
                fb, back = left_of(fc, lane_w), left_of(flux, lane_w)
                for ct in everywhere:
                    up, down = face_l[l - 1, ct, work], face_l[l, ct, work]
                    fr, fa = face_r[l, ct, work], face_r[l, ct, above]
                    whole = cap[l, ct, work] + up + down + fr + fa + fc[ct] + fb[ct]
                    res = up - down + up * (head[l - 1, ct, work] - v[ct]) + down * (head[l + 1, ct, work] - v[ct])
                    res = res + fr * (head[l, ct, under] - v[ct]) + fa * (head[l, ct, above] - v[ct])
                    res = res + flux[ct] - back[ct]
                    if j == 0:
                        res = res + enter[s, ct, work]
                    if j == layers - 1:
                        res = res - leave[s, ct, work]
                    inverse = jnp.where(whole > 0.0, 1.0 / jnp.maximum(whole, 1e-30), 0.0)
                    z = res * inverse
                    diag[l, ct, work] = whole
                    dinv[l, ct, work] = 2.0 * inverse
                    basis[0][l, ct, work] = z
                    if ct < tiles:
                        acc = acc + own_of(res * z)
            for j in range(0, layers, 2):
                rows_of(0, 1 + s * layers + j)
            return acc

        def land_copy(p, d, c=c):
            return pltpu.make_async_remote_copy(
                src_ref=rows_out.at[p, d],
                dst_ref=landed.at[c, p, d],
                send_sem=land_send.at[d],
                recv_sem=land_recv.at[c, d, p],
                device_id={"gx": toward(d)},
                device_id_type=MESH,
            )

        def send_land(k):
            for p, slots in enumerate(SHIPPED):
                if c + 1 < steps and slots[-1][0] == k:
                    for d in (0, 1):
                        @pl.when(sends_to(d))
                        def _(d=d, p=p):
                            land_copy(p, d).start()

        g = [lax.fori_loop(0, n_sec, first, none)]
        send_land(0)
        h = []
        for k in range(ITERS - 1):
            def apply(i, acc, k=k):
                v_of = basis[k]
                for j in range(2 * layers):
                    l = 1 + i * 2 * layers + j
                    v = [v_of[l, ct, work] for ct in everywhere]
                    fc = [face_c[l, ct, work] for ct in everywhere]
                    aside = right_of(v, lane_w)
                    back = left_of([a * b for a, b in zip(fc, v)], lane_w)
                    for ct in everywhere:
                        near = face_l[l - 1, ct, work] * v_of[l - 1, ct, work] + face_l[l, ct, work] * v_of[l + 1, ct, work]
                        near = near + face_r[l, ct, work] * v_of[l, ct, under] + face_r[l, ct, above] * v_of[l, ct, above]
                        near = near + (fc[ct] * aside[ct] + back[ct])
                        new = dinv[l, ct, work] * near
                        new = 0.5 * new if k == 0 else new - basis[k - 1][l, ct, work]
                        basis[k + 1][l, ct, work] = new
                        if ct < tiles:
                            acc = (acc[0] + own_of(v[ct] * near), acc[1] + own_of(diag[l, ct, work] * new * new))
                for j in range(0, 2 * layers, 2):
                    rows_of(k + 1, 1 + i * 2 * layers + j)
                return acc

            ah, ag = lax.fori_loop(0, n_sec // 2, apply, (none, none))
            h.append(ah)
            g.append(ag)
            send_land(k + 1)

        def last(l, acc):
            v_of = basis[ITERS - 1]
            v = [v_of[l, ct, own] for ct in everywhere]
            aside = right_of(v, lane_o)
            for ct in inner:
                near = face_l[l, ct, own] * v_of[l + 1, ct, own] + face_c[l, ct, own] * aside[ct]
                near = v[ct] * (near + face_r[l, ct, own] * v_of[l, ct, RIM + 1:RIM + rows + 1])
                for i in range(0, rows, RIM):
                    acc = acc + near[i:i + RIM]
            return acc

        h.append(2.0 * by_group(1, total + 1, 2 * layers, last, none))

        flat = jnp.concatenate([jnp.sum(v, axis=0, keepdims=True) for v in g + h], axis=0)
        part = LANES // (2 * ITERS)
        by = LANES // 2
        while by >= part:
            flat = flat + pltpu.roll(flat, by, 1)
            by //= 2
        which = lax.broadcasted_iota(jnp.int32, flat.shape, 0)
        group = lax.broadcasted_iota(jnp.int32, flat.shape, 1) // part
        mine = sec * n_gx + gx
        stats[c, mine] = jnp.sum(jnp.where(which == group, flat, 0.0), axis=0, keepdims=True)
        if c == 0:
            pl.semaphore_wait(met_sem, n_sec - 1)
        for k, peer in enumerate(everyone):
            copy = pltpu.make_async_remote_copy(
                src_ref=stats.at[c, mine],
                dst_ref=stats.at[c, mine],
                send_sem=sum_send,
                recv_sem=sum_recv.at[c],
                device_id=peer,
                device_id_type=MESH,
            )
            copy.start()
        if c + 1 < steps:
            send_cols(c)
            if c == 0:
                side[0] = packed(head, tiles, True, slice(0, ext), lane)
                side[1] = packed(head, tiles, False, slice(0, ext), lane)
            settle(c)
            take_cols(c)
        drain(len(everyone), sum_recv.at[c])
        drain(len(everyone), sum_send)
        if c == 0:
            for d in (0, 1):
                @pl.when(sends_to(d))
                def _(d=d):
                    drain(2 * n_sec * row_size + rain_size, row_send.at[d])
        summed = stats[c, 0]
        for k in range(1, n_sec * n_gx):
            summed = summed + stats[c, k]
        parts = [
            jnp.sum(jnp.where(group[0:1] == k, summed, 0.0), axis=1, keepdims=True)
            for k in range(2 * ITERS)
        ]
        x = coefficients(parts[:ITERS], parts[ITERS:])
        x = [jnp.broadcast_to(v, (ext, LANES)) for v in x]

        def update(which, at_rows, count, l, carry):
            for ct in which:
                v = head[l, ct, at_rows]
                for k in range(ITERS):
                    v = v + x[k][0:count] * t[k, l, ct, at_rows]
                head[l, ct, at_rows] = v
            return carry

        if c + 1 == steps:
            final = functools.partial(update, inner, own, rows)
            for i in range(1, n_sec):
                peer = sec_peers[i - 1]
                by_group(1 + peer * layers, 1 + (peer + 1) * layers, layers, final, 0)
                for copy in back_copies(peer):
                    copy.start()
            by_group(1 + sec * layers, 1 + (sec + 1) * layers, layers, final, 0)
        else:
            by_group(1, total + 1, 2 * layers, functools.partial(update, inner, slice(0, ext), ext), 0)
            side_heads(c, x)

    for ct in inner:
        copy = pltpu.make_async_copy(
            head.at[layers_of(sec), ct, own], out_ref.at[:, :, lanes_at(here, ct)], out_own
        )
        copy.start()
    drain(2 * (n_sec - 1) * swap_size, swap_send)
    drain(flow_size + back_size, out_own)
    drain((n_sec - 1) * (flow_size + back_size), out_send)
    drain((n_sec - 1) * (flow_size + back_size), out_recv)


def hand_over(*refs):
    a, b, out_a, out_b, hold_a, hold_b, sem = refs
    trips = ((a, hold_a, out_a), (b, hold_b, out_b))
    come = [pltpu.make_async_copy(src, hold, sem.at[0, i]) for i, (src, hold, _) in enumerate(trips)]
    go = [pltpu.make_async_copy(hold, dst, sem.at[1, i]) for i, (_, hold, dst) in enumerate(trips)]
    for copy in come:
        copy.start()
    for i in range(2):
        come[i].wait()
        go[i].start()
    for copy in go:
        copy.wait()


def body(n_sec, n_gx, start, soil, conductivity, storage, rain):
    layers, rows, wide = start.shape
    steps = rain.shape[0]
    cols = wide // n_sec
    tiles = cols // LANES
    total = layers * n_sec
    assert total * RIM <= LANES and cols % LANES == 0 and rows % RIM == 0 and n_sec == 4
    assert ITERS == LOW and sum(len(slots) for slots in SHIPPED) == ITERS
    assert layers * 2 * RIM <= LANES and layers % 2 == 0 and n_gx & (n_gx - 1) == 0
    ext = rows + 2 * RIM
    f32, i32 = jnp.float32, jnp.int32
    field = pltpu.VMEM((total + 2, tiles + 1, ext, LANES), f32)
    per_sec = pltpu.VMEM((n_sec, tiles + 1, ext, LANES), f32)
    dma = pltpu.SemaphoreType.DMA
    longest = max(
        (2 * layers + steps) * rows * wide // LANES,
        2 * rows * (layers * tiles + 1) * (n_sec - 1),
        2 * RIM * (layers * tiles + 1) * n_sec + steps * (tiles + 1) * RIM,
        len(SHIPPED) * (total // 2) * tiles * RIM,
        ITERS * ext,
        (n_sec - 1) * (steps + layers) * rows * tiles,
        n_sec * n_gx,
    )
    hbm = pl.BlockSpec(memory_space=pl.ANY)
    made = pl.pallas_call(
        functools.partial(kernel, n_sec, n_gx, steps, conductivity.shape[0]),
        out_shape=(
            jax.ShapeDtypeStruct(start.shape, f32),
            jax.ShapeDtypeStruct((1, steps, rows, wide), f32),
        ),
        in_specs=[hbm] * 5,
        out_specs=(hbm, hbm),
        scratch_shapes=[field, pltpu.VMEM((total + 2, tiles + 1, ext, LANES), i32)]
        + [field] * 9
        + [pltpu.VMEM((ITERS, total + 2, tiles + 1, ext, LANES), f32)]
        + [per_sec] * 3
        + [
            pltpu.VMEM((steps, tiles + 1, ext, LANES), f32),
            pltpu.VMEM((n_sec, steps, rows, cols), f32),
            pltpu.VMEM((2, ITERS, rows, LANES), f32),
            pltpu.VMEM((steps - 1, 2, ITERS, ext, LANES), f32),
            pltpu.VMEM((2, ext, LANES), f32),
            pltpu.VMEM((n_sec, ext, LANES), f32),
            pltpu.VMEM((n_sec, ext, LANES), i32),
            pltpu.VMEM((n_sec, rows, LANES), f32),
            pltpu.VMEM((n_sec, rows, LANES), i32),
            pltpu.VMEM(start.shape, f32),
            pltpu.VMEM(start.shape, i32),
            pltpu.VMEM(rain.shape, f32),
            pltpu.VMEM((len(SHIPPED), 2, total // 2, tiles, RIM, LANES), f32),
            pltpu.VMEM((steps - 1, len(SHIPPED), 2, total // 2, tiles, RIM, LANES), f32),
            pltpu.VMEM((steps, n_sec * n_gx, 1, LANES), f32),
            pltpu.VMEM((longest, LANES), f32),
            pltpu.SMEM((2, conductivity.shape[0]), f32),
            pltpu.SemaphoreType.REGULAR,
            dma,
            dma((2,)),
            dma((2,)),
            dma,
            dma((n_sec - 1, 2)),
            dma((2,)),
            dma((n_sec, 2, 2)),
            dma((2,)),
            dma((2, 3)),
            dma((steps - 1, 2, 3)),
            dma((2,)),
            dma((steps - 1, 2, len(SHIPPED))),
            dma,
            dma((steps,)),
            dma,
            dma,
            dma,
        ],
        compiler_params=pltpu.CompilerParams(collective_id=0, has_side_effects=True),
    )(start, soil, conductivity, storage, rain)
    return tuple(pl.pallas_call(
        hand_over,
        out_shape=tuple(jax.ShapeDtypeStruct(a.shape, a.dtype) for a in made),
        in_specs=[hbm] * 2,
        out_specs=(hbm,) * 2,
        scratch_shapes=[pltpu.VMEM(a.shape, a.dtype) for a in made] + [dma((2, 2))],
    )(*made))


def solution(mesh):
    placed = (P("sec", "gx", None), P("sec", "gx", None), P(), P(), P(None, "gx", None))
    return jax.shard_map(
        functools.partial(body, mesh.shape["sec"], mesh.shape["gx"]),
        mesh=mesh,
        in_specs=placed,
        out_specs=(P("sec", "gx", None), P("sec", None, "gx", None)),
        check_vma=False,
    )
```
